256 devices in a mesh: segment: 4 (over x_lo, core), dp: 64 (over z, x_hi, y).
Axes of the slice: x: 4 (x_hi: 2, x_lo: 2; x = x_hi * 2 + x_lo), y: 4, z: 8, core: 2. Of those that a mesh axis runs over, the one named last changes fastest.
Arguments:
- latents: bfloat16 [128, 16, 16, 320], P('dp'), may hold values from -6 to 6
- cotangent: bfloat16 [128, 16, 16, 320], P('dp'), may hold values from -6 to 6
- bucket: int32 [128, 2], P('dp'), may hold values from 8 to 16, as said below
- timesteps: int32 [128], P('dp'), may hold values from 0 to 999
- w_enc: bfloat16 [4, 3, 3, 320, 320], P('segment'), may hold values from -0.109375 to 0.109375
- w_dec: bfloat16 [4, 3, 3, 320, 320], P('segment'), may hold values from -0.109375 to 0.109375
- w_time: bfloat16 [4, 2, 320, 320], P('segment'), may hold values from -0.3125 to 0.3125
Outputs:
- grad_enc: float32 [4, 3, 3, 320, 320], P('segment')
- grad_dec: float32 [4, 3, 3, 320, 320], P('segment')
The draws below stay inside these ranges and needn't reach their ends.
Inputs may be any that keep to these rules, and one draw needn't show every extreme that they name: `bucket`: row b holds the height and width of the valid region at the start of microbatch b's 16 x 16 crop; in every draw some microbatch is 16 x 16 and another 16 // 2 x 16 // 2.
All inputs are finite; a program needn't handle non-finite values.
Results may differ from the reference program's by a relative error of at most 0.018.
Values may be sent and summed in bfloat16 or wider, within the bound.
No kernel may reach another device: no remote copies, remote signals or barrier semaphores. Data moves between devices by JAX's collectives and lax.ppermute only.
A program may use at most 128 MiB of HBM per device.

```python
import math
import jax
import jax.numpy as jnp
from jax import lax

C = 320
G = 32
E = 320
P_SIZE = 16
BATCH = 128
N_SEGMENT = 4


def draw_bucket(key, part):
    sizes_drawn = jax.random.randint(key, (BATCH, 2), P_SIZE // 2, P_SIZE + 1, dtype=jnp.int32)
    first_row = jax.random.randint(jax.random.fold_in(key, 11), (), 0, BATCH, dtype=jnp.int32)
    step_ahead = jax.random.randint(jax.random.fold_in(key, 12), (), 1, BATCH, dtype=jnp.int32)
    other_row = (first_row + step_ahead) % BATCH
    sizes_drawn = sizes_drawn.at[first_row].set(P_SIZE)
    return sizes_drawn.at[other_row].set(P_SIZE // 2)


def set_ends(array, key, least, high):
    shape = array.shape
    place = [jax.random.randint(jax.random.fold_in(key, axis), (), 0, shape[axis]) for axis in range(len(shape))]
    array = array.at[tuple(place)].set(least)
    longest = shape.index(max(shape))
    place[longest] = (place[longest] + 1) % shape[longest]
    return array.at[tuple(place)].set(high)


def shard_levels(rng, shape, pieces, low, high):
    loudness, own = 1.0, jax.random.fold_in(rng, 6)
    for position, shards_of in pieces:
        draws = jnp.exp(jax.random.uniform(jax.random.fold_in(own, position), (shards_of,), jnp.float32, low / len(pieces), high / len(pieces)))
        loudness = loudness * jnp.repeat(draws, shape[position] // shards_of).reshape([-1 if axis == position else 1 for axis in range(len(shape))])
    return loudness


def normal_values(stream_key, dims, scale, bound, shards=(), kind=jnp.bfloat16):
    values = scale * jax.random.normal(stream_key, dims, jnp.float32)
    if shards:
        values = values * shard_levels(stream_key, dims, shards, -0.22, 0.18)
    return jnp.clip(values, -bound, bound).astype(kind)


def setup_inputs(seed: int = 0) -> dict:
    seeds = jax.random.split(jax.random.key(seed), 8)
    return {
        "latents": normal_values(seeds[0], (BATCH, P_SIZE, P_SIZE, C), 1.0, 6.0, ((0, 64),)),
        "cotangent": normal_values(seeds[1], (BATCH, P_SIZE, P_SIZE, C), 1.0, 6.0, ((0, 64),)),
        "bucket": draw_bucket(jax.random.fold_in(seeds[7], 71), 0),
        "timesteps": set_ends(jax.random.randint(seeds[3], (BATCH,), 0, 1000), jax.random.fold_in(seeds[3], 1), 0, 999).astype(jnp.int32),
        "w_enc": normal_values(seeds[4], (N_SEGMENT, 3, 3, C, C), (9 * C) ** -0.5, 0.109375, ((0, 4),)),
        "w_dec": normal_values(seeds[5], (N_SEGMENT, 3, 3, C, C), (9 * C) ** -0.5, 0.109375, ((0, 4),)),
        "w_time": normal_values(seeds[6], (N_SEGMENT, 2, E, C), E ** -0.5, 0.3125, ((0, 4),)),
    }


def crop_mask(bucket, side):
    row_index = jnp.arange(side, dtype=jnp.int32)
    inside = (row_index[None, :, None] < bucket[:, 0, None, None]) & (row_index[None, None, :] < bucket[:, 1, None, None])
    return inside.astype(jnp.float32)

def time_embed(timesteps, embed_width):
    half_width = embed_width // 2
    frequencies = jnp.exp(-math.log(10000.0) * jnp.arange(half_width, dtype=jnp.float32) / half_width)
    angles = timesteps.astype(jnp.float32)[:, None] * frequencies[None, :]
    return jnp.concatenate([jnp.cos(angles), jnp.sin(angles)], axis=1).astype(jnp.bfloat16)

def prepare(values, cell_mask, temb, groups):
    count_n, side, other_side, width = values.shape
    grouped = values.reshape(count_n, side, other_side, groups, width // groups)
    weighting = cell_mask[:, :, :, None, None]
    entries = lax.optimization_barrier(jnp.sum(cell_mask, axis=(1, 2))) * (width // groups)
    group_mean = lax.optimization_barrier(jnp.sum(grouped * weighting, axis=(1, 2, 4))) / entries[:, None]
    centered = grouped - group_mean[:, None, None, :, None]
    group_var = lax.optimization_barrier(jnp.sum(centered * centered * weighting, axis=(1, 2, 4))) / entries[:, None]
    normed = (centered * lax.rsqrt(group_var + 1e-05)[:, None, None, :, None]).reshape(count_n, side, other_side, width)
    return jax.nn.silu(normed + temb[:, None, None, :]) * cell_mask[..., None]

def conv_apply(hidden, kernel):
    return lax.conv_general_dilated(hidden, kernel, (1, 1), 'SAME', dimension_numbers=('NHWC', 'HWIO', 'NHWC'), preferred_element_type=jnp.float32)

def block_forward(values, cell_mask, temb, kernel, groups):
    hidden = prepare(values, cell_mask, temb, groups).astype(jnp.bfloat16)
    result = ((values + conv_apply(hidden, kernel)) * cell_mask[..., None]).astype(jnp.bfloat16)
    return (result, hidden)

def block_backward(values, cell_mask, temb, kernel, cot_out, groups):
    residual_cot = cot_out.astype(jnp.float32) * cell_mask[..., None]
    cot_conv = residual_cot.astype(jnp.bfloat16)
    flipped = jnp.transpose(kernel[::-1, ::-1], (0, 1, 3, 2))
    hidden_cot = conv_apply(cot_conv, flipped)
    primal, pull_back = jax.vjp(lambda inner: prepare(inner, cell_mask, temb, groups), values)
    return (residual_cot + pull_back(hidden_cot)[0], cot_conv)

def weight_grad(hidden, cot_conv):
    side = hidden.shape[1]
    width = hidden.shape[3]
    flat_cot = cot_conv.reshape(-1, cot_conv.shape[3])
    padded = jnp.pad(hidden, ((0, 0), (1, 1), (1, 1), (0, 0)))
    rows_list = []
    for row_shift in range(3):
        across = []
        for col_shift in range(3):
            window = padded[:, row_shift:row_shift + side, col_shift:col_shift + side, :].reshape(-1, width)
            across.append(lax.dot_general(window, flat_cot, (((0,), (0,)), ((), ())), preferred_element_type=jnp.float32))
        rows_list.append(jnp.stack(across))
    return jnp.stack(rows_list)

def reference(latents, cotangent, bucket, timesteps, w_enc, w_dec, w_time):
    cell_mask = crop_mask(bucket, P_SIZE)
    embedding = time_embed(timesteps, E)
    loss_scale = float(latents.shape[0] * P_SIZE * P_SIZE) ** (-0.5)
    temb_enc = [jnp.dot(embedding, w_time[index, 0], preferred_element_type=jnp.float32) for index in range(N_SEGMENT)]
    temb_dec = [jnp.dot(embedding, w_time[index, 1], preferred_element_type=jnp.float32) for index in range(N_SEGMENT)]
    enc_inputs = []
    enc_hidden = []
    current = latents
    for index in range(N_SEGMENT):
        enc_inputs.append(current)
        current, hidden = block_forward(current.astype(jnp.float32), cell_mask, temb_enc[index], w_enc[index], G)
        enc_hidden.append(hidden)
    dec_upper = [None] * N_SEGMENT
    dec_hidden = [None] * N_SEGMENT
    for index in reversed(range(N_SEGMENT)):
        dec_upper[index] = current
        summed = current.astype(jnp.float32) + enc_inputs[index].astype(jnp.float32)
        current, hidden = block_forward(summed, cell_mask, temb_dec[index], w_dec[index], G)
        dec_hidden[index] = hidden
    cot_here = (cotangent.astype(jnp.float32) * loss_scale).astype(jnp.bfloat16)
    skip_cot = []
    grad_dec = []
    for index in range(N_SEGMENT):
        summed = dec_upper[index].astype(jnp.float32) + enc_inputs[index].astype(jnp.float32)
        grad_in, cot_conv = block_backward(summed, cell_mask, temb_dec[index], w_dec[index], cot_here, G)
        grad_dec.append(weight_grad(dec_hidden[index], cot_conv))
        cot_here = grad_in.astype(jnp.bfloat16)
        skip_cot.append(cot_here)
    grad_enc = [None] * N_SEGMENT
    for index in reversed(range(N_SEGMENT)):
        grad_in, cot_conv = block_backward(enc_inputs[index].astype(jnp.float32), cell_mask, temb_enc[index], w_enc[index], cot_here, G)
        grad_enc[index] = weight_grad(enc_hidden[index], cot_conv)
        cot_here = (grad_in + skip_cot[index].astype(jnp.float32)).astype(jnp.bfloat16)
    return (jnp.stack(grad_enc), jnp.stack(grad_dec))
```

```python
import functools
import math

import jax
import jax.numpy as jnp
import numpy as np
from jax import lax
from jax.experimental import pallas as pl
from jax.experimental.layout import Layout, with_layout_constraint
from jax.experimental.pallas import tpu as pltpu
from jax.sharding import Mesh, PartitionSpec as P

G = 32
SIDE = 16
CELLS = SIDE * SIDE
C = 320
TAPS = 3 * C
F32 = jnp.float32
BF16 = jnp.bfloat16
VMEM_LIMIT = 40 * 1024 * 1024
LANES = 128
FLAT = 9 * C
TAIL = C - 2 * LANES
PACKED_USED = 2 * FLAT + FLAT // 2
PACKED = 64 * 128

NT = (((1,), (1,)), ((), ()))


def group_matrix():
    index = np.arange(C) // (C // G)
    return jnp.asarray((index[:, None] == index[None, :]).astype(np.float32), BF16)


def group_sums(columns, matrix):
    row = lax.broadcasted_iota(jnp.int32, (16, C), 0)
    stacked = jnp.zeros((16, C), F32)
    for at, column in enumerate(columns):
        high = column.astype(BF16).astype(F32)
        rest = column - high
        middle = rest.astype(BF16).astype(F32)
        low = (rest - middle).astype(BF16).astype(F32)
        for part, value in enumerate((high, middle, low)):
            stacked = jnp.where(row == 3 * at + part, value, stacked)
    sums = jnp.dot(stacked.astype(BF16), matrix, preferred_element_type=F32)
    return [
        sums[3 * at : 3 * at + 1] + sums[3 * at + 1 : 3 * at + 2] + sums[3 * at + 2 : 3 * at + 3]
        for at in range(len(columns))
    ]


def col_sum(values):
    return jnp.sum(values, axis=0, keepdims=True)


def column_index():
    return lax.broadcasted_iota(jnp.int32, (CELLS, C), 0) % SIDE


def shift_right(values, column):
    return jnp.where(column == 0, 0.0, pltpu.roll(values, 1, axis=0))


def shift_left(values, column):
    return jnp.where(column == SIDE - 1, 0.0, pltpu.roll(values, CELLS - 1, axis=0))


def clear_edges(padded):
    width = padded.shape[1]
    padded[0:SIDE, :] = jnp.zeros((SIDE, width), BF16)
    padded[SIDE + CELLS :, :] = jnp.zeros((SIDE, width), BF16)


def store_windows(padded, hidden, column):
    padded[SIDE : SIDE + CELLS, 0:C] = shift_right(hidden, column).astype(BF16)
    padded[SIDE : SIDE + CELLS, C : 2 * C] = hidden.astype(BF16)
    padded[SIDE : SIDE + CELLS, 2 * C : 3 * C] = shift_left(hidden, column).astype(BF16)


def norm_hidden(values, mask, temb, entries, matrix):
    mean = group_sums([col_sum(values * mask)], matrix)[0] / entries
    centered = values - mean
    variance = group_sums([col_sum(centered * centered * mask)], matrix)[0] / entries
    scale = lax.rsqrt(variance + 1e-05)
    normed = centered * scale
    shifted = normed + temb
    hidden = shifted / (1.0 + jnp.exp(-shifted)) * mask
    return normed, scale, hidden


def conv(padded, kernel):
    total = None
    for row in range(3):
        part = jnp.dot(
            padded[row * SIDE : row * SIDE + CELLS, :], kernel[row], preferred_element_type=F32
        )
        total = part if total is None else total + part
    return total


def conv_back(cot_padded, kernel, column):
    total = None
    for row in range(3):
        part = lax.dot_general(
            cot_padded[(2 - row) * SIDE : (2 - row) * SIDE + CELLS, :],
            kernel[row],
            NT,
            preferred_element_type=F32,
        )
        total = part if total is None else total + part
    left, middle, right = total[:, 0:C], total[:, C : 2 * C], total[:, 2 * C : 3 * C]
    return shift_left(left, column) + middle + shift_right(right, column)


def norm_back(hidden_cot, normed, scale, temb, mask, entries, matrix):
    shifted = normed + temb
    gate = 1.0 / (1.0 + jnp.exp(-shifted))
    flow = hidden_cot * mask * (gate * (1.0 + shifted * (1.0 - gate)))
    plain, cross = group_sums([col_sum(flow), col_sum(flow * normed)], matrix)
    return scale * (flow - mask * (plain / entries + normed * (cross / entries)))


def mask_of(bucket_ref, core):
    row = lax.broadcasted_iota(jnp.int32, (CELLS, C), 0)
    inside = (row // SIDE < bucket_ref[core, 0]) & (row % SIDE < bucket_ref[core, 1])
    return inside.astype(F32)


def entries_of(bucket_ref, core):
    return (bucket_ref[core, 0] * bucket_ref[core, 1] * (C // G)).astype(F32)


class Setup:
    def __init__(self, core, bucket, embedding, time_ref, matrix):
        self.core = core
        self.column = column_index()
        self.mask = mask_of(bucket, core)
        self.entries = entries_of(bucket, core)
        self.matrix = matrix[...]
        self.embedding = embedding
        self.time_ref = time_ref

    def temb(self, k, side):
        rows = jnp.dot(self.embedding[...], self.time_ref[k, side], preferred_element_type=F32)
        at = lax.broadcasted_iota(jnp.int32, rows.shape, 0)
        return col_sum(jnp.where(at == self.core, rows, 0.0))


def fetch_pair(core, own, other, target, sems):
    copies = [
        pltpu.make_async_copy(own, target.at[core], sems.at[0]),
        pltpu.make_async_copy(other, target.at[1 - core], sems.at[1]),
    ]
    for copy in copies:
        copy.start()
    return copies


def wait_all(*groups):
    for copies in groups:
        for copy in copies:
            copy.wait()


def forward_block(setup, values, k, side, kernel, padded, out):
    normed_ref, scale_ref, hidden_ref = out
    normed, scale, hidden = norm_hidden(
        values, setup.mask, setup.temb(k, side), setup.entries, setup.matrix
    )
    normed_ref[k] = normed
    scale_ref[k] = jnp.broadcast_to(scale, (8, C))
    hidden_ref[k] = hidden.astype(BF16)
    if kernel is None:
        return None
    store_windows(padded, hidden, setup.column)
    return ((values + conv(padded, kernel)) * setup.mask).astype(BF16)


def encoder_pair(setup, value, w_enc, padded, out, inputs_ref):
    for k in range(2):
        inputs_ref[k] = value
        value = forward_block(setup, value.astype(F32), k, 0, w_enc.at[k], padded, out)
    return value


def decoder_pair(setup, value, w_dec, padded, out, inputs_ref, last):
    for k in (1, 0):
        summed = value.astype(F32) + inputs_ref[k].astype(F32)
        kernel = w_dec.at[k] if last or k == 1 else None
        value = forward_block(setup, summed, k, 1, kernel, padded, out)
    return value


def backward_pair(setup, value, side, order, kernels, padded_cot, kept, cot_ref, skips, skip_in, last):
    normed_ref, scale_ref = kept
    for at, k in enumerate(order):
        residual = value.astype(F32) * setup.mask
        conv_cot = residual.astype(BF16)
        cot_ref[k] = conv_cot
        if at == 1 and not last:
            return None
        padded_cot[SIDE : SIDE + CELLS, :] = conv_cot
        hidden_cot = conv_back(padded_cot, kernels.at[k], setup.column)
        total = residual + norm_back(
            hidden_cot, normed_ref[k], scale_ref[k, 0:1], setup.temb(k, side), setup.mask,
            setup.entries, setup.matrix,
        )
        if skip_in is not None:
            total = total + skip_in[k].astype(F32)
        value = total.astype(BF16)
        if skips is not None:
            skips[k] = value
    return value


def phase_one(
    where, bucket, latents, time_own, time_other, enc_own, enc_other, emb, matrix,
    normed, scale, hidden, kept, sent, x, time_ref, w_enc, padded, sems,
):
    core = where[1]
    enc_copies = fetch_pair(core, enc_own, enc_other, w_enc, sems.at[0])
    time_copies = fetch_pair(core, time_own, time_other, time_ref, sems.at[1])
    x_copy = pltpu.make_async_copy(latents.at[core], x, sems.at[2, 0])
    x_copy.start()
    clear_edges(padded)
    wait_all([x_copy], time_copies, enc_copies)
    setup = Setup(core, bucket, emb, time_ref, matrix)
    sent[...] = encoder_pair(setup, x[...], w_enc, padded, (normed, scale, hidden), kept)


def phase_two(
    where, bucket, x, time_own, time_other, enc_own, enc_other, dec_own, dec_other, emb, matrix,
    e_normed, e_scale, e_hidden, d_normed, d_scale, d_hidden, sent,
    kept, time_ref, w_enc, w_dec, padded, sems,
):
    core = where[1]
    time_copies = fetch_pair(core, time_own, time_other, time_ref, sems.at[1])
    enc_copies = fetch_pair(core, enc_own, enc_other, w_enc, sems.at[0])
    dec_copies = fetch_pair(core, dec_own, dec_other, w_dec, sems.at[2])
    clear_edges(padded)
    wait_all(time_copies, enc_copies)
    setup = Setup(core, bucket, emb, time_ref, matrix)
    upper = encoder_pair(setup, x[...], w_enc, padded, (e_normed, e_scale, e_hidden), kept)
    wait_all(dec_copies)
    sent[...] = decoder_pair(
        setup, upper, w_dec, padded, (d_normed, d_scale, d_hidden), kept, True
    )


def phase_three(
    scaling, where, bucket, x, cotangent, time_own, time_other, dec_own, dec_other, kept, emb,
    matrix, d_hidden, cots, skips, sent,
    d_normed, d_scale, start, time_ref, w_dec, padded, padded_cot, sems,
):
    core = where[1]
    time_copies = fetch_pair(core, time_own, time_other, time_ref, sems.at[1])
    dec_copies = fetch_pair(core, dec_own, dec_other, w_dec, sems.at[0])
    start_copy = pltpu.make_async_copy(cotangent.at[core], start, sems.at[2, 0])
    start_copy.start()
    clear_edges(padded)
    clear_edges(padded_cot)
    wait_all(time_copies, dec_copies, [start_copy])
    setup = Setup(core, bucket, emb, time_ref, matrix)
    decoder_pair(setup, x[...], w_dec, padded, (d_normed, d_scale, d_hidden), kept, False)
    cot = (start[...].astype(F32) * scaling).astype(BF16)
    sent[...] = backward_pair(
        setup, cot, 1, (0, 1), w_dec, padded_cot, (d_normed, d_scale), cots, skips, None, True
    )


def phase_four(
    where, bucket, x, time_own, time_other, enc_own, enc_other, dec_own, dec_other, emb, matrix,
    d_normed, d_scale, e_normed, e_scale, d_cots, e_cots, sent,
    skips, time_ref, w_enc, w_dec, padded_cot, sems,
):
    core = where[1]
    time_copies = fetch_pair(core, time_own, time_other, time_ref, sems.at[1])
    dec_copies = fetch_pair(core, dec_own, dec_other, w_dec, sems.at[0])
    enc_copies = fetch_pair(core, enc_own, enc_other, w_enc, sems.at[2])
    clear_edges(padded_cot)
    wait_all(time_copies, dec_copies)
    setup = Setup(core, bucket, emb, time_ref, matrix)
    cot = backward_pair(
        setup, x[...], 1, (0, 1), w_dec, padded_cot, (d_normed, d_scale), d_cots, skips, None, True
    )
    wait_all(enc_copies)
    sent[...] = backward_pair(
        setup, cot, 0, (1, 0), w_enc, padded_cot, (e_normed, e_scale), e_cots, None, skips, True
    )


def store_packed(target, row, values):
    values = values.astype(target.dtype)
    first = row * TAPS
    target[first : first + TAPS, :] = values[:, 0:LANES]
    target[FLAT + first : FLAT + first + TAPS, :] = values[:, LANES : 2 * LANES]
    half = FLAT // 2
    for begin, end in ((0, TAPS), (0, TAPS // 2), (TAPS // 2, TAPS)):
        low, high = first + begin, first + end
        if row == 1 and end - begin == TAPS or row != 1 and end - begin != TAPS:
            continue
        side = 0 if high <= half else 1
        at = 2 * FLAT + low - side * half
        target[at : at + end - begin, side * TAIL : (side + 1) * TAIL] = values[
            begin:end, 2 * LANES : C
        ]


def store_gradients(core, hidden, cots, own, other, padded_cot, turned):
    column = column_index()
    own[PACKED_USED:, :] = jnp.zeros((PACKED - PACKED_USED, LANES), F32)
    other[PACKED_USED:, :] = jnp.zeros((PACKED - PACKED_USED, LANES), BF16)
    for k in range(2):
        values = hidden[k].astype(F32)
        padded_cot[SIDE : SIDE + CELLS, :] = cots[k]
        turned[0:C, :] = shift_right(values, column).T.astype(BF16)
        turned[C : 2 * C, :] = values.T.astype(BF16)
        turned[2 * C : 3 * C, :] = shift_left(values, column).T.astype(BF16)
        for row in range(3):
            part = jnp.dot(
                turned[...],
                padded_cot[(2 - row) * SIDE : (2 - row) * SIDE + CELLS, :],
                preferred_element_type=F32,
            )

            @pl.when(core == k)
            def _(part=part, row=row):
                store_packed(own, row, part)

            @pl.when(core != k)
            def _(part=part, row=row):
                store_packed(other, row, part)


def weight_phase(
    where, a_hidden, a_cots, b_hidden, b_cots, own, other, padded_cot, turned, hidden, cots
):
    clear_edges(padded_cot)

    @pl.when(where[0] == 0)
    def _():
        hidden[...] = a_hidden[...]
        cots[...] = a_cots[...]

    @pl.when(where[0] != 0)
    def _():
        hidden[...] = b_hidden[...]
        cots[...] = b_cots[...]

    store_gradients(where[1], hidden, cots, own, other, padded_cot, turned)


def phase_five(
    where, bucket, x, time_own, time_other, enc_own, enc_other, skips, emb, matrix,
    e_normed, e_scale, a_hidden, b_hidden, b_cots,
    own, other, padded_cot, turned, hidden, cots, time_ref, w_enc, sems,
):
    clear_edges(padded_cot)
    core = where[1]
    time_copies = fetch_pair(core, time_own, time_other, time_ref, sems.at[1])
    enc_copies = fetch_pair(core, enc_own, enc_other, w_enc, sems.at[0])
    wait_all(time_copies, enc_copies)

    @pl.when(where[0] == 0)
    def _():
        hidden[...] = a_hidden[...]
        setup = Setup(core, bucket, emb, time_ref, matrix)
        backward_pair(
            setup, x[...], 0, (1, 0), w_enc, padded_cot, (e_normed, e_scale), cots, None, skips,
            False,
        )

    @pl.when(where[0] != 0)
    def _():
        hidden[...] = b_hidden[...]
        cots[...] = b_cots[...]

    store_gradients(core, hidden, cots, own, other, padded_cot, turned)


def unpack(packed, grad):
    half = FLAT // 2
    grad[:, 0:LANES] = packed[0:FLAT, :].astype(F32)
    grad[:, LANES : 2 * LANES] = packed[FLAT : 2 * FLAT, :].astype(F32)
    tail = packed[2 * FLAT : PACKED_USED, :].astype(F32)
    grad[0:half, 2 * LANES : C] = tail[:, 0:TAIL]
    grad[half:FLAT, 2 * LANES : C] = tail[:, TAIL : 2 * TAIL]


def shape(dims, dtype):
    return jax.ShapeDtypeStruct(dims, dtype)


NORMED = ((2, CELLS, C), F32)
SCALE = ((2, 8, C), F32)
ACTS = ((2, CELLS, C), BF16)
ONE = ((CELLS, C), BF16)
PADDED = pltpu.VMEM((CELLS + 2 * SIDE, TAPS), BF16)
PADDED_COT = pltpu.VMEM((CELLS + 2 * SIDE, C), BF16)
TURNED = pltpu.VMEM((TAPS, CELLS), BF16)
OWN = ((PACKED, LANES), F32)
OTHER = ((PACKED, LANES), BF16)
WEIGHTS = pltpu.VMEM((2, 3, TAPS, C), BF16)
TIMES = pltpu.VMEM((2, 2, C, C), BF16)
SEMS = pltpu.SemaphoreType.DMA((3, 2))


def call(body, spaces, outs, scratch, flops, name):
    def run(*args):
        kinds = {"s": pltpu.SMEM, "h": pl.ANY, "v": pltpu.VMEM}
        moved = sum(a.size * a.dtype.itemsize for a in args) + sum(
            math.prod(d) * jnp.dtype(t).itemsize for d, t in outs
        )
        return pl.pallas_call(
            body,
            out_shape=tuple(shape(d, t) for d, t in outs),
            in_specs=[pl.BlockSpec(memory_space=kinds[space]) for space in spaces],
            out_specs=tuple(pl.BlockSpec(memory_space=pltpu.VMEM) for _ in outs),
            scratch_shapes=list(scratch),
            compiler_params=pltpu.CompilerParams(vmem_limit_bytes=VMEM_LIMIT),
            cost_estimate=pl.CostEstimate(flops=flops, bytes_accessed=moved, transcendentals=0),
            name=name,
        )(*args)

    return run


CONV = 2 * CELLS * 9 * C * C


def time_embed(timesteps):
    half_width = C // 2
    frequencies = jnp.exp(
        -math.log(10000.0) * jnp.arange(half_width, dtype=F32) / half_width
    )
    angles = timesteps.astype(F32)[:, None] * frequencies[None, :]
    return jnp.concatenate([jnp.cos(angles), jnp.sin(angles)], axis=1).astype(BF16)


DP = ("z", "far", "y")


def row_major(array):
    return with_layout_constraint(array, Layout(major_to_minor=tuple(range(array.ndim))))


def to_other_core(array):
    swap = [(0, 1), (1, 0)]
    return row_major(lax.ppermute(row_major(array), "core", swap))


def sum_by_scatter(pair):
    part = lax.psum_scatter(pair.astype(BF16), DP, scatter_dimension=0, tiled=True)
    return lax.all_gather(part, DP, axis=0, tiled=True)


def sum_by_exchange(pair):
    count = lax.axis_size(DP)
    parts = lax.all_to_all(
        pair.astype(BF16).reshape(count, -1, LANES), DP, split_axis=0, concat_axis=0, tiled=True
    )
    part = jnp.sum(parts.astype(F32), axis=0).astype(BF16)
    return lax.all_gather(part, DP, axis=0, tiled=True)


def local(latents, cotangent, bucket, timesteps, w_enc, w_dec, w_time):
    where = jnp.stack([lax.axis_index("near"), lax.axis_index("core")]).astype(jnp.int32)
    micro_count = latents.shape[0]
    loss_scale = float(micro_count * lax.axis_size(DP) * CELLS) ** (-0.5)

    enc = w_enc.reshape(3, TAPS, C)
    dec = w_dec.reshape(3, TAPS, C)
    times = w_time.reshape(2, C, C)
    enc = (enc, to_other_core(enc))
    times = (times, to_other_core(times))
    dec = (dec, to_other_core(dec))
    latents = latents.reshape(micro_count, CELLS, C)
    cotangent = cotangent.reshape(micro_count, CELLS, C)
    emb = jnp.pad(time_embed(timesteps), ((0, 16 - micro_count), (0, 0)))
    matrix = group_matrix()

    def up(value):
        return lax.ppermute(value, "near", [(0, 1)])

    def down(value):
        return lax.ppermute(value, "near", [(1, 0)])

    one = call(
        phase_one, "ss" + "h" * 5 + "vv", [NORMED, SCALE, ACTS, ACTS, ONE],
        [pltpu.VMEM(*ONE), TIMES, WEIGHTS, PADDED, SEMS], 2 * CONV, "one",
    )
    a_normed, a_scale, a_hidden, a_kept, sent = one(
        where, bucket, latents, *times, *enc, emb, matrix
    )
    two = call(
        phase_two, "ssv" + "h" * 6 + "vv", [NORMED, SCALE, ACTS, NORMED, SCALE, ACTS, ONE],
        [pltpu.VMEM(*ACTS), TIMES, WEIGHTS, WEIGHTS, PADDED, SEMS], 4 * CONV, "two",
    )
    be_normed, be_scale, be_hidden, bd_normed, bd_scale, bd_hidden, sent = two(
        where, bucket, up(sent), *times, *enc, *dec, emb, matrix
    )
    three = call(
        functools.partial(phase_three, loss_scale), "ssv" + "h" * 5 + "vvv",
        [ACTS, ACTS, ACTS, ONE],
        [
            pltpu.VMEM(*NORMED), pltpu.VMEM(*SCALE), pltpu.VMEM(*ONE), TIMES, WEIGHTS, PADDED,
            PADDED_COT, SEMS,
        ],
        3 * CONV, "three",
    )
    ad_hidden, ad_cots, a_skips, sent = three(
        where, bucket, down(sent), cotangent, *times, *dec, a_kept, emb, matrix
    )
    four = call(
        phase_four, "ssv" + "h" * 6 + "v" * 6, [ACTS, ACTS, ONE],
        [pltpu.VMEM(*ACTS), TIMES, WEIGHTS, WEIGHTS, PADDED_COT, SEMS], 4 * CONV, "four",
    )
    bd_cots, be_cots, sent = four(
        where, bucket, up(sent), *times, *enc, *dec, emb, matrix,
        bd_normed, bd_scale, be_normed, be_scale,
    )
    received = down(sent)
    work = [PADDED_COT, TURNED, pltpu.VMEM(*ACTS), pltpu.VMEM(*ACTS)]
    weights = call(weight_phase, "svvvv", [OWN, OTHER], work, 2 * CONV, "weights")
    own_dec, other_dec = weights(where, ad_hidden, ad_cots, bd_hidden, bd_cots)
    five = call(
        phase_five, "ssv" + "h" * 4 + "v" * 8, [OWN, OTHER], [*work, TIMES, WEIGHTS, SEMS],
        3 * CONV, "five",
    )
    own_enc, other_enc = five(
        where, bucket, received, *times, *enc, a_skips, emb, matrix, a_normed, a_scale, a_hidden,
        be_hidden, be_cots,
    )
    spread = call(unpack, "v", [((FLAT, C), F32)], [], 0, "unpack")

    def finish(own, other, add):
        pair = own + lax.ppermute(other, "core", [(0, 1), (1, 0)]).astype(F32)
        (grad,) = spread(add(pair))
        return grad.reshape(1, 3, 3, C, C)

    grad_dec = finish(own_dec, other_dec, sum_by_scatter)
    return finish(own_enc, other_enc, sum_by_exchange), grad_dec


def solution(mesh):
    segments, dp = mesh.shape["segment"], mesh.shape["dp"]
    near, far, rows = segments // 2, 2, 4
    split = Mesh(
        mesh.devices.reshape(near, 2, dp // (far * rows), far, rows),
        ("near", "core", "z", "far", "y"),
    )
    section, micro = ("near", "core"), ("z", "far", "y")
    placed = (
        P(micro, None, None, None),
        P(micro, None, None, None),
        P(micro, None),
        P(micro),
        P(section, None, None, None, None),
        P(section, None, None, None, None),
        P(section, None, None, None),
    )
    grads = P(section, None, None, None, None)
    return jax.shard_map(
        local, mesh=split, in_specs=placed, out_specs=(grads, grads), check_vma=False
    )
```

```python
import functools
import math

import jax
import jax.numpy as jnp
import numpy as np
from jax import lax
from jax.experimental import pallas as pl
from jax.experimental.pallas import tpu as pltpu
from jax.sharding import Mesh, PartitionSpec as P

G = 32
SIDE = 16
CELLS = SIDE * SIDE
C = 320
TAPS = 3 * C
F32 = jnp.float32
BF16 = jnp.bfloat16
VMEM_LIMIT = 30 * 1024 * 1024
LANES = 128
FLAT = 9 * C
TAIL = C - 2 * LANES
PACKED_USED = 2 * FLAT + FLAT // 2
PACKED = 64 * 120

NT = (((1,), (1,)), ((), ()))


def group_matrix():
    index = np.arange(C) // (C // G)
    return jnp.asarray((index[:, None] == index[None, :]).astype(np.float32), BF16)


def group_sums(columns, matrix):
    row = lax.broadcasted_iota(jnp.int32, (16, C), 0)
    stacked = jnp.zeros((16, C), F32)
    for at, column in enumerate(columns):
        high = column.astype(BF16).astype(F32)
        rest = column - high
        middle = rest.astype(BF16).astype(F32)
        low = (rest - middle).astype(BF16).astype(F32)
        for part, value in enumerate((high, middle, low)):
            stacked = jnp.where(row == 3 * at + part, value, stacked)
    sums = jnp.dot(stacked.astype(BF16), matrix, preferred_element_type=F32)
    return [
        sums[3 * at : 3 * at + 1] + sums[3 * at + 1 : 3 * at + 2] + sums[3 * at + 2 : 3 * at + 3]
        for at in range(len(columns))
    ]


def col_sum(values):
    return jnp.sum(values, axis=0, keepdims=True)


def column_index():
    return lax.broadcasted_iota(jnp.int32, (CELLS, C), 0) % SIDE


def shift_right(values, column):
    return jnp.where(column == 0, 0.0, pltpu.roll(values, 1, axis=0))


def shift_left(values, column):
    return jnp.where(column == SIDE - 1, 0.0, pltpu.roll(values, CELLS - 1, axis=0))


def clear_edges(padded):
    width = padded.shape[1]
    padded[0:SIDE, :] = jnp.zeros((SIDE, width), BF16)
    padded[SIDE + CELLS :, :] = jnp.zeros((SIDE, width), BF16)


def store_windows(padded, hidden, column):
    padded[SIDE : SIDE + CELLS, 0:C] = shift_right(hidden, column).astype(BF16)
    padded[SIDE : SIDE + CELLS, C : 2 * C] = hidden.astype(BF16)
    padded[SIDE : SIDE + CELLS, 2 * C : 3 * C] = shift_left(hidden, column).astype(BF16)


def norm_hidden(values, mask, temb, entries, matrix):
    mean = group_sums([col_sum(values * mask)], matrix)[0] / entries
    centered = values - mean
    variance = group_sums([col_sum(centered * centered * mask)], matrix)[0] / entries
    scale = lax.rsqrt(variance + 1e-05)
    normed = centered * scale
    shifted = normed + temb
    hidden = shifted / (1.0 + jnp.exp(-shifted)) * mask
    return normed, scale, hidden


def taps(kernel, row):
    return kernel[3 * row : 3 * row + 3].reshape(TAPS, C)


def conv(padded, kernel):
    total = None
    for row in range(3):
        part = jnp.dot(
            padded[row * SIDE : row * SIDE + CELLS, :], taps(kernel, row), preferred_element_type=F32
        )
        total = part if total is None else total + part
    return total


def conv_back(cot_padded, kernel, column):
    total = None
    for row in range(3):
        part = lax.dot_general(
            cot_padded[(2 - row) * SIDE : (2 - row) * SIDE + CELLS, :],
            taps(kernel, row),
            NT,
            preferred_element_type=F32,
        )
        total = part if total is None else total + part
    left, middle, right = total[:, 0:C], total[:, C : 2 * C], total[:, 2 * C : 3 * C]
    return shift_left(left, column) + middle + shift_right(right, column)


def norm_back(hidden_cot, normed, scale, temb, mask, entries, matrix):
    shifted = normed + temb
    gate = 1.0 / (1.0 + jnp.exp(-shifted))
    flow = hidden_cot * mask * (gate * (1.0 + shifted * (1.0 - gate)))
    plain, cross = group_sums([col_sum(flow), col_sum(flow * normed)], matrix)
    return scale * (flow - mask * (plain / entries + normed * (cross / entries)))


def mask_of(bucket_ref, core):
    row = lax.broadcasted_iota(jnp.int32, (CELLS, C), 0)
    inside = (row // SIDE < bucket_ref[core, 0]) & (row % SIDE < bucket_ref[core, 1])
    return inside.astype(F32)


def entries_of(bucket_ref, core):
    return (bucket_ref[core, 0] * bucket_ref[core, 1] * (C // G)).astype(F32)


class Setup:
    def __init__(self, core, bucket, embedding, time_ref, matrix):
        self.core = core
        self.column = column_index()
        self.mask = mask_of(bucket, core)
        self.entries = entries_of(bucket, core)
        self.matrix = matrix[...]
        self.embedding = embedding
        self.time_ref = time_ref

    def temb(self, k, side):
        rows = jnp.dot(self.embedding[...], self.time_ref[k, side], preferred_element_type=F32)
        at = lax.broadcasted_iota(jnp.int32, rows.shape, 0)
        return col_sum(jnp.where(at == self.core, rows, 0.0))


def fetch_pair(core, own, other, target, sems):
    copies = [
        pltpu.make_async_copy(own, target.at[core], sems.at[0]),
        pltpu.make_async_copy(other, target.at[1 - core], sems.at[1]),
    ]
    for copy in copies:
        copy.start()
    return copies


def wait_all(*groups):
    for copies in groups:
        for copy in copies:
            copy.wait()


def forward_block(setup, values, k, side, kernel, padded, out):
    normed_ref, scale_ref, hidden_ref = out
    normed, scale, hidden = norm_hidden(
        values, setup.mask, setup.temb(k, side), setup.entries, setup.matrix
    )
    normed_ref[k] = normed
    scale_ref[k] = jnp.broadcast_to(scale, (8, C))
    hidden_ref[k] = hidden.astype(BF16)
    if kernel is None:
        return None
    store_windows(padded, hidden, setup.column)
    return ((values + conv(padded, kernel)) * setup.mask).astype(BF16)


def encoder_pair(setup, value, w_enc, padded, out, inputs_ref):
    for k in range(2):
        inputs_ref[k] = value
        value = forward_block(setup, value.astype(F32), k, 0, w_enc.at[k], padded, out)
    return value


def decoder_pair(setup, value, w_dec, padded, out, inputs_ref, last):
    for k in (1, 0):
        summed = value.astype(F32) + inputs_ref[k].astype(F32)
        kernel = w_dec.at[k] if last or k == 1 else None
        value = forward_block(setup, summed, k, 1, kernel, padded, out)
    return value


def backward_pair(setup, value, side, order, kernels, padded_cot, kept, cot_ref, skips, skip_in, last):
    normed_ref, scale_ref = kept
    for at, k in enumerate(order):
        residual = value.astype(F32) * setup.mask
        conv_cot = residual.astype(BF16)
        cot_ref[k] = conv_cot
        if at == 1 and not last:
            return None
        padded_cot[SIDE : SIDE + CELLS, :] = conv_cot
        hidden_cot = conv_back(padded_cot, kernels.at[k], setup.column)
        total = residual + norm_back(
            hidden_cot, normed_ref[k], scale_ref[k, 0:1], setup.temb(k, side), setup.mask,
            setup.entries, setup.matrix,
        )
        if skip_in is not None:
            total = total + skip_in[k].astype(F32)
        value = total.astype(BF16)
        if skips is not None:
            skips[k] = value
    return value


def phase_one(
    where, bucket, latents, time_own, time_other, enc_own, enc_other, emb, matrix,
    normed, scale, hidden, kept, sent, x, time_ref, w_enc, padded, sems,
):
    core = where[1]
    enc_copies = fetch_pair(core, enc_own, enc_other, w_enc, sems.at[0])
    time_copies = fetch_pair(core, time_own, time_other, time_ref, sems.at[1])
    x_copy = pltpu.make_async_copy(latents.at[core], x, sems.at[2, 0])
    x_copy.start()
    clear_edges(padded)
    wait_all([x_copy], time_copies, enc_copies)
    setup = Setup(core, bucket, emb, time_ref, matrix)
    sent[...] = encoder_pair(setup, x[...], w_enc, padded, (normed, scale, hidden), kept)


def phase_two(
    where, bucket, x, time_own, time_other, enc_own, enc_other, dec_own, dec_other, emb, matrix,
    e_normed, e_scale, e_hidden, d_normed, d_scale, d_hidden, sent,
    kept, time_ref, w_enc, w_dec, padded, sems,
):
    core = where[1]
    time_copies = fetch_pair(core, time_own, time_other, time_ref, sems.at[1])
    enc_copies = fetch_pair(core, enc_own, enc_other, w_enc, sems.at[0])
    dec_copies = fetch_pair(core, dec_own, dec_other, w_dec, sems.at[2])
    clear_edges(padded)
    wait_all(time_copies, enc_copies)
    setup = Setup(core, bucket, emb, time_ref, matrix)
    upper = encoder_pair(setup, x[...], w_enc, padded, (e_normed, e_scale, e_hidden), kept)
    wait_all(dec_copies)
    sent[...] = decoder_pair(
        setup, upper, w_dec, padded, (d_normed, d_scale, d_hidden), kept, True
    )


def phase_three(
    scaling, where, bucket, x, cotangent, time_own, time_other, dec_own, dec_other, kept, emb,
    matrix, d_hidden, cots, skips, sent,
    d_normed, d_scale, start, time_ref, w_dec, padded, padded_cot, sems,
):
    core = where[1]
    time_copies = fetch_pair(core, time_own, time_other, time_ref, sems.at[1])
    dec_copies = fetch_pair(core, dec_own, dec_other, w_dec, sems.at[0])
    start_copy = pltpu.make_async_copy(cotangent.at[core], start, sems.at[2, 0])
    start_copy.start()
    clear_edges(padded)
    clear_edges(padded_cot)
    wait_all(time_copies, dec_copies, [start_copy])
    setup = Setup(core, bucket, emb, time_ref, matrix)
    decoder_pair(setup, x[...], w_dec, padded, (d_normed, d_scale, d_hidden), kept, False)
    cot = (start[...].astype(F32) * scaling).astype(BF16)
    sent[...] = backward_pair(
        setup, cot, 1, (0, 1), w_dec, padded_cot, (d_normed, d_scale), cots, skips, None, True
    )


def phase_four(
    where, bucket, x, time_own, time_other, enc_own, enc_other, dec_own, dec_other, emb, matrix,
    d_normed, d_scale, e_normed, e_scale, d_cots, e_cots, sent,
    skips, time_ref, w_enc, w_dec, padded_cot, sems,
):
    core = where[1]
    time_copies = fetch_pair(core, time_own, time_other, time_ref, sems.at[1])
    dec_copies = fetch_pair(core, dec_own, dec_other, w_dec, sems.at[0])
    enc_copies = fetch_pair(core, enc_own, enc_other, w_enc, sems.at[2])
    clear_edges(padded_cot)
    wait_all(time_copies, dec_copies)
    setup = Setup(core, bucket, emb, time_ref, matrix)
    cot = backward_pair(
        setup, x[...], 1, (0, 1), w_dec, padded_cot, (d_normed, d_scale), d_cots, skips, None, True
    )
    wait_all(enc_copies)
    sent[...] = backward_pair(
        setup, cot, 0, (1, 0), w_enc, padded_cot, (e_normed, e_scale), e_cots, None, skips, True
    )


def store_packed(target, row, values):
    values = values.astype(target.dtype)
    first = row * TAPS
    target[first : first + TAPS, :] = values[:, 0:LANES]
    target[FLAT + first : FLAT + first + TAPS, :] = values[:, LANES : 2 * LANES]
    half = FLAT // 2
    for begin, end in ((0, TAPS), (0, TAPS // 2), (TAPS // 2, TAPS)):
        low, high = first + begin, first + end
        if row == 1 and end - begin == TAPS or row != 1 and end - begin != TAPS:
            continue
        side = 0 if high <= half else 1
        at = 2 * FLAT + low - side * half
        target[at : at + end - begin, side * TAIL : (side + 1) * TAIL] = values[
            begin:end, 2 * LANES : C
        ]


def store_gradients(core, hidden, cots, own, other, padded_cot, turned):
    column = column_index()
    own[PACKED_USED:, :] = jnp.zeros((PACKED - PACKED_USED, LANES), F32)
    other[PACKED_USED:, :] = jnp.zeros((PACKED - PACKED_USED, LANES), BF16)
    for k in range(2):
        values = hidden[k].astype(F32)
        padded_cot[SIDE : SIDE + CELLS, :] = cots[k]
        turned[0:C, :] = shift_right(values, column).T.astype(BF16)
        turned[C : 2 * C, :] = values.T.astype(BF16)
        turned[2 * C : 3 * C, :] = shift_left(values, column).T.astype(BF16)
        for row in range(3):
            part = jnp.dot(
                turned[...],
                padded_cot[(2 - row) * SIDE : (2 - row) * SIDE + CELLS, :],
                preferred_element_type=F32,
            )

            @pl.when(core == k)
            def _(part=part, row=row):
                store_packed(own, row, part)

            @pl.when(core != k)
            def _(part=part, row=row):
                store_packed(other, row, part)


def weight_phase(
    where, a_hidden, a_cots, b_hidden, b_cots, own, other, padded_cot, turned, hidden, cots
):
    clear_edges(padded_cot)

    @pl.when(where[0] == 0)
    def _():
        hidden[...] = a_hidden[...]
        cots[...] = a_cots[...]

    @pl.when(where[0] != 0)
    def _():
        hidden[...] = b_hidden[...]
        cots[...] = b_cots[...]

    store_gradients(where[1], hidden, cots, own, other, padded_cot, turned)


def phase_five(
    where, bucket, x, time_own, time_other, enc_own, enc_other, skips, emb, matrix,
    e_normed, e_scale, a_hidden, b_hidden, b_cots,
    own, other, padded_cot, turned, hidden, cots, time_ref, w_enc, sems,
):
    clear_edges(padded_cot)
    core = where[1]
    time_copies = fetch_pair(core, time_own, time_other, time_ref, sems.at[1])
    enc_copies = fetch_pair(core, enc_own, enc_other, w_enc, sems.at[0])
    wait_all(time_copies, enc_copies)

    @pl.when(where[0] == 0)
    def _():
        hidden[...] = a_hidden[...]
        setup = Setup(core, bucket, emb, time_ref, matrix)
        backward_pair(
            setup, x[...], 0, (1, 0), w_enc, padded_cot, (e_normed, e_scale), cots, None, skips,
            False,
        )

    @pl.when(where[0] != 0)
    def _():
        hidden[...] = b_hidden[...]
        cots[...] = b_cots[...]

    store_gradients(core, hidden, cots, own, other, padded_cot, turned)


def unpack(packed, grad):
    half = FLAT // 2
    grad[:, 0:LANES] = packed[0:FLAT, :].astype(F32)
    grad[:, LANES : 2 * LANES] = packed[FLAT : 2 * FLAT, :].astype(F32)
    tail = packed[2 * FLAT : PACKED_USED, :].astype(F32)
    grad[0:half, 2 * LANES : C] = tail[:, 0:TAIL]
    grad[half:FLAT, 2 * LANES : C] = tail[:, TAIL : 2 * TAIL]


def shape(dims, dtype):
    return jax.ShapeDtypeStruct(dims, dtype)


NORMED = ((2, CELLS, C), F32)
SCALE = ((2, 8, C), F32)
ACTS = ((2, CELLS, C), BF16)
ONE = ((CELLS, C), BF16)
PADDED = pltpu.VMEM((CELLS + 2 * SIDE, TAPS), BF16)
PADDED_COT = pltpu.VMEM((CELLS + 2 * SIDE, C), BF16)
TURNED = pltpu.VMEM((TAPS, CELLS), BF16)
OWN = ((PACKED, LANES), F32)
OTHER = ((PACKED, LANES), BF16)
WEIGHTS = pltpu.VMEM((2, 9, C, C), BF16)
TIMES = pltpu.VMEM((2, 2, C, C), BF16)
SEMS = pltpu.SemaphoreType.DMA((3, 2))


def call(body, spaces, outs, scratch, flops, name):
    def run(*args):
        kinds = {"s": pltpu.SMEM, "h": pltpu.HBM, "v": pltpu.VMEM}
        moved = sum(a.size * a.dtype.itemsize for a in args) + sum(
            math.prod(d) * jnp.dtype(t).itemsize for d, t in outs
        )
        return pl.pallas_call(
            body,
            out_shape=tuple(shape(d, t) for d, t in outs),
            in_specs=[pl.BlockSpec(memory_space=kinds[space]) for space in spaces],
            out_specs=tuple(pl.BlockSpec(memory_space=pltpu.VMEM) for _ in outs),
            scratch_shapes=list(scratch),
            compiler_params=pltpu.CompilerParams(vmem_limit_bytes=VMEM_LIMIT),
            cost_estimate=pl.CostEstimate(flops=flops, bytes_accessed=moved, transcendentals=0),
            name=name,
        )(*args)

    return run


CONV = 2 * CELLS * 9 * C * C


def time_embed(timesteps):
    half_width = C // 2
    frequencies = jnp.exp(
        -math.log(10000.0) * jnp.arange(half_width, dtype=F32) / half_width
    )
    angles = timesteps.astype(F32)[:, None] * frequencies[None, :]
    return jnp.concatenate([jnp.cos(angles), jnp.sin(angles)], axis=1).astype(BF16)


DP = ("z", "far", "y")


def to_other_core(array):
    return lax.ppermute(array, "core", [(0, 1), (1, 0)])


def scatter_sum(rows, axes):
    count = lax.axis_size(axes)
    parts = lax.all_to_all(
        rows.astype(BF16).reshape(count, -1, LANES), axes, split_axis=0, concat_axis=0, tiled=True
    )
    return jnp.sum(parts.astype(F32), axis=0)


def gather_rows(rows, axes):
    count = lax.axis_size(axes)
    spread = jnp.broadcast_to(rows[None], (count, *rows.shape))
    return lax.all_to_all(spread, axes, split_axis=0, concat_axis=0, tiled=True).reshape(-1, LANES)


def sum_over_dp(pair):
    part = scatter_sum(scatter_sum(pair, "y"), ("z", "far")).astype(BF16)
    return gather_rows(gather_rows(part, ("z", "far")), "y")


def local(latents, cotangent, bucket, timesteps, w_enc, w_dec, w_time):
    where = jnp.stack([lax.axis_index("near"), lax.axis_index("core")]).astype(jnp.int32)
    micro_count = latents.shape[0]
    loss_scale = float(micro_count * lax.axis_size(DP) * CELLS) ** (-0.5)

    enc = w_enc.reshape(9, C, C)
    dec = w_dec.reshape(9, C, C)
    times = w_time.reshape(2, C, C)
    enc = (enc, to_other_core(enc))
    times = (times, to_other_core(times))
    dec = (dec, to_other_core(dec))
    latents = latents.reshape(micro_count, CELLS, C)
    cotangent = cotangent.reshape(micro_count, CELLS, C)
    emb = jnp.pad(time_embed(timesteps), ((0, 16 - micro_count), (0, 0)))
    matrix = group_matrix()

    def up(value):
        return lax.ppermute(value, "near", [(0, 1)])

    def down(value):
        return lax.ppermute(value, "near", [(1, 0)])

    one = call(
        phase_one, "ss" + "h" * 5 + "vv", [NORMED, SCALE, ACTS, ACTS, ONE],
        [pltpu.VMEM(*ONE), TIMES, WEIGHTS, PADDED, SEMS], 2 * CONV, "one",
    )
    a_normed, a_scale, a_hidden, a_kept, sent = one(
        where, bucket, latents, *times, *enc, emb, matrix
    )
    two = call(
        phase_two, "ssv" + "h" * 6 + "vv", [NORMED, SCALE, ACTS, NORMED, SCALE, ACTS, ONE],
        [pltpu.VMEM(*ACTS), TIMES, WEIGHTS, WEIGHTS, PADDED, SEMS], 4 * CONV, "two",
    )
    be_normed, be_scale, be_hidden, bd_normed, bd_scale, bd_hidden, sent = two(
        where, bucket, up(sent), *times, *enc, *dec, emb, matrix
    )
    three = call(
        functools.partial(phase_three, loss_scale), "ssv" + "h" * 5 + "vvv",
        [ACTS, ACTS, ACTS, ONE],
        [
            pltpu.VMEM(*NORMED), pltpu.VMEM(*SCALE), pltpu.VMEM(*ONE), TIMES, WEIGHTS, PADDED,
            PADDED_COT, SEMS,
        ],
        3 * CONV, "three",
    )
    ad_hidden, ad_cots, a_skips, sent = three(
        where, bucket, down(sent), cotangent, *times, *dec, a_kept, emb, matrix
    )
    four = call(
        phase_four, "ssv" + "h" * 6 + "v" * 6, [ACTS, ACTS, ONE],
        [pltpu.VMEM(*ACTS), TIMES, WEIGHTS, WEIGHTS, PADDED_COT, SEMS], 4 * CONV, "four",
    )
    bd_cots, be_cots, sent = four(
        where, bucket, up(sent), *times, *enc, *dec, emb, matrix,
        bd_normed, bd_scale, be_normed, be_scale,
    )
    received = down(sent)
    work = [PADDED_COT, TURNED, pltpu.VMEM(*ACTS), pltpu.VMEM(*ACTS)]
    weights = call(weight_phase, "svvvv", [OWN, OTHER], work, 2 * CONV, "weights")
    own_dec, other_dec = weights(where, ad_hidden, ad_cots, bd_hidden, bd_cots)
    five = call(
        phase_five, "ssv" + "h" * 4 + "v" * 8, [OWN, OTHER], [*work, TIMES, WEIGHTS, SEMS],
        3 * CONV, "five",
    )
    own_enc, other_enc = five(
        where, bucket, received, *times, *enc, a_skips, emb, matrix, a_normed, a_scale, a_hidden,
        be_hidden, be_cots,
    )
    spread = call(unpack, "v", [((FLAT, C), F32)], [], 0, "unpack")

    def finish(own, other):
        pair = own + lax.ppermute(other, "core", [(0, 1), (1, 0)]).astype(F32)
        (grad,) = spread(sum_over_dp(pair))
        return grad.reshape(1, 3, 3, C, C)

    grad_dec = finish(own_dec, other_dec)
    return finish(own_enc, other_enc), grad_dec


def solution(mesh):
    segments, dp = mesh.shape["segment"], mesh.shape["dp"]
    near, far, rows = segments // 2, 2, 4
    split = Mesh(
        mesh.devices.reshape(near, 2, dp // (far * rows), far, rows),
        ("near", "core", "z", "far", "y"),
    )
    section, micro = ("near", "core"), ("z", "far", "y")
    placed = (
        P(micro, None, None, None),
        P(micro, None, None, None),
        P(micro, None),
        P(micro),
        P(section, None, None, None, None),
        P(section, None, None, None, None),
        P(section, None, None, None),
    )
    grads = P(section, None, None, None, None)
    return jax.shard_map(
        local, mesh=split, in_specs=placed, out_specs=(grads, grads), check_vma=False
    )
```

```python
import functools
import math

import jax
import jax.numpy as jnp
import numpy as np
from jax import lax
from jax.experimental import pallas as pl
from jax.experimental.pallas import tpu as pltpu
from jax.sharding import Mesh, PartitionSpec as P

G = 32
SIDE = 16
CELLS = SIDE * SIDE
C = 320
TAPS = 3 * C
F32 = jnp.float32
BF16 = jnp.bfloat16
VMEM_LIMIT = 30 * 1024 * 1024
LANES = 128
FLAT = 9 * C
TAIL = C - 2 * LANES
PACKED_USED = 2 * FLAT + FLAT // 2
PACKED = 64 * 120
STRIP = 240

NT = (((1,), (1,)), ((), ()))


def group_matrix():
    index = np.arange(C) // (C // G)
    return jnp.asarray((index[:, None] == index[None, :]).astype(np.float32), BF16)


def group_sums(columns, matrix):
    row = lax.broadcasted_iota(jnp.int32, (16, C), 0)
    stacked = jnp.zeros((16, C), F32)
    for at, column in enumerate(columns):
        high = column.astype(BF16).astype(F32)
        rest = column - high
        middle = rest.astype(BF16).astype(F32)
        low = (rest - middle).astype(BF16).astype(F32)
        for part, value in enumerate((high, middle, low)):
            stacked = jnp.where(row == 3 * at + part, value, stacked)
    sums = jnp.dot(stacked.astype(BF16), matrix, preferred_element_type=F32)
    return [
        sums[3 * at : 3 * at + 1] + sums[3 * at + 1 : 3 * at + 2] + sums[3 * at + 2 : 3 * at + 3]
        for at in range(len(columns))
    ]


def col_sum(values):
    return jnp.sum(values, axis=0, keepdims=True)


def column_index():
    return lax.broadcasted_iota(jnp.int32, (CELLS, C), 0) % SIDE


def shift_right(values, column):
    return jnp.where(column == 0, 0.0, pltpu.roll(values, 1, axis=0))


def shift_left(values, column):
    return jnp.where(column == SIDE - 1, 0.0, pltpu.roll(values, CELLS - 1, axis=0))


def clear_edges(padded):
    width = padded.shape[1]
    padded[0:SIDE, :] = jnp.zeros((SIDE, width), BF16)
    padded[SIDE + CELLS :, :] = jnp.zeros((SIDE, width), BF16)


def store_windows(padded, hidden, column):
    padded[SIDE : SIDE + CELLS, 0:C] = shift_right(hidden, column).astype(BF16)
    padded[SIDE : SIDE + CELLS, C : 2 * C] = hidden.astype(BF16)
    padded[SIDE : SIDE + CELLS, 2 * C : 3 * C] = shift_left(hidden, column).astype(BF16)


def norm_hidden(values, mask, temb, entries, matrix):
    mean = group_sums([col_sum(values * mask)], matrix)[0] / entries
    centered = values - mean
    variance = group_sums([col_sum(centered * centered * mask)], matrix)[0] / entries
    scale = lax.rsqrt(variance + 1e-05)
    normed = centered * scale
    shifted = normed + temb
    hidden = shifted / (1.0 + jnp.exp(-shifted)) * mask
    return normed, scale, hidden


def taps(kernel, row):
    return kernel[3 * row : 3 * row + 3].reshape(TAPS, C)


def conv(padded, kernel):
    total = None
    for row in range(3):
        part = jnp.dot(
            padded[row * SIDE : row * SIDE + CELLS, :], taps(kernel, row), preferred_element_type=F32
        )
        total = part if total is None else total + part
    return total


def conv_back(cot_padded, kernel, column):
    total = None
    for row in range(3):
        part = lax.dot_general(
            cot_padded[(2 - row) * SIDE : (2 - row) * SIDE + CELLS, :],
            taps(kernel, row),
            NT,
            preferred_element_type=F32,
        )
        total = part if total is None else total + part
    left, middle, right = total[:, 0:C], total[:, C : 2 * C], total[:, 2 * C : 3 * C]
    return shift_left(left, column) + middle + shift_right(right, column)


def norm_back(hidden_cot, normed, scale, temb, mask, entries, matrix):
    shifted = normed + temb
    gate = 1.0 / (1.0 + jnp.exp(-shifted))
    flow = hidden_cot * mask * (gate * (1.0 + shifted * (1.0 - gate)))
    plain, cross = group_sums([col_sum(flow), col_sum(flow * normed)], matrix)
    return scale * (flow - mask * (plain / entries + normed * (cross / entries)))


def mask_of(bucket_ref, core):
    row = lax.broadcasted_iota(jnp.int32, (CELLS, C), 0)
    inside = (row // SIDE < bucket_ref[core, 0]) & (row % SIDE < bucket_ref[core, 1])
    return inside.astype(F32)


def entries_of(bucket_ref, core):
    return (bucket_ref[core, 0] * bucket_ref[core, 1] * (C // G)).astype(F32)


class Setup:
    def __init__(self, core, bucket, embedding, time_ref, matrix):
        self.core = core
        self.column = column_index()
        self.mask = mask_of(bucket, core)
        self.entries = entries_of(bucket, core)
        self.matrix = matrix[...]
        self.embedding = embedding
        self.time_ref = time_ref

    def temb(self, k, side):
        rows = jnp.dot(self.embedding[...], self.time_ref[k, side], preferred_element_type=F32)
        at = lax.broadcasted_iota(jnp.int32, rows.shape, 0)
        return col_sum(jnp.where(at == self.core, rows, 0.0))


def fetch_pair(core, own, other, target, sems):
    copies = [
        pltpu.make_async_copy(own, target.at[core], sems.at[0]),
        pltpu.make_async_copy(other, target.at[1 - core], sems.at[1]),
    ]
    for copy in copies:
        copy.start()
    return copies


def wait_all(*groups):
    for copies in groups:
        for copy in copies:
            copy.wait()


def forward_block(setup, values, k, side, kernel, padded, out):
    normed_ref, scale_ref, hidden_ref = out
    normed, scale, hidden = norm_hidden(
        values, setup.mask, setup.temb(k, side), setup.entries, setup.matrix
    )
    normed_ref[k] = normed
    scale_ref[k] = jnp.broadcast_to(scale, (8, C))
    hidden_ref[k] = hidden.astype(BF16)
    if kernel is None:
        return None
    store_windows(padded, hidden, setup.column)
    return ((values + conv(padded, kernel)) * setup.mask).astype(BF16)


def encoder_pair(setup, value, w_enc, padded, out, inputs_ref):
    def block(k, value):
        inputs_ref[k] = value
        return forward_block(setup, value.astype(F32), k, 0, w_enc.at[k], padded, out)

    return lax.fori_loop(0, 2, block, value)


def decoder_pair(setup, value, w_dec, padded, out, inputs_ref, last):
    def block(step, value, conv_too=True):
        k = 1 - step
        summed = value.astype(F32) + inputs_ref[k].astype(F32)
        kernel = w_dec.at[k] if conv_too else None
        return forward_block(setup, summed, k, 1, kernel, padded, out)

    if last:
        return lax.fori_loop(0, 2, block, value)
    return block(1, block(0, value), conv_too=False)


def backward_pair(setup, value, side, upward, kernels, padded_cot, kept, cot_ref, skips, skip_in, last):
    normed_ref, scale_ref = kept

    def masked(k, value):
        residual = value.astype(F32) * setup.mask
        conv_cot = residual.astype(BF16)
        cot_ref[k] = conv_cot
        return residual, conv_cot

    def block(step, value):
        k = step if upward else 1 - step
        residual, conv_cot = masked(k, value)
        padded_cot[SIDE : SIDE + CELLS, :] = conv_cot
        hidden_cot = conv_back(padded_cot, kernels.at[k], setup.column)
        total = residual + norm_back(
            hidden_cot, normed_ref[k], scale_ref[k, 0:1], setup.temb(k, side), setup.mask,
            setup.entries, setup.matrix,
        )
        if skip_in is not None:
            total = total + skip_in[k].astype(F32)
        value = total.astype(BF16)
        if skips is not None:
            skips[k] = value
        return value

    if last:
        return lax.fori_loop(0, 2, block, value)
    masked(1 if upward else 0, block(0, value))
    return None


def phase_one(
    where, bucket, latents, time_own, time_other, enc_own, enc_other, emb, matrix,
    normed, scale, hidden, kept, sent, x, time_ref, w_enc, padded, sems,
):
    core = where[1]
    enc_copies = fetch_pair(core, enc_own, enc_other, w_enc, sems.at[0])
    time_copies = fetch_pair(core, time_own, time_other, time_ref, sems.at[1])
    x_copy = pltpu.make_async_copy(latents.at[core], x, sems.at[2, 0])
    x_copy.start()
    clear_edges(padded)
    wait_all([x_copy], time_copies, enc_copies)
    setup = Setup(core, bucket, emb, time_ref, matrix)
    sent[...] = encoder_pair(setup, x[...], w_enc, padded, (normed, scale, hidden), kept)


def phase_two(
    where, bucket, x, time_own, time_other, enc_own, enc_other, dec_own, dec_other, emb, matrix,
    e_normed, e_scale, e_hidden, d_normed, d_scale, d_hidden, sent,
    kept, time_ref, w_enc, w_dec, padded, sems,
):
    core = where[1]
    time_copies = fetch_pair(core, time_own, time_other, time_ref, sems.at[1])
    enc_copies = fetch_pair(core, enc_own, enc_other, w_enc, sems.at[0])
    dec_copies = fetch_pair(core, dec_own, dec_other, w_dec, sems.at[2])
    clear_edges(padded)
    wait_all(time_copies, enc_copies)
    setup = Setup(core, bucket, emb, time_ref, matrix)
    upper = encoder_pair(setup, x[...], w_enc, padded, (e_normed, e_scale, e_hidden), kept)
    wait_all(dec_copies)
    sent[...] = decoder_pair(
        setup, upper, w_dec, padded, (d_normed, d_scale, d_hidden), kept, True
    )


def phase_three(
    scaling, where, bucket, x, cotangent, time_own, time_other, dec_own, dec_other, kept, emb,
    matrix, d_hidden, cots, skips, sent,
    d_normed, d_scale, start, time_ref, w_dec, padded, padded_cot, sems,
):
    core = where[1]
    time_copies = fetch_pair(core, time_own, time_other, time_ref, sems.at[1])
    dec_copies = fetch_pair(core, dec_own, dec_other, w_dec, sems.at[0])
    start_copy = pltpu.make_async_copy(cotangent.at[core], start, sems.at[2, 0])
    start_copy.start()
    clear_edges(padded)
    clear_edges(padded_cot)
    wait_all(time_copies, dec_copies, [start_copy])
    setup = Setup(core, bucket, emb, time_ref, matrix)
    decoder_pair(setup, x[...], w_dec, padded, (d_normed, d_scale, d_hidden), kept, False)
    cot = (start[...].astype(F32) * scaling).astype(BF16)
    sent[...] = backward_pair(
        setup, cot, 1, True, w_dec, padded_cot, (d_normed, d_scale), cots, skips, None, True
    )


def phase_four(
    where, bucket, x, time_own, time_other, enc_own, enc_other, dec_own, dec_other, emb, matrix,
    d_normed, d_scale, e_normed, e_scale, d_cots, e_cots, sent,
    skips, time_ref, w_enc, w_dec, padded_cot, sems,
):
    core = where[1]
    time_copies = fetch_pair(core, time_own, time_other, time_ref, sems.at[1])
    dec_copies = fetch_pair(core, dec_own, dec_other, w_dec, sems.at[0])
    enc_copies = fetch_pair(core, enc_own, enc_other, w_enc, sems.at[2])
    clear_edges(padded_cot)
    wait_all(time_copies, dec_copies)
    setup = Setup(core, bucket, emb, time_ref, matrix)
    cot = backward_pair(
        setup, x[...], 1, True, w_dec, padded_cot, (d_normed, d_scale), d_cots, skips, None, True
    )
    wait_all(enc_copies)
    sent[...] = backward_pair(
        setup, cot, 0, False, w_enc, padded_cot, (e_normed, e_scale), e_cots, None, skips, True
    )


def store_packed(target, slot, row, values):
    first = row * TAPS
    target[slot, first : first + TAPS, :] = values[:, 0:LANES]
    target[slot, FLAT + first : FLAT + first + TAPS, :] = values[:, LANES : 2 * LANES]
    half = FLAT // 2
    pieces = ((0, TAPS // 2), (TAPS // 2, TAPS)) if row == 1 else ((0, TAPS),)
    for begin, end in pieces:
        side = 0 if first + end <= half else 1
        at = 2 * FLAT + first + begin - side * half
        target[slot, at : at + end - begin, side * TAIL : (side + 1) * TAIL] = values[
            begin:end, 2 * LANES : C
        ]


def store_gradients(core, hidden, cots, own, other, padded_cot, turned, pair):
    column = column_index()
    pair[:, PACKED_USED:, :] = jnp.zeros((2, PACKED - PACKED_USED, LANES), F32)

    def section(k, carry):
        values = hidden[k].astype(F32)
        padded_cot[SIDE : SIDE + CELLS, :] = cots[k]
        turned[0:C, :] = shift_right(values, column).T.astype(BF16)
        turned[C : 2 * C, :] = values.T.astype(BF16)
        turned[2 * C : 3 * C, :] = shift_left(values, column).T.astype(BF16)
        for row in range(3):
            part = jnp.dot(
                turned[...],
                padded_cot[(2 - row) * SIDE : (2 - row) * SIDE + CELLS, :],
                preferred_element_type=F32,
            )
            store_packed(pair, jnp.where(core == k, 0, 1), row, part)
        return carry

    lax.fori_loop(0, 2, section, 0)

    def copy(step, carry):
        begin = pl.multiple_of(step * STRIP, STRIP)
        own[pl.ds(begin, STRIP), :] = pair[0, pl.ds(begin, STRIP), :]
        other[pl.ds(begin, STRIP), :] = pair[1, pl.ds(begin, STRIP), :].astype(BF16)
        return carry

    lax.fori_loop(0, PACKED // STRIP, copy, 0)


def weight_phase(
    where, a_hidden, a_cots, b_hidden, b_cots, own, other, padded_cot, turned, pair, hidden, cots
):
    clear_edges(padded_cot)

    @pl.when(where[0] == 0)
    def _():
        hidden[...] = a_hidden[...]
        cots[...] = a_cots[...]

    @pl.when(where[0] != 0)
    def _():
        hidden[...] = b_hidden[...]
        cots[...] = b_cots[...]

    store_gradients(where[1], hidden, cots, own, other, padded_cot, turned, pair)


def phase_five(
    where, bucket, x, time_own, time_other, enc_own, enc_other, skips, emb, matrix,
    e_normed, e_scale, a_hidden, b_hidden, b_cots,
    own, other, padded_cot, turned, pair, hidden, cots, time_ref, w_enc, sems,
):
    clear_edges(padded_cot)
    core = where[1]
    time_copies = fetch_pair(core, time_own, time_other, time_ref, sems.at[1])
    enc_copies = fetch_pair(core, enc_own, enc_other, w_enc, sems.at[0])
    wait_all(time_copies, enc_copies)

    @pl.when(where[0] == 0)
    def _():
        hidden[...] = a_hidden[...]
        setup = Setup(core, bucket, emb, time_ref, matrix)
        backward_pair(
            setup, x[...], 0, False, w_enc, padded_cot, (e_normed, e_scale), cots, None, skips,
            False,
        )

    @pl.when(where[0] != 0)
    def _():
        hidden[...] = b_hidden[...]
        cots[...] = b_cots[...]

    store_gradients(core, hidden, cots, own, other, padded_cot, turned, pair)


def emit_chunks(total, me, kept, chunks):
    count = len(chunks) + 1
    rows = total.shape[0] // count
    for ahead in range(count):
        begin = pl.multiple_of(lax.rem(me + ahead, count) * rows, 8)
        part = total[pl.ds(begin, rows), :]
        if ahead == 0:
            kept[...] = part
        else:
            chunks[ahead - 1][...] = part.astype(BF16)


def place_chunks(target, me, chunks):
    count = len(chunks)
    rows = target.shape[0] // count
    for behind, chunk in enumerate(chunks):
        begin = pl.multiple_of(lax.rem(me + count - behind, count) * rows, 8)
        target[pl.ds(begin, rows), :] = chunk[...].astype(F32)


def core_split(where, own, other, kept, *chunks):
    count = len(chunks) + 1
    rows = own.shape[0] // count
    for ahead in range(count):
        begin = pl.multiple_of(lax.rem(where[2] + ahead, count) * rows, 16)
        part = own[pl.ds(begin, rows), :] + other[pl.ds(begin, rows), :].astype(F32)
        if ahead == 0:
            kept[...] = part
        else:
            chunks[ahead - 1][...] = part.astype(BF16)


def sum_of(kept, received):
    value = kept[...]
    for part in received:
        value = value + part[...].astype(F32)
    return value


def plane_split(planes, where, before, *rest):
    received, (kept, *chunks), total = rest[: planes - 1], rest[planes - 1 : -1], rest[-1]
    total[...] = sum_of(before, received)
    emit_chunks(total, where[3], kept, chunks)


def last_sum(before, *rest):
    *received, out = rest
    out[...] = sum_of(before, received).astype(BF16)


def assemble(where, *rest):
    *chunks, out, total = rest
    place_chunks(total, where[3], chunks)
    out[...] = total[...].astype(BF16)


def unpack(where, *rest):
    *chunks, grad, packed = rest
    place_chunks(packed, where[2], chunks)
    half = FLAT // 2

    def strip(step, carry):
        begin = pl.multiple_of(step * STRIP, STRIP)
        for side in range(2):
            at = begin + side * half
            grad[pl.ds(at, STRIP), 0:LANES] = packed[pl.ds(at, STRIP), :]
            grad[pl.ds(at, STRIP), LANES : 2 * LANES] = packed[pl.ds(FLAT + at, STRIP), :]
        tail = packed[pl.ds(2 * FLAT + begin, STRIP), :]
        grad[pl.ds(begin, STRIP), 2 * LANES : C] = tail[:, 0:TAIL]
        grad[pl.ds(begin + half, STRIP), 2 * LANES : C] = tail[:, TAIL : 2 * TAIL]
        return carry

    lax.fori_loop(0, half // STRIP, strip, 0)


def shape(dims, dtype):
    return jax.ShapeDtypeStruct(dims, dtype)


NORMED = ((2, CELLS, C), F32)
SCALE = ((2, 8, C), F32)
ACTS = ((2, CELLS, C), BF16)
ONE = ((CELLS, C), BF16)
PADDED = pltpu.VMEM((CELLS + 2 * SIDE, TAPS), BF16)
PADDED_COT = pltpu.VMEM((CELLS + 2 * SIDE, C), BF16)
TURNED = pltpu.VMEM((TAPS, CELLS), BF16)
OWN = ((PACKED, LANES), F32)
OTHER = ((PACKED, LANES), BF16)
WEIGHTS = pltpu.VMEM((2, 9, C, C), BF16)
TIMES = pltpu.VMEM((2, 2, C, C), BF16)
SEMS = pltpu.SemaphoreType.DMA((3, 2))


def call(body, spaces, outs, scratch, flops, name):
    def run(*args):
        kinds = {"s": pltpu.SMEM, "h": pltpu.HBM, "v": pltpu.VMEM}
        moved = sum(a.size * a.dtype.itemsize for a in args) + sum(
            math.prod(d) * jnp.dtype(t).itemsize for d, t in outs
        )
        return pl.pallas_call(
            body,
            out_shape=tuple(shape(d, t) for d, t in outs),
            in_specs=[pl.BlockSpec(memory_space=kinds[space]) for space in spaces],
            out_specs=tuple(pl.BlockSpec(memory_space=pltpu.VMEM) for _ in outs),
            scratch_shapes=list(scratch),
            compiler_params=pltpu.CompilerParams(vmem_limit_bytes=VMEM_LIMIT),
            cost_estimate=pl.CostEstimate(flops=flops, bytes_accessed=moved, transcendentals=0),
            name=name,
        )(*args)

    return run


CONV = 2 * CELLS * 9 * C * C


def time_embed(timesteps):
    half_width = C // 2
    frequencies = jnp.exp(
        -math.log(10000.0) * jnp.arange(half_width, dtype=F32) / half_width
    )
    angles = timesteps.astype(F32)[:, None] * frequencies[None, :]
    return jnp.concatenate([jnp.cos(angles), jnp.sin(angles)], axis=1).astype(BF16)


DP = ("z", "far", "y")


def to_other_core(array):
    return lax.ppermute(array, "core", [(0, 1), (1, 0)])


def ahead(value, axes, steps):
    count = lax.axis_size(axes)
    return lax.ppermute(value, axes, [(at, (at + steps) % count) for at in range(count)])


PLANE = ("far", "y")


def plane_chunks(where, own, other):
    planes = lax.axis_size(PLANE)
    rows = PACKED // planes
    return call(
        core_split, "svv", [((rows, LANES), F32)] + [((rows, LANES), BF16)] * (planes - 1),
        [], PACKED * LANES, "core_split",
    )(where, own, to_other_core(other))


def sum_over_dp(where, kept, *chunks):
    planes, layers = lax.axis_size(PLANE), lax.axis_size("z")
    rows = PACKED // planes
    part = rows // layers
    received = [ahead(chunk, PLANE, step + 1) for step, chunk in enumerate(chunks)]
    kept, *chunks = call(
        functools.partial(plane_split, planes), "s" + "v" * planes,
        [((part, LANES), F32)] + [((part, LANES), BF16)] * (layers - 1),
        [pltpu.VMEM((rows, LANES), F32)], PACKED * LANES, "plane_split",
    )(where, kept, *received)
    received = [ahead(chunk, "z", step + 1) for step, chunk in enumerate(chunks)]
    (mine,) = call(
        last_sum, "v" * layers, [((part, LANES), BF16)], [], rows * LANES, "last_sum"
    )(kept, *received)
    received = [ahead(mine, "z", step) for step in range(1, layers)]
    (mine,) = call(
        assemble, "s" + "v" * layers, [((rows, LANES), BF16)],
        [pltpu.VMEM((rows, LANES), F32)], rows * LANES, "assemble",
    )(where, mine, *received)
    received = [ahead(mine, PLANE, step) for step in range(1, planes)]
    (grad,) = call(
        unpack, "s" + "v" * planes, [((FLAT, C), F32)],
        [pltpu.VMEM((PACKED, LANES), F32)], PACKED * LANES, "unpack",
    )(where, mine, *received)
    return grad.reshape(1, 3, 3, C, C)


def local(latents, cotangent, bucket, timesteps, w_enc, w_dec, w_time):
    where = jnp.stack([lax.axis_index(axis) for axis in ("near", "core", PLANE, "z")])
    where = where.astype(jnp.int32)
    micro_count = latents.shape[0]
    loss_scale = float(micro_count * lax.axis_size(DP) * CELLS) ** (-0.5)

    enc = w_enc.reshape(9, C, C)
    dec = w_dec.reshape(9, C, C)
    times = w_time.reshape(2, C, C)
    enc = (enc, to_other_core(enc))
    times = (times, to_other_core(times))
    dec = (dec, to_other_core(dec))
    latents = latents.reshape(micro_count, CELLS, C)
    cotangent = cotangent.reshape(micro_count, CELLS, C)
    emb = jnp.pad(time_embed(timesteps), ((0, 16 - micro_count), (0, 0)))
    matrix = group_matrix()

    def up(value):
        return lax.ppermute(value, "near", [(0, 1)])

    def down(value):
        return lax.ppermute(value, "near", [(1, 0)])

    one = call(
        phase_one, "ss" + "h" * 5 + "vv", [NORMED, SCALE, ACTS, ACTS, ONE],
        [pltpu.VMEM(*ONE), TIMES, WEIGHTS, PADDED, SEMS], 2 * CONV, "one",
    )
    a_normed, a_scale, a_hidden, a_kept, sent = one(
        where, bucket, latents, *times, *enc, emb, matrix
    )
    two = call(
        phase_two, "ssv" + "h" * 6 + "vv", [NORMED, SCALE, ACTS, NORMED, SCALE, ACTS, ONE],
        [pltpu.VMEM(*ACTS), TIMES, WEIGHTS, WEIGHTS, PADDED, SEMS], 4 * CONV, "two",
    )
    be_normed, be_scale, be_hidden, bd_normed, bd_scale, bd_hidden, sent = two(
        where, bucket, up(sent), *times, *enc, *dec, emb, matrix
    )
    three = call(
        functools.partial(phase_three, loss_scale), "ssv" + "h" * 5 + "vvv",
        [ACTS, ACTS, ACTS, ONE],
        [
            pltpu.VMEM(*NORMED), pltpu.VMEM(*SCALE), pltpu.VMEM(*ONE), TIMES, WEIGHTS, PADDED,
            PADDED_COT, SEMS,
        ],
        3 * CONV, "three",
    )
    ad_hidden, ad_cots, a_skips, sent = three(
        where, bucket, down(sent), cotangent, *times, *dec, a_kept, emb, matrix
    )
    four = call(
        phase_four, "ssv" + "h" * 6 + "v" * 6, [ACTS, ACTS, ONE],
        [pltpu.VMEM(*ACTS), TIMES, WEIGHTS, WEIGHTS, PADDED_COT, SEMS], 4 * CONV, "four",
    )
    bd_cots, be_cots, sent = four(
        where, bucket, up(sent), *times, *enc, *dec, emb, matrix,
        bd_normed, bd_scale, be_normed, be_scale,
    )
    received = down(sent)
    work = [PADDED_COT, TURNED, pltpu.VMEM((2, PACKED, LANES), F32), pltpu.VMEM(*ACTS), pltpu.VMEM(*ACTS)]
    weights = call(weight_phase, "svvvv", [OWN, OTHER], work, 2 * CONV, "weights")
    dec_chunks = plane_chunks(where, *weights(where, ad_hidden, ad_cots, bd_hidden, bd_cots))
    received, dec_chunks = lax.optimization_barrier((received, dec_chunks))
    five = call(
        phase_five, "ssv" + "h" * 4 + "v" * 8, [OWN, OTHER], [*work, TIMES, WEIGHTS, SEMS],
        3 * CONV, "five",
    )
    enc_grads = five(
        where, bucket, received, *times, *enc, a_skips, emb, matrix, a_normed, a_scale, a_hidden,
        be_hidden, be_cots,
    )

    enc_chunks = plane_chunks(where, *enc_grads)
    return sum_over_dp(where, *enc_chunks), sum_over_dp(where, *dec_chunks)


def solution(mesh):
    segments, dp = mesh.shape["segment"], mesh.shape["dp"]
    near, far, rows = segments // 2, 2, 4
    split = Mesh(
        mesh.devices.reshape(near, 2, dp // (far * rows), far, rows),
        ("near", "core", "z", "far", "y"),
    )
    section, micro = ("near", "core"), ("z", "far", "y")
    placed = (
        P(micro, None, None, None),
        P(micro, None, None, None),
        P(micro, None),
        P(micro),
        P(section, None, None, None, None),
        P(section, None, None, None, None),
        P(section, None, None, None),
    )
    grads = P(section, None, None, None, None)
    return jax.shard_map(
        local, mesh=split, in_specs=placed, out_specs=(grads, grads), check_vma=False
    )
```

```python
import functools
import math

import jax
import jax.numpy as jnp
import numpy as np
from jax import lax
from jax.experimental import pallas as pl
from jax.experimental.pallas import tpu as pltpu
from jax.sharding import Mesh, PartitionSpec as P

G = 32
SIDE = 16
CELLS = SIDE * SIDE
C = 320
TAPS = 3 * C
F32 = jnp.float32
BF16 = jnp.bfloat16
VMEM_LIMIT = 30 * 1024 * 1024
ALL_VMEM = 60 * 1024 * 1024
LANES = 128
FLAT = 9 * C
TAIL = C - 2 * LANES
PACKED_USED = 2 * FLAT + FLAT // 2
PACKED = 64 * 120
STRIP = 240

NT = (((1,), (1,)), ((), ()))


def group_matrix():
    index = np.arange(C) // (C // G)
    return jnp.asarray((index[:, None] == index[None, :]).astype(np.float32), BF16)


def group_sums(columns, matrix):
    row = lax.broadcasted_iota(jnp.int32, (16, C), 0)
    stacked = jnp.zeros((16, C), F32)
    for at, column in enumerate(columns):
        high = column.astype(BF16).astype(F32)
        rest = column - high
        middle = rest.astype(BF16).astype(F32)
        low = (rest - middle).astype(BF16).astype(F32)
        for part, value in enumerate((high, middle, low)):
            stacked = jnp.where(row == 3 * at + part, value, stacked)
    sums = jnp.dot(stacked.astype(BF16), matrix, preferred_element_type=F32)
    return [
        sums[3 * at : 3 * at + 1] + sums[3 * at + 1 : 3 * at + 2] + sums[3 * at + 2 : 3 * at + 3]
        for at in range(len(columns))
    ]


def col_sum(values):
    return jnp.sum(values, axis=0, keepdims=True)


def column_index():
    return lax.broadcasted_iota(jnp.int32, (CELLS, C), 0) % SIDE


def shift_right(values, column):
    return jnp.where(column == 0, 0.0, pltpu.roll(values, 1, axis=0))


def shift_left(values, column):
    return jnp.where(column == SIDE - 1, 0.0, pltpu.roll(values, CELLS - 1, axis=0))


def clear_edges(padded):
    width = padded.shape[1]
    padded[0:SIDE, :] = jnp.zeros((SIDE, width), BF16)
    padded[SIDE + CELLS :, :] = jnp.zeros((SIDE, width), BF16)


def store_windows(padded, hidden, column):
    padded[SIDE : SIDE + CELLS, 0:C] = shift_right(hidden, column).astype(BF16)
    padded[SIDE : SIDE + CELLS, C : 2 * C] = hidden.astype(BF16)
    padded[SIDE : SIDE + CELLS, 2 * C : 3 * C] = shift_left(hidden, column).astype(BF16)


def norm_hidden(values, mask, temb, entries, matrix):
    mean = group_sums([col_sum(values * mask)], matrix)[0] / entries
    centered = values - mean
    variance = group_sums([col_sum(centered * centered * mask)], matrix)[0] / entries
    scale = lax.rsqrt(variance + 1e-05)
    normed = centered * scale
    shifted = normed + temb
    hidden = shifted / (1.0 + jnp.exp(-shifted)) * mask
    return normed, scale, hidden


def taps(kernel, row):
    return kernel[3 * row : 3 * row + 3].reshape(TAPS, C)


def conv(padded, kernel):
    total = None
    for row in range(3):
        part = jnp.dot(
            padded[row * SIDE : row * SIDE + CELLS, :], taps(kernel, row), preferred_element_type=F32
        )
        total = part if total is None else total + part
    return total


def conv_back(cot_padded, kernel, column):
    total = None
    for row in range(3):
        part = lax.dot_general(
            cot_padded[(2 - row) * SIDE : (2 - row) * SIDE + CELLS, :],
            taps(kernel, row),
            NT,
            preferred_element_type=F32,
        )
        total = part if total is None else total + part
    left, middle, right = total[:, 0:C], total[:, C : 2 * C], total[:, 2 * C : 3 * C]
    return shift_left(left, column) + middle + shift_right(right, column)


def norm_back(hidden_cot, normed, scale, temb, mask, entries, matrix):
    shifted = normed + temb
    gate = 1.0 / (1.0 + jnp.exp(-shifted))
    flow = hidden_cot * mask * (gate * (1.0 + shifted * (1.0 - gate)))
    plain, cross = group_sums([col_sum(flow), col_sum(flow * normed)], matrix)
    return scale * (flow - mask * (plain / entries + normed * (cross / entries)))


def mask_of(bucket_ref, core):
    row = lax.broadcasted_iota(jnp.int32, (CELLS, C), 0)
    inside = (row // SIDE < bucket_ref[core, 0]) & (row % SIDE < bucket_ref[core, 1])
    return inside.astype(F32)


def entries_of(bucket_ref, core):
    return (bucket_ref[core, 0] * bucket_ref[core, 1] * (C // G)).astype(F32)


class Setup:
    def __init__(self, core, bucket, embedding, time_ref, matrix):
        self.core = core
        self.column = column_index()
        self.mask = mask_of(bucket, core)
        self.entries = entries_of(bucket, core)
        self.matrix = matrix[...]
        self.embedding = embedding
        self.time_ref = time_ref

    def temb(self, k, side):
        rows = jnp.dot(self.embedding[...], self.time_ref[k, side], preferred_element_type=F32)
        at = lax.broadcasted_iota(jnp.int32, rows.shape, 0)
        return col_sum(jnp.where(at == self.core, rows, 0.0))


def fetch_pair(core, own, other, target, sems):
    copies = [
        pltpu.make_async_copy(own, target.at[core], sems.at[0]),
        pltpu.make_async_copy(other, target.at[1 - core], sems.at[1]),
    ]
    for copy in copies:
        copy.start()
    return copies


def wait_all(*groups):
    for copies in groups:
        for copy in copies:
            copy.wait()


def forward_block(setup, values, k, side, kernel, padded, out):
    normed_ref, scale_ref, hidden_ref = out
    normed, scale, hidden = norm_hidden(
        values, setup.mask, setup.temb(k, side), setup.entries, setup.matrix
    )
    normed_ref[k] = normed
    scale_ref[k] = jnp.broadcast_to(scale, (8, C))
    hidden_ref[k] = hidden.astype(BF16)
    if kernel is None:
        return None
    store_windows(padded, hidden, setup.column)
    return ((values + conv(padded, kernel)) * setup.mask).astype(BF16)


def encoder_pair(setup, value, w_enc, padded, out, inputs_ref):
    def block(k, value):
        inputs_ref[k] = value
        return forward_block(setup, value.astype(F32), k, 0, w_enc.at[k], padded, out)

    return lax.fori_loop(0, 2, block, value)


def decoder_pair(setup, value, w_dec, padded, out, inputs_ref, last):
    def block(step, value, conv_too=True):
        k = 1 - step
        summed = value.astype(F32) + inputs_ref[k].astype(F32)
        kernel = w_dec.at[k] if conv_too else None
        return forward_block(setup, summed, k, 1, kernel, padded, out)

    if last:
        return lax.fori_loop(0, 2, block, value)
    return block(1, block(0, value), conv_too=False)


def backward_pair(setup, value, side, upward, kernels, padded_cot, kept, cot_ref, skips, skip_in, last):
    normed_ref, scale_ref = kept

    def masked(k, value):
        residual = value.astype(F32) * setup.mask
        conv_cot = residual.astype(BF16)
        cot_ref[k] = conv_cot
        return residual, conv_cot

    def block(step, value):
        k = step if upward else 1 - step
        residual, conv_cot = masked(k, value)
        padded_cot[SIDE : SIDE + CELLS, :] = conv_cot
        hidden_cot = conv_back(padded_cot, kernels.at[k], setup.column)
        total = residual + norm_back(
            hidden_cot, normed_ref[k], scale_ref[k, 0:1], setup.temb(k, side), setup.mask,
            setup.entries, setup.matrix,
        )
        if skip_in is not None:
            total = total + skip_in[k].astype(F32)
        value = total.astype(BF16)
        if skips is not None:
            skips[k] = value
        return value

    if last:
        return lax.fori_loop(0, 2, block, value)
    masked(1 if upward else 0, block(0, value))
    return None


def phase_one(
    where, bucket, latents, time_own, time_other, enc_own, enc_other, emb, matrix,
    normed, scale, hidden, kept, sent, x, time_ref, w_enc, padded, sems,
):
    core = where[1]
    enc_copies = fetch_pair(core, enc_own, enc_other, w_enc, sems.at[0])
    time_copies = fetch_pair(core, time_own, time_other, time_ref, sems.at[1])
    x_copy = pltpu.make_async_copy(latents.at[core], x, sems.at[2, 0])
    x_copy.start()
    clear_edges(padded)
    wait_all([x_copy], time_copies, enc_copies)
    setup = Setup(core, bucket, emb, time_ref, matrix)
    sent[...] = encoder_pair(setup, x[...], w_enc, padded, (normed, scale, hidden), kept)


def phase_two(
    where, bucket, x, time_own, time_other, enc_own, enc_other, dec_own, dec_other, emb, matrix,
    e_normed, e_scale, e_hidden, d_normed, d_scale, d_hidden, sent,
    kept, time_ref, w_enc, w_dec, padded, sems,
):
    core = where[1]
    time_copies = fetch_pair(core, time_own, time_other, time_ref, sems.at[1])
    enc_copies = fetch_pair(core, enc_own, enc_other, w_enc, sems.at[0])
    dec_copies = fetch_pair(core, dec_own, dec_other, w_dec, sems.at[2])
    clear_edges(padded)
    wait_all(time_copies, enc_copies)
    setup = Setup(core, bucket, emb, time_ref, matrix)
    upper = encoder_pair(setup, x[...], w_enc, padded, (e_normed, e_scale, e_hidden), kept)
    wait_all(dec_copies)
    sent[...] = decoder_pair(
        setup, upper, w_dec, padded, (d_normed, d_scale, d_hidden), kept, True
    )


def phase_three(
    scaling, where, bucket, x, cotangent, time_own, time_other, dec_own, dec_other, kept, emb,
    matrix, d_hidden, cots, skips, sent,
    d_normed, d_scale, start, time_ref, w_dec, padded, padded_cot, sems,
):
    core = where[1]
    time_copies = fetch_pair(core, time_own, time_other, time_ref, sems.at[1])
    dec_copies = fetch_pair(core, dec_own, dec_other, w_dec, sems.at[0])
    start_copy = pltpu.make_async_copy(cotangent.at[core], start, sems.at[2, 0])
    start_copy.start()
    clear_edges(padded)
    clear_edges(padded_cot)
    wait_all(time_copies, dec_copies, [start_copy])
    setup = Setup(core, bucket, emb, time_ref, matrix)
    decoder_pair(setup, x[...], w_dec, padded, (d_normed, d_scale, d_hidden), kept, False)
    cot = (start[...].astype(F32) * scaling).astype(BF16)
    sent[...] = backward_pair(
        setup, cot, 1, True, w_dec, padded_cot, (d_normed, d_scale), cots, skips, None, True
    )


def phase_four(
    where, bucket, x, time_own, time_other, enc_own, enc_other, dec_own, dec_other, emb, matrix,
    d_normed, d_scale, e_normed, e_scale, d_cots, e_cots, sent,
    skips, time_ref, w_enc, w_dec, padded_cot, sems,
):
    core = where[1]
    time_copies = fetch_pair(core, time_own, time_other, time_ref, sems.at[1])
    dec_copies = fetch_pair(core, dec_own, dec_other, w_dec, sems.at[0])
    enc_copies = fetch_pair(core, enc_own, enc_other, w_enc, sems.at[2])
    clear_edges(padded_cot)
    wait_all(time_copies, dec_copies)
    setup = Setup(core, bucket, emb, time_ref, matrix)
    cot = backward_pair(
        setup, x[...], 1, True, w_dec, padded_cot, (d_normed, d_scale), d_cots, skips, None, True
    )
    wait_all(enc_copies)
    sent[...] = backward_pair(
        setup, cot, 0, False, w_enc, padded_cot, (e_normed, e_scale), e_cots, None, skips, True
    )


def store_packed(target, slot, row, values):
    first = row * TAPS
    target[slot, first : first + TAPS, :] = values[:, 0:LANES]
    target[slot, FLAT + first : FLAT + first + TAPS, :] = values[:, LANES : 2 * LANES]
    half = FLAT // 2
    pieces = ((0, TAPS // 2), (TAPS // 2, TAPS)) if row == 1 else ((0, TAPS),)
    for begin, end in pieces:
        side = 0 if first + end <= half else 1
        at = 2 * FLAT + first + begin - side * half
        target[slot, at : at + end - begin, side * TAIL : (side + 1) * TAIL] = values[
            begin:end, 2 * LANES : C
        ]


def store_gradients(core, hidden, cots, own, other, padded_cot, turned, pair):
    column = column_index()
    pair[:, PACKED_USED:, :] = jnp.zeros((2, PACKED - PACKED_USED, LANES), F32)

    def section(k, carry):
        values = hidden[k].astype(F32)
        padded_cot[SIDE : SIDE + CELLS, :] = cots[k]
        turned[0:C, :] = shift_right(values, column).T.astype(BF16)
        turned[C : 2 * C, :] = values.T.astype(BF16)
        turned[2 * C : 3 * C, :] = shift_left(values, column).T.astype(BF16)
        for row in range(3):
            part = jnp.dot(
                turned[...],
                padded_cot[(2 - row) * SIDE : (2 - row) * SIDE + CELLS, :],
                preferred_element_type=F32,
            )
            store_packed(pair, jnp.where(core == k, 0, 1), row, part)
        return carry

    lax.fori_loop(0, 2, section, 0)

    def copy(step, carry):
        begin = pl.multiple_of(step * STRIP, STRIP)
        own[pl.ds(begin, STRIP), :] = pair[0, pl.ds(begin, STRIP), :]
        other[pl.ds(begin, STRIP), :] = pair[1, pl.ds(begin, STRIP), :].astype(BF16)
        return carry

    lax.fori_loop(0, PACKED // STRIP, copy, 0)


def weight_phase(
    where, a_hidden, a_cots, b_hidden, b_cots, own, other, padded_cot, turned, pair, hidden, cots
):
    clear_edges(padded_cot)

    @pl.when(where[0] == 0)
    def _():
        hidden[...] = a_hidden[...]
        cots[...] = a_cots[...]

    @pl.when(where[0] != 0)
    def _():
        hidden[...] = b_hidden[...]
        cots[...] = b_cots[...]

    store_gradients(where[1], hidden, cots, own, other, padded_cot, turned, pair)


def phase_five(
    where, bucket, x, time_own, time_other, enc_own, enc_other, skips, emb, matrix,
    e_normed, e_scale, a_hidden, b_hidden, b_cots,
    own, other, padded_cot, turned, pair, hidden, cots, time_ref, w_enc, sems,
):
    clear_edges(padded_cot)
    core = where[1]
    time_copies = fetch_pair(core, time_own, time_other, time_ref, sems.at[1])
    enc_copies = fetch_pair(core, enc_own, enc_other, w_enc, sems.at[0])
    wait_all(time_copies, enc_copies)

    @pl.when(where[0] == 0)
    def _():
        hidden[...] = a_hidden[...]
        setup = Setup(core, bucket, emb, time_ref, matrix)
        backward_pair(
            setup, x[...], 0, False, w_enc, padded_cot, (e_normed, e_scale), cots, None, skips,
            False,
        )

    @pl.when(where[0] != 0)
    def _():
        hidden[...] = b_hidden[...]
        cots[...] = b_cots[...]

    store_gradients(core, hidden, cots, own, other, padded_cot, turned, pair)


def emit_chunks(total, me, kept, chunks):
    count = len(chunks) + 1
    rows = total.shape[0] // count
    for ahead in range(count):
        begin = pl.multiple_of(lax.rem(me + ahead, count) * rows, 8)
        part = total[pl.ds(begin, rows), :]
        if ahead == 0:
            kept[...] = part
        else:
            chunks[ahead - 1][...] = part.astype(BF16)


def place_chunks(target, me, chunks):
    count = len(chunks)
    rows = target.shape[0] // count
    for behind, chunk in enumerate(chunks):
        begin = pl.multiple_of(lax.rem(me + count - behind, count) * rows, 8)
        target[pl.ds(begin, rows), :] = chunk[...].astype(F32)


def core_add(own, other, out):
    def strip(step, carry):
        at = pl.ds(pl.multiple_of(step * 2 * STRIP, 2 * STRIP), 2 * STRIP)
        out[at, :] = (own[at, :] + other[at, :].astype(F32)).astype(BF16)
        return carry

    lax.fori_loop(0, PACKED // (2 * STRIP), strip, 0)


def sum_of(kept, received):
    value = kept[...]
    for part in received:
        value = value + part[...].astype(F32)
    return value


def block_sum(where, parts, kept, *rest):
    *chunks, total = rest
    value = parts[0].astype(F32)
    for at in range(1, parts.shape[0]):
        value = value + parts[at].astype(F32)
    total[...] = value
    emit_chunks(total, where[2], kept, chunks)


def last_sum(before, *rest):
    *received, out = rest
    out[...] = sum_of(before, received).astype(BF16)


def assemble(where, *rest):
    *chunks, out, total = rest
    place_chunks(total, where[2], chunks)
    value = total[...].astype(BF16)
    for at in range(out.shape[0]):
        out[at] = value


def unpack(packed, grad):
    half = FLAT // 2

    def strip(step, carry):
        begin = pl.multiple_of(step * 2 * STRIP, 2 * STRIP)
        for side in range(2):
            at = begin + side * half
            grad[pl.ds(at, 2 * STRIP), 0:LANES] = packed[pl.ds(at, 2 * STRIP), :].astype(F32)
            grad[pl.ds(at, 2 * STRIP), LANES : 2 * LANES] = packed[
                pl.ds(FLAT + at, 2 * STRIP), :
            ].astype(F32)
        tail = packed[pl.ds(2 * FLAT + begin, 2 * STRIP), :].astype(F32)
        grad[pl.ds(begin, 2 * STRIP), 2 * LANES : C] = tail[:, 0:TAIL]
        grad[pl.ds(begin + half, 2 * STRIP), 2 * LANES : C] = tail[:, TAIL : 2 * TAIL]
        return carry

    lax.fori_loop(0, half // (2 * STRIP), strip, 0)


def shape(dims, dtype):
    return jax.ShapeDtypeStruct(dims, dtype)


NORMED = ((2, CELLS, C), F32)
SCALE = ((2, 8, C), F32)
ACTS = ((2, CELLS, C), BF16)
ONE = ((CELLS, C), BF16)
PADDED = pltpu.VMEM((CELLS + 2 * SIDE, TAPS), BF16)
PADDED_COT = pltpu.VMEM((CELLS + 2 * SIDE, C), BF16)
TURNED = pltpu.VMEM((TAPS, CELLS), BF16)
OWN = ((PACKED, LANES), F32)
OTHER = ((PACKED, LANES), BF16)
WEIGHTS = pltpu.VMEM((2, 9, C, C), BF16)
TIMES = pltpu.VMEM((2, 2, C, C), BF16)
SEMS = pltpu.SemaphoreType.DMA((3, 2))


def call(body, spaces, outs, scratch, flops, name, vmem=VMEM_LIMIT):
    def run(*args):
        kinds = {"s": pltpu.SMEM, "h": pltpu.HBM, "v": pltpu.VMEM}
        moved = sum(a.size * a.dtype.itemsize for a in args) + sum(
            math.prod(d) * jnp.dtype(t).itemsize for d, t in outs
        )
        return pl.pallas_call(
            body,
            out_shape=tuple(shape(d, t) for d, t in outs),
            in_specs=[pl.BlockSpec(memory_space=kinds[space]) for space in spaces],
            out_specs=tuple(pl.BlockSpec(memory_space=pltpu.VMEM) for _ in outs),
            scratch_shapes=list(scratch),
            compiler_params=pltpu.CompilerParams(vmem_limit_bytes=vmem),
            cost_estimate=pl.CostEstimate(flops=flops, bytes_accessed=moved, transcendentals=0),
            name=name,
        )(*args)

    return run


CONV = 2 * CELLS * 9 * C * C


def time_embed(timesteps):
    half_width = C // 2
    frequencies = jnp.exp(
        -math.log(10000.0) * jnp.arange(half_width, dtype=F32) / half_width
    )
    angles = timesteps.astype(F32)[:, None] * frequencies[None, :]
    return jnp.concatenate([jnp.cos(angles), jnp.sin(angles)], axis=1).astype(BF16)


DP = ("z", "far", "y")


def to_other_core(array):
    return lax.ppermute(array, "core", [(0, 1), (1, 0)])


def ahead(value, axes, steps):
    count = lax.axis_size(axes)
    return lax.ppermute(value, axes, [(at, (at + steps) % count) for at in range(count)])


BLOCK = ("z_low", "far", "y")
LAYERS = "z_high"
DP = (LAYERS, *BLOCK)


def exchange(parts):
    return lax.all_to_all(parts, BLOCK, split_axis=0, concat_axis=0, tiled=True)


def core_sum(own, other):
    (pair,) = call(core_add, "vv", [((PACKED, LANES), BF16)], [], PACKED * LANES, "core_add", ALL_VMEM)(
        own, to_other_core(other)
    )
    return pair


def spread_parts(pair):
    count = lax.axis_size(BLOCK)
    return exchange(pair.reshape(count, PACKED // count, LANES))


def layer_sum(where, parts):
    count, rows, _ = parts.shape
    layers = lax.axis_size(LAYERS)
    part = (rows // layers, LANES)
    kept, *chunks = call(
        block_sum, "sv", [(part, F32)] + [(part, BF16)] * (layers - 1),
        [pltpu.VMEM((rows, LANES), F32)], PACKED * LANES, "block_sum",
    )(where, parts)
    received = [ahead(chunk, LAYERS, step + 1) for step, chunk in enumerate(chunks)]
    (mine,) = call(last_sum, "v" * layers, [(part, BF16)], [], rows * LANES, "last_sum")(
        kept, *received
    )
    received = [ahead(mine, LAYERS, step) for step in range(1, layers)]
    (copies,) = call(
        assemble, "s" + "v" * layers, [((count, rows, LANES), BF16)],
        [pltpu.VMEM((rows, LANES), F32)], PACKED * LANES, "assemble",
    )(where, mine, *received)
    return copies


def gradient(packed):
    (grad,) = call(unpack, "v", [((FLAT, C), F32)], [], PACKED * LANES, "unpack")(
        packed.reshape(PACKED, LANES)
    )
    return grad.reshape(1, 3, 3, C, C)


def local(latents, cotangent, bucket, timesteps, w_enc, w_dec, w_time):
    where = jnp.stack([lax.axis_index(axis) for axis in ("near", "core", LAYERS)])
    where = where.astype(jnp.int32)
    micro_count = latents.shape[0]
    loss_scale = float(micro_count * lax.axis_size(DP) * CELLS) ** (-0.5)

    enc = w_enc.reshape(9, C, C)
    dec = w_dec.reshape(9, C, C)
    times = w_time.reshape(2, C, C)
    enc = (enc, to_other_core(enc))
    times = (times, to_other_core(times))
    dec = (dec, to_other_core(dec))
    latents = latents.reshape(micro_count, CELLS, C)
    cotangent = cotangent.reshape(micro_count, CELLS, C)
    emb = jnp.pad(time_embed(timesteps), ((0, 16 - micro_count), (0, 0)))
    matrix = group_matrix()

    def up(value):
        return lax.ppermute(value, "near", [(0, 1)])

    def down(value):
        return lax.ppermute(value, "near", [(1, 0)])

    one = call(
        phase_one, "ss" + "h" * 5 + "vv", [NORMED, SCALE, ACTS, ACTS, ONE],
        [pltpu.VMEM(*ONE), TIMES, WEIGHTS, PADDED, SEMS], 2 * CONV, "one", ALL_VMEM,
    )
    a_normed, a_scale, a_hidden, a_kept, sent = one(
        where, bucket, latents, *times, *enc, emb, matrix
    )
    two = call(
        phase_two, "ssv" + "h" * 6 + "vv", [NORMED, SCALE, ACTS, NORMED, SCALE, ACTS, ONE],
        [pltpu.VMEM(*ACTS), TIMES, WEIGHTS, WEIGHTS, PADDED, SEMS], 4 * CONV, "two", ALL_VMEM,
    )
    be_normed, be_scale, be_hidden, bd_normed, bd_scale, bd_hidden, sent = two(
        where, bucket, up(sent), *times, *enc, *dec, emb, matrix
    )
    three = call(
        functools.partial(phase_three, loss_scale), "ssv" + "h" * 5 + "vvv",
        [ACTS, ACTS, ACTS, ONE],
        [
            pltpu.VMEM(*NORMED), pltpu.VMEM(*SCALE), pltpu.VMEM(*ONE), TIMES, WEIGHTS, PADDED,
            PADDED_COT, SEMS,
        ],
        3 * CONV, "three", ALL_VMEM,
    )
    ad_hidden, ad_cots, a_skips, sent = three(
        where, bucket, down(sent), cotangent, *times, *dec, a_kept, emb, matrix
    )
    four = call(
        phase_four, "ssv" + "h" * 6 + "v" * 6, [ACTS, ACTS, ONE],
        [pltpu.VMEM(*ACTS), TIMES, WEIGHTS, WEIGHTS, PADDED_COT, SEMS], 4 * CONV, "four", ALL_VMEM,
    )
    bd_cots, be_cots, sent = four(
        where, bucket, up(sent), *times, *enc, *dec, emb, matrix,
        bd_normed, bd_scale, be_normed, be_scale,
    )
    received = down(sent)
    work = [PADDED_COT, TURNED, pltpu.VMEM((2, PACKED, LANES), F32), pltpu.VMEM(*ACTS), pltpu.VMEM(*ACTS)]
    weights = call(weight_phase, "svvvv", [OWN, OTHER], work, 2 * CONV, "weights", ALL_VMEM)
    dec_pair = core_sum(*weights(where, ad_hidden, ad_cots, bd_hidden, bd_cots))
    received, dec_pair = lax.optimization_barrier((received, dec_pair))
    dec_parts = spread_parts(dec_pair)
    five = call(
        phase_five, "ssv" + "h" * 4 + "v" * 8, [OWN, OTHER], [*work, TIMES, WEIGHTS, SEMS],
        3 * CONV, "five", ALL_VMEM,
    )
    enc_grads = five(
        where, bucket, received, *times, *enc, a_skips, emb, matrix, a_normed, a_scale, a_hidden,
        be_hidden, be_cots,
    )

    enc_parts = spread_parts(core_sum(*enc_grads))
    dec_copies = exchange(layer_sum(where, dec_parts))
    enc_copies = exchange(layer_sum(where, enc_parts))
    return gradient(enc_copies), gradient(dec_copies)


def solution(mesh):
    segments, dp = mesh.shape["segment"], mesh.shape["dp"]
    near, far, rows = segments // 2, 2, 4
    split = Mesh(
        mesh.devices.reshape(near, 2, dp // (2 * far * rows), 2, far, rows),
        ("near", "core", *DP),
    )
    section, micro = ("near", "core"), DP
    placed = (
        P(micro, None, None, None),
        P(micro, None, None, None),
        P(micro, None),
        P(micro),
        P(section, None, None, None, None),
        P(section, None, None, None, None),
        P(section, None, None, None),
    )
    grads = P(section, None, None, None, None)
    return jax.shard_map(
        local, mesh=split, in_specs=placed, out_specs=(grads, grads), check_vma=False
    )
```

```python
import functools
import math

import jax
import jax.numpy as jnp
import numpy as np
from jax import lax
from jax.experimental import pallas as pl
from jax.experimental.pallas import tpu as pltpu
from jax.sharding import Mesh, PartitionSpec as P

G = 32
SIDE = 16
CELLS = SIDE * SIDE
C = 320
TAPS = 3 * C
F32 = jnp.float32
BF16 = jnp.bfloat16
VMEM_LIMIT = 30 * 1024 * 1024
ALL_VMEM = 60 * 1024 * 1024
LANES = 128
FLAT = 9 * C
TAIL = C - 2 * LANES
PACKED_USED = 2 * FLAT + FLAT // 2
PACKED = 64 * 120
STRIP = 240

NT = (((1,), (1,)), ((), ()))


def group_matrix():
    index = np.arange(C) // (C // G)
    return jnp.asarray((index[:, None] == index[None, :]).astype(np.float32), BF16)


def group_sums(columns, matrix):
    row = lax.broadcasted_iota(jnp.int32, (16, C), 0)
    stacked = jnp.zeros((16, C), F32)
    for at, column in enumerate(columns):
        high = column.astype(BF16).astype(F32)
        rest = column - high
        middle = rest.astype(BF16).astype(F32)
        low = (rest - middle).astype(BF16).astype(F32)
        for part, value in enumerate((high, middle, low)):
            stacked = jnp.where(row == 3 * at + part, value, stacked)
    sums = jnp.dot(stacked.astype(BF16), matrix, preferred_element_type=F32)
    return [
        sums[3 * at : 3 * at + 1] + sums[3 * at + 1 : 3 * at + 2] + sums[3 * at + 2 : 3 * at + 3]
        for at in range(len(columns))
    ]


def col_sum(values):
    return jnp.sum(values, axis=0, keepdims=True)


def column_index():
    return lax.broadcasted_iota(jnp.int32, (CELLS, C), 0) % SIDE


def shift_right(values, column):
    return jnp.where(column == 0, 0.0, pltpu.roll(values, 1, axis=0))


def shift_left(values, column):
    return jnp.where(column == SIDE - 1, 0.0, pltpu.roll(values, CELLS - 1, axis=0))


def clear_edges(padded):
    width = padded.shape[1]
    padded[0:SIDE, :] = jnp.zeros((SIDE, width), BF16)
    padded[SIDE + CELLS :, :] = jnp.zeros((SIDE, width), BF16)


def store_windows(padded, hidden, column):
    padded[SIDE : SIDE + CELLS, 0:C] = shift_right(hidden, column).astype(BF16)
    padded[SIDE : SIDE + CELLS, C : 2 * C] = hidden.astype(BF16)
    padded[SIDE : SIDE + CELLS, 2 * C : 3 * C] = shift_left(hidden, column).astype(BF16)


def norm_hidden(values, mask, temb, entries, matrix):
    mean = group_sums([col_sum(values * mask)], matrix)[0] / entries
    centered = values - mean
    variance = group_sums([col_sum(centered * centered * mask)], matrix)[0] / entries
    scale = lax.rsqrt(variance + 1e-05)
    normed = centered * scale
    shifted = normed + temb
    hidden = shifted / (1.0 + jnp.exp(-shifted)) * mask
    return normed, scale, hidden


def taps(kernel, row):
    return kernel[3 * row : 3 * row + 3].reshape(TAPS, C)


def conv(padded, kernel):
    total = None
    for row in range(3):
        part = jnp.dot(
            padded[row * SIDE : row * SIDE + CELLS, :], taps(kernel, row), preferred_element_type=F32
        )
        total = part if total is None else total + part
    return total


def conv_back(cot_padded, kernel, column):
    total = None
    for row in range(3):
        part = lax.dot_general(
            cot_padded[(2 - row) * SIDE : (2 - row) * SIDE + CELLS, :],
            taps(kernel, row),
            NT,
            preferred_element_type=F32,
        )
        total = part if total is None else total + part
    left, middle, right = total[:, 0:C], total[:, C : 2 * C], total[:, 2 * C : 3 * C]
    return shift_left(left, column) + middle + shift_right(right, column)


def norm_back(hidden_cot, normed, scale, temb, mask, entries, matrix):
    shifted = normed + temb
    gate = 1.0 / (1.0 + jnp.exp(-shifted))
    flow = hidden_cot * mask * (gate * (1.0 + shifted * (1.0 - gate)))
    plain, cross = group_sums([col_sum(flow), col_sum(flow * normed)], matrix)
    return scale * (flow - mask * (plain / entries + normed * (cross / entries)))


def mask_of(bucket_ref, core):
    row = lax.broadcasted_iota(jnp.int32, (CELLS, C), 0)
    inside = (row // SIDE < bucket_ref[core, 0]) & (row % SIDE < bucket_ref[core, 1])
    return inside.astype(F32)


def entries_of(bucket_ref, core):
    return (bucket_ref[core, 0] * bucket_ref[core, 1] * (C // G)).astype(F32)


class Setup:
    def __init__(self, core, bucket, embedding, time_ref, matrix):
        self.core = core
        self.column = column_index()
        self.mask = mask_of(bucket, core)
        self.entries = entries_of(bucket, core)
        self.matrix = matrix[...]
        self.embedding = embedding
        self.time_ref = time_ref

    def temb(self, k, side):
        rows = jnp.dot(self.embedding[...], self.time_ref[k, side], preferred_element_type=F32)
        at = lax.broadcasted_iota(jnp.int32, rows.shape, 0)
        return col_sum(jnp.where(at == self.core, rows, 0.0))


def fetch_pair(core, own, other, target, sems):
    copies = [
        pltpu.make_async_copy(own, target.at[core], sems.at[0]),
        pltpu.make_async_copy(other, target.at[1 - core], sems.at[1]),
    ]
    for copy in copies:
        copy.start()
    return copies


def wait_all(*groups):
    for copies in groups:
        for copy in copies:
            copy.wait()


def forward_block(setup, values, k, side, kernel, padded, out):
    normed_ref, scale_ref, hidden_ref = out
    normed, scale, hidden = norm_hidden(
        values, setup.mask, setup.temb(k, side), setup.entries, setup.matrix
    )
    normed_ref[k] = normed
    scale_ref[k] = jnp.broadcast_to(scale, (8, C))
    hidden_ref[k] = hidden.astype(BF16)
    if kernel is None:
        return None
    store_windows(padded, hidden, setup.column)
    return ((values + conv(padded, kernel)) * setup.mask).astype(BF16)


def encoder_pair(setup, value, w_enc, padded, out, inputs_ref):
    def block(k, value):
        inputs_ref[k] = value
        return forward_block(setup, value.astype(F32), k, 0, w_enc.at[k], padded, out)

    return lax.fori_loop(0, 2, block, value)


def decoder_pair(setup, value, w_dec, padded, out, inputs_ref, last):
    def block(step, value, conv_too=True):
        k = 1 - step
        summed = value.astype(F32) + inputs_ref[k].astype(F32)
        kernel = w_dec.at[k] if conv_too else None
        return forward_block(setup, summed, k, 1, kernel, padded, out)

    if last:
        return lax.fori_loop(0, 2, block, value)
    return block(1, block(0, value), conv_too=False)


def backward_pair(setup, value, side, upward, kernels, padded_cot, kept, cot_ref, skips, skip_in, last):
    normed_ref, scale_ref = kept

    def masked(k, value):
        residual = value.astype(F32) * setup.mask
        conv_cot = residual.astype(BF16)
        cot_ref[k] = conv_cot
        return residual, conv_cot

    def block(step, value):
        k = step if upward else 1 - step
        residual, conv_cot = masked(k, value)
        padded_cot[SIDE : SIDE + CELLS, :] = conv_cot
        hidden_cot = conv_back(padded_cot, kernels.at[k], setup.column)
        total = residual + norm_back(
            hidden_cot, normed_ref[k], scale_ref[k, 0:1], setup.temb(k, side), setup.mask,
            setup.entries, setup.matrix,
        )
        if skip_in is not None:
            total = total + skip_in[k].astype(F32)
        value = total.astype(BF16)
        if skips is not None:
            skips[k] = value
        return value

    if last:
        return lax.fori_loop(0, 2, block, value)
    masked(1 if upward else 0, block(0, value))
    return None


def phase_one(
    where, bucket, latents, time_own, time_other, enc_own, enc_other, emb, matrix,
    normed, scale, hidden, kept, sent, x, time_ref, w_enc, padded, sems,
):
    core = where[1]
    enc_copies = fetch_pair(core, enc_own, enc_other, w_enc, sems.at[0])
    time_copies = fetch_pair(core, time_own, time_other, time_ref, sems.at[1])
    x_copy = pltpu.make_async_copy(latents.at[core], x, sems.at[2, 0])
    x_copy.start()
    clear_edges(padded)
    wait_all([x_copy], time_copies, enc_copies)
    setup = Setup(core, bucket, emb, time_ref, matrix)
    sent[...] = encoder_pair(setup, x[...], w_enc, padded, (normed, scale, hidden), kept)


def phase_two(
    where, bucket, x, time_own, time_other, enc_own, enc_other, dec_own, dec_other, emb, matrix,
    e_normed, e_scale, e_hidden, d_normed, d_scale, d_hidden, sent,
    kept, time_ref, w_enc, w_dec, padded, sems,
):
    core = where[1]
    time_copies = fetch_pair(core, time_own, time_other, time_ref, sems.at[1])
    enc_copies = fetch_pair(core, enc_own, enc_other, w_enc, sems.at[0])
    dec_copies = fetch_pair(core, dec_own, dec_other, w_dec, sems.at[2])
    clear_edges(padded)
    wait_all(time_copies, enc_copies)
    setup = Setup(core, bucket, emb, time_ref, matrix)
    upper = encoder_pair(setup, x[...], w_enc, padded, (e_normed, e_scale, e_hidden), kept)
    wait_all(dec_copies)
    sent[...] = decoder_pair(
        setup, upper, w_dec, padded, (d_normed, d_scale, d_hidden), kept, True
    )


def phase_three(
    scaling, where, bucket, x, cotangent, time_own, time_other, dec_own, dec_other, kept, emb,
    matrix, d_hidden, cots, skips, sent,
    d_normed, d_scale, start, time_ref, w_dec, padded, padded_cot, sems,
):
    core = where[1]
    time_copies = fetch_pair(core, time_own, time_other, time_ref, sems.at[1])
    dec_copies = fetch_pair(core, dec_own, dec_other, w_dec, sems.at[0])
    start_copy = pltpu.make_async_copy(cotangent.at[core], start, sems.at[2, 0])
    start_copy.start()
    clear_edges(padded)
    clear_edges(padded_cot)
    wait_all(time_copies, dec_copies, [start_copy])
    setup = Setup(core, bucket, emb, time_ref, matrix)
    decoder_pair(setup, x[...], w_dec, padded, (d_normed, d_scale, d_hidden), kept, False)
    cot = (start[...].astype(F32) * scaling).astype(BF16)
    sent[...] = backward_pair(
        setup, cot, 1, True, w_dec, padded_cot, (d_normed, d_scale), cots, skips, None, True
    )


def phase_four(
    where, bucket, x, time_own, time_other, enc_own, enc_other, dec_own, dec_other, emb, matrix,
    d_normed, d_scale, e_normed, e_scale, d_cots, e_cots, sent,
    skips, time_ref, w_enc, w_dec, padded_cot, sems,
):
    core = where[1]
    time_copies = fetch_pair(core, time_own, time_other, time_ref, sems.at[1])
    dec_copies = fetch_pair(core, dec_own, dec_other, w_dec, sems.at[0])
    enc_copies = fetch_pair(core, enc_own, enc_other, w_enc, sems.at[2])
    clear_edges(padded_cot)
    wait_all(time_copies, dec_copies)
    setup = Setup(core, bucket, emb, time_ref, matrix)
    cot = backward_pair(
        setup, x[...], 1, True, w_dec, padded_cot, (d_normed, d_scale), d_cots, skips, None, True
    )
    wait_all(enc_copies)
    sent[...] = backward_pair(
        setup, cot, 0, False, w_enc, padded_cot, (e_normed, e_scale), e_cots, None, skips, True
    )


def store_packed(target, slot, row, values):
    first = row * TAPS
    target[slot, first : first + TAPS, :] = values[:, 0:LANES]
    target[slot, FLAT + first : FLAT + first + TAPS, :] = values[:, LANES : 2 * LANES]
    half = FLAT // 2
    pieces = ((0, TAPS // 2), (TAPS // 2, TAPS)) if row == 1 else ((0, TAPS),)
    for begin, end in pieces:
        side = 0 if first + end <= half else 1
        at = 2 * FLAT + first + begin - side * half
        target[slot, at : at + end - begin, side * TAIL : (side + 1) * TAIL] = values[
            begin:end, 2 * LANES : C
        ]


def store_gradients(core, hidden, cots, own, other, padded_cot, turned, pair):
    column = column_index()
    pair[:, PACKED_USED:, :] = jnp.zeros((2, PACKED - PACKED_USED, LANES), F32)

    def section(k, carry):
        values = hidden[k].astype(F32)
        padded_cot[SIDE : SIDE + CELLS, :] = cots[k]
        turned[0:C, :] = shift_right(values, column).T.astype(BF16)
        turned[C : 2 * C, :] = values.T.astype(BF16)
        turned[2 * C : 3 * C, :] = shift_left(values, column).T.astype(BF16)
        for row in range(3):
            part = jnp.dot(
                turned[...],
                padded_cot[(2 - row) * SIDE : (2 - row) * SIDE + CELLS, :],
                preferred_element_type=F32,
            )
            store_packed(pair, jnp.where(core == k, 0, 1), row, part)
        return carry

    lax.fori_loop(0, 2, section, 0)

    def copy(step, carry):
        begin = pl.multiple_of(step * STRIP, STRIP)
        own[pl.ds(begin, STRIP), :] = pair[0, pl.ds(begin, STRIP), :]
        other[pl.ds(begin, STRIP), :] = pair[1, pl.ds(begin, STRIP), :].astype(BF16)
        return carry

    lax.fori_loop(0, PACKED // STRIP, copy, 0)


def weight_phase(
    where, a_hidden, a_cots, b_hidden, b_cots, own, other, padded_cot, turned, pair, hidden, cots
):
    clear_edges(padded_cot)

    @pl.when(where[0] == 0)
    def _():
        hidden[...] = a_hidden[...]
        cots[...] = a_cots[...]

    @pl.when(where[0] != 0)
    def _():
        hidden[...] = b_hidden[...]
        cots[...] = b_cots[...]

    store_gradients(where[1], hidden, cots, own, other, padded_cot, turned, pair)


def phase_five(
    where, bucket, x, time_own, time_other, enc_own, enc_other, skips, emb, matrix,
    e_normed, e_scale, a_hidden, b_hidden, b_cots,
    own, other, padded_cot, turned, pair, hidden, cots, time_ref, w_enc, sems,
):
    clear_edges(padded_cot)
    core = where[1]
    time_copies = fetch_pair(core, time_own, time_other, time_ref, sems.at[1])
    enc_copies = fetch_pair(core, enc_own, enc_other, w_enc, sems.at[0])
    wait_all(time_copies, enc_copies)

    @pl.when(where[0] == 0)
    def _():
        hidden[...] = a_hidden[...]
        setup = Setup(core, bucket, emb, time_ref, matrix)
        backward_pair(
            setup, x[...], 0, False, w_enc, padded_cot, (e_normed, e_scale), cots, None, skips,
            False,
        )

    @pl.when(where[0] != 0)
    def _():
        hidden[...] = b_hidden[...]
        cots[...] = b_cots[...]

    store_gradients(core, hidden, cots, own, other, padded_cot, turned, pair)


def core_add(own, other, out):
    def strip(step, carry):
        at = pl.ds(pl.multiple_of(step * 2 * STRIP, 2 * STRIP), 2 * STRIP)
        out[at, :] = (own[at, :] + other[at, :].astype(F32)).astype(BF16)
        return carry

    lax.fori_loop(0, PACKED // (2 * STRIP), strip, 0)


def added(parts):
    value = parts[0].astype(F32)
    for at in range(1, parts.shape[0]):
        value = value + parts[at].astype(F32)
    return value


def block_sums(first, second, out):
    rows = out.shape[2]
    for which, parts in enumerate((first, second)):
        value = added(parts)
        for layer in range(out.shape[0]):
            out[layer, which] = value[layer * rows : (layer + 1) * rows].astype(BF16)


def layer_sums(parts, out):
    value = added(parts).astype(BF16)
    for layer in range(out.shape[0]):
        out[layer] = value


def assemble(parts, out, total):
    layers, _, rows, _ = parts.shape
    for which in range(2):
        for layer in range(layers):
            begin = (which * layers + layer) * rows
            total[begin : begin + rows, :] = parts[layer, which].astype(F32)
    value = total[...].astype(BF16)
    for at in range(out.shape[0]):
        out[at] = value


def unpack(packed, first, second):
    rows = packed.shape[1] // 2
    size = 2 * STRIP
    half = FLAT // 2

    def strip(step, carry):
        for which, grad in enumerate((first, second)):

            def source(begin, which=which):
                begin = begin + step * size
                at = pl.multiple_of(which * rows + lax.rem(begin, rows), 16)
                return packed[lax.div(begin, rows), pl.ds(at, size), :].astype(F32)

            tail = source(2 * FLAT)
            for side in range(2):
                to = pl.ds(pl.multiple_of(step * size + side * half, 16), size)
                grad[to, 0:LANES] = source(side * half)
                grad[to, LANES : 2 * LANES] = source(FLAT + side * half)
                grad[to, 2 * LANES : C] = tail[:, side * TAIL : (side + 1) * TAIL]
        return carry

    lax.fori_loop(0, half // size, strip, 0)


def shape(dims, dtype):
    return jax.ShapeDtypeStruct(dims, dtype)


NORMED = ((2, CELLS, C), F32)
SCALE = ((2, 8, C), F32)
ACTS = ((2, CELLS, C), BF16)
ONE = ((CELLS, C), BF16)
PADDED = pltpu.VMEM((CELLS + 2 * SIDE, TAPS), BF16)
PADDED_COT = pltpu.VMEM((CELLS + 2 * SIDE, C), BF16)
TURNED = pltpu.VMEM((TAPS, CELLS), BF16)
OWN = ((PACKED, LANES), F32)
OTHER = ((PACKED, LANES), BF16)
WEIGHTS = pltpu.VMEM((2, 9, C, C), BF16)
TIMES = pltpu.VMEM((2, 2, C, C), BF16)
SEMS = pltpu.SemaphoreType.DMA((3, 2))


def call(body, spaces, outs, scratch, flops, name, vmem=VMEM_LIMIT):
    def run(*args):
        kinds = {"s": pltpu.SMEM, "h": pltpu.HBM, "v": pltpu.VMEM}
        moved = sum(a.size * a.dtype.itemsize for a in args) + sum(
            math.prod(d) * jnp.dtype(t).itemsize for d, t in outs
        )
        return pl.pallas_call(
            body,
            out_shape=tuple(shape(d, t) for d, t in outs),
            in_specs=[pl.BlockSpec(memory_space=kinds[space]) for space in spaces],
            out_specs=tuple(pl.BlockSpec(memory_space=pltpu.VMEM) for _ in outs),
            scratch_shapes=list(scratch),
            compiler_params=pltpu.CompilerParams(vmem_limit_bytes=vmem),
            cost_estimate=pl.CostEstimate(flops=flops, bytes_accessed=moved, transcendentals=0),
            name=name,
        )(*args)

    return run


CONV = 2 * CELLS * 9 * C * C


def time_embed(timesteps):
    half_width = C // 2
    frequencies = jnp.exp(
        -math.log(10000.0) * jnp.arange(half_width, dtype=F32) / half_width
    )
    angles = timesteps.astype(F32)[:, None] * frequencies[None, :]
    return jnp.concatenate([jnp.cos(angles), jnp.sin(angles)], axis=1).astype(BF16)


DP = ("z", "far", "y")


def to_other_core(array):
    return lax.ppermute(array, "core", [(0, 1), (1, 0)])


BLOCK = ("z_low", "far", "y")
LAYERS = "z_high"
DP = (LAYERS, *BLOCK)


def exchange(parts, axes):
    return lax.all_to_all(parts, axes, split_axis=0, concat_axis=0, tiled=True)


def core_sum(own, other):
    (pair,) = call(core_add, "vv", [((PACKED, LANES), BF16)], [], PACKED * LANES, "core_add")(
        own, to_other_core(other)
    )
    return pair


def spread_parts(pair):
    count = lax.axis_size(BLOCK)
    return exchange(pair.reshape(count, PACKED // count, LANES), BLOCK)


def gradients(first, second):
    count, rows, _ = first.shape
    layers = lax.axis_size(LAYERS)
    cut = ((layers, 2, rows // layers, LANES), BF16)
    (sums,) = call(block_sums, "vv", [cut], [], 2 * PACKED * LANES, "block_sums")(first, second)
    (sums,) = call(layer_sums, "v", [cut], [], 2 * rows * LANES, "layer_sums")(
        exchange(sums, LAYERS)
    )
    (copies,) = call(
        assemble, "v", [((count, 2 * rows, LANES), BF16)], [pltpu.VMEM((2 * rows, LANES), F32)],
        2 * PACKED * LANES, "assemble",
    )(exchange(sums, LAYERS))
    grads = call(unpack, "v", [((FLAT, C), F32)] * 2, [], 2 * PACKED * LANES, "unpack")(
        exchange(copies, BLOCK)
    )
    return tuple(grad.reshape(1, 3, 3, C, C) for grad in grads)


def local(latents, cotangent, bucket, timesteps, w_enc, w_dec, w_time):
    where = jnp.stack([lax.axis_index(axis) for axis in ("near", "core")])
    where = where.astype(jnp.int32)
    micro_count = latents.shape[0]
    loss_scale = float(micro_count * lax.axis_size(DP) * CELLS) ** (-0.5)

    enc = w_enc.reshape(9, C, C)
    dec = w_dec.reshape(9, C, C)
    times = w_time.reshape(2, C, C)
    times = (times, to_other_core(times))
    enc = (enc, to_other_core(enc))
    dec, enc, times = lax.optimization_barrier((dec, enc, times))
    dec = (dec, to_other_core(dec))
    latents = latents.reshape(micro_count, CELLS, C)
    cotangent = cotangent.reshape(micro_count, CELLS, C)
    emb = jnp.pad(time_embed(timesteps), ((0, 16 - micro_count), (0, 0)))
    matrix = group_matrix()

    def up(value):
        return lax.ppermute(value, "near", [(0, 1)])

    def down(value):
        return lax.ppermute(value, "near", [(1, 0)])

    one = call(
        phase_one, "ss" + "h" * 5 + "vv", [NORMED, SCALE, ACTS, ACTS, ONE],
        [pltpu.VMEM(*ONE), TIMES, WEIGHTS, PADDED, SEMS], 2 * CONV, "one", ALL_VMEM,
    )
    a_normed, a_scale, a_hidden, a_kept, sent = one(
        where, bucket, latents, *times, *enc, emb, matrix
    )
    two = call(
        phase_two, "ssv" + "h" * 6 + "vv", [NORMED, SCALE, ACTS, NORMED, SCALE, ACTS, ONE],
        [pltpu.VMEM(*ACTS), TIMES, WEIGHTS, WEIGHTS, PADDED, SEMS], 4 * CONV, "two",
    )
    be_normed, be_scale, be_hidden, bd_normed, bd_scale, bd_hidden, sent = two(
        where, bucket, up(sent), *times, *enc, *dec, emb, matrix
    )
    three = call(
        functools.partial(phase_three, loss_scale), "ssv" + "h" * 5 + "vvv",
        [ACTS, ACTS, ACTS, ONE],
        [
            pltpu.VMEM(*NORMED), pltpu.VMEM(*SCALE), pltpu.VMEM(*ONE), TIMES, WEIGHTS, PADDED,
            PADDED_COT, SEMS,
        ],
        3 * CONV, "three",
    )
    ad_hidden, ad_cots, a_skips, sent = three(
        where, bucket, down(sent), cotangent, *times, *dec, a_kept, emb, matrix
    )
    four = call(
        phase_four, "ssv" + "h" * 6 + "v" * 6, [ACTS, ACTS, ONE],
        [pltpu.VMEM(*ACTS), TIMES, WEIGHTS, WEIGHTS, PADDED_COT, SEMS], 4 * CONV, "four",
    )
    bd_cots, be_cots, sent = four(
        where, bucket, up(sent), *times, *enc, *dec, emb, matrix,
        bd_normed, bd_scale, be_normed, be_scale,
    )
    received = down(sent)
    work = [PADDED_COT, TURNED, pltpu.VMEM((2, PACKED, LANES), F32), pltpu.VMEM(*ACTS), pltpu.VMEM(*ACTS)]
    weights = call(weight_phase, "svvvv", [OWN, OTHER], work, 2 * CONV, "weights")
    dec_pair = core_sum(*weights(where, ad_hidden, ad_cots, bd_hidden, bd_cots))
    received, dec_pair = lax.optimization_barrier((received, dec_pair))
    dec_parts = spread_parts(dec_pair)
    five = call(
        phase_five, "ssv" + "h" * 4 + "v" * 8, [OWN, OTHER], [*work, TIMES, WEIGHTS, SEMS],
        3 * CONV, "five",
    )
    enc_grads = five(
        where, bucket, received, *times, *enc, a_skips, emb, matrix, a_normed, a_scale, a_hidden,
        be_hidden, be_cots,
    )

    enc_parts = spread_parts(core_sum(*enc_grads))
    return gradients(enc_parts, dec_parts)


def solution(mesh):
    segments, dp = mesh.shape["segment"], mesh.shape["dp"]
    near, far, rows = segments // 2, 2, 4
    split = Mesh(
        mesh.devices.reshape(near, 2, dp // (2 * far * rows), 2, far, rows),
        ("near", "core", *DP),
    )
    section, micro = ("near", "core"), DP
    placed = (
        P(micro, None, None, None),
        P(micro, None, None, None),
        P(micro, None),
        P(micro),
        P(section, None, None, None, None),
        P(section, None, None, None, None),
        P(section, None, None, None),
    )
    grads = P(section, None, None, None, None)
    return jax.shard_map(
        local, mesh=split, in_specs=placed, out_specs=(grads, grads), check_vma=False
    )
```

```python
import functools
import math

import jax
import jax.numpy as jnp
import numpy as np
from jax import lax
from jax.experimental import pallas as pl
from jax.experimental.pallas import tpu as pltpu
from jax.sharding import Mesh, PartitionSpec as P

G = 32
SIDE = 16
CELLS = SIDE * SIDE
C = 320
TAPS = 3 * C
F32 = jnp.float32
BF16 = jnp.bfloat16
VMEM_LIMIT = 30 * 1024 * 1024
ALL_VMEM = 60 * 1024 * 1024
LANES = 128
FLAT = 9 * C
TAIL = C - 2 * LANES
PACKED_USED = 2 * FLAT + FLAT // 2
PACKED = 64 * 120
STRIP = 240

NT = (((1,), (1,)), ((), ()))


def group_matrix():
    index = np.arange(C) // (C // G)
    return jnp.asarray((index[:, None] == index[None, :]).astype(np.float32), BF16)


def group_sums(columns, matrix):
    row = lax.broadcasted_iota(jnp.int32, (16, C), 0)
    stacked = jnp.zeros((16, C), F32)
    for at, column in enumerate(columns):
        high = column.astype(BF16).astype(F32)
        rest = column - high
        middle = rest.astype(BF16).astype(F32)
        low = (rest - middle).astype(BF16).astype(F32)
        for part, value in enumerate((high, middle, low)):
            stacked = jnp.where(row == 3 * at + part, value, stacked)
    sums = jnp.dot(stacked.astype(BF16), matrix, preferred_element_type=F32)
    return [
        sums[3 * at : 3 * at + 1] + sums[3 * at + 1 : 3 * at + 2] + sums[3 * at + 2 : 3 * at + 3]
        for at in range(len(columns))
    ]


def col_sum(values):
    return jnp.sum(values, axis=0, keepdims=True)


def column_index():
    return lax.broadcasted_iota(jnp.int32, (CELLS, C), 0) % SIDE


def shift_right(values, column):
    return jnp.where(column == 0, 0.0, pltpu.roll(values, 1, axis=0))


def shift_left(values, column):
    return jnp.where(column == SIDE - 1, 0.0, pltpu.roll(values, CELLS - 1, axis=0))


def clear_edges(padded):
    width = padded.shape[1]
    padded[0:SIDE, :] = jnp.zeros((SIDE, width), BF16)
    padded[SIDE + CELLS :, :] = jnp.zeros((SIDE, width), BF16)


def store_windows(padded, hidden, column):
    padded[SIDE : SIDE + CELLS, 0:C] = shift_right(hidden, column).astype(BF16)
    padded[SIDE : SIDE + CELLS, C : 2 * C] = hidden.astype(BF16)
    padded[SIDE : SIDE + CELLS, 2 * C : 3 * C] = shift_left(hidden, column).astype(BF16)


def norm_hidden(values, mask, temb, entries, matrix):
    mean = group_sums([col_sum(values * mask)], matrix)[0] / entries
    centered = values - mean
    variance = group_sums([col_sum(centered * centered * mask)], matrix)[0] / entries
    scale = lax.rsqrt(variance + 1e-05)
    normed = centered * scale
    shifted = normed + temb
    hidden = shifted / (1.0 + jnp.exp(-shifted)) * mask
    return normed, scale, hidden


def taps(kernel, row):
    return kernel[3 * row : 3 * row + 3].reshape(TAPS, C)


def conv(padded, kernel):
    total = None
    for row in range(3):
        part = jnp.dot(
            padded[row * SIDE : row * SIDE + CELLS, :], taps(kernel, row), preferred_element_type=F32
        )
        total = part if total is None else total + part
    return total


def conv_back(cot_padded, kernel, column):
    total = None
    for row in range(3):
        part = lax.dot_general(
            cot_padded[(2 - row) * SIDE : (2 - row) * SIDE + CELLS, :],
            taps(kernel, row),
            NT,
            preferred_element_type=F32,
        )
        total = part if total is None else total + part
    left, middle, right = total[:, 0:C], total[:, C : 2 * C], total[:, 2 * C : 3 * C]
    return shift_left(left, column) + middle + shift_right(right, column)


def norm_back(hidden_cot, normed, scale, temb, mask, entries, matrix):
    shifted = normed + temb
    gate = 1.0 / (1.0 + jnp.exp(-shifted))
    flow = hidden_cot * mask * (gate * (1.0 + shifted * (1.0 - gate)))
    plain, cross = group_sums([col_sum(flow), col_sum(flow * normed)], matrix)
    return scale * (flow - mask * (plain / entries + normed * (cross / entries)))


def mask_of(bucket_ref, core):
    row = lax.broadcasted_iota(jnp.int32, (CELLS, C), 0)
    inside = (row // SIDE < bucket_ref[core, 0]) & (row % SIDE < bucket_ref[core, 1])
    return inside.astype(F32)


def entries_of(bucket_ref, core):
    return (bucket_ref[core, 0] * bucket_ref[core, 1] * (C // G)).astype(F32)


class Setup:
    def __init__(self, core, bucket, embedding, time_ref, matrix):
        self.core = core
        self.column = column_index()
        self.mask = mask_of(bucket, core)
        self.entries = entries_of(bucket, core)
        self.matrix = matrix[...]
        self.embedding = embedding
        self.time_ref = time_ref

    def temb(self, k, side):
        rows = jnp.dot(self.embedding[...], self.time_ref[k, side], preferred_element_type=F32)
        at = lax.broadcasted_iota(jnp.int32, rows.shape, 0)
        return col_sum(jnp.where(at == self.core, rows, 0.0))


def fetch_pair(core, own, other, target, sems):
    copies = [
        pltpu.make_async_copy(own, target.at[core], sems.at[0]),
        pltpu.make_async_copy(other, target.at[1 - core], sems.at[1]),
    ]
    for copy in copies:
        copy.start()
    return copies


def wait_all(*groups):
    for copies in groups:
        for copy in copies:
            copy.wait()


def forward_block(setup, values, k, side, kernel, padded, out):
    normed_ref, scale_ref, hidden_ref = out
    normed, scale, hidden = norm_hidden(
        values, setup.mask, setup.temb(k, side), setup.entries, setup.matrix
    )
    normed_ref[k] = normed
    scale_ref[k] = jnp.broadcast_to(scale, (8, C))
    hidden_ref[k] = hidden.astype(BF16)
    if kernel is None:
        return None
    store_windows(padded, hidden, setup.column)
    return ((values + conv(padded, kernel)) * setup.mask).astype(BF16)


def encoder_pair(setup, value, w_enc, padded, out, inputs_ref):
    def block(k, value):
        inputs_ref[k] = value
        return forward_block(setup, value.astype(F32), k, 0, w_enc.at[k], padded, out)

    return lax.fori_loop(0, 2, block, value)


def decoder_pair(setup, value, w_dec, padded, out, inputs_ref, last):
    def block(step, value, conv_too=True):
        k = 1 - step
        summed = value.astype(F32) + inputs_ref[k].astype(F32)
        kernel = w_dec.at[k] if conv_too else None
        return forward_block(setup, summed, k, 1, kernel, padded, out)

    if last:
        return lax.fori_loop(0, 2, block, value)
    return block(1, block(0, value), conv_too=False)


def backward_pair(setup, value, side, upward, kernels, padded_cot, kept, cot_ref, skips, skip_in, last):
    normed_ref, scale_ref = kept

    def masked(k, value):
        residual = value.astype(F32) * setup.mask
        conv_cot = residual.astype(BF16)
        cot_ref[k] = conv_cot
        return residual, conv_cot

    def block(step, value):
        k = step if upward else 1 - step
        residual, conv_cot = masked(k, value)
        padded_cot[SIDE : SIDE + CELLS, :] = conv_cot
        hidden_cot = conv_back(padded_cot, kernels.at[k], setup.column)
        total = residual + norm_back(
            hidden_cot, normed_ref[k], scale_ref[k, 0:1], setup.temb(k, side), setup.mask,
            setup.entries, setup.matrix,
        )
        if skip_in is not None:
            total = total + skip_in[k].astype(F32)
        value = total.astype(BF16)
        if skips is not None:
            skips[k] = value
        return value

    if last:
        return lax.fori_loop(0, 2, block, value)
    masked(1 if upward else 0, block(0, value))
    return None


def phase_one(
    where, bucket, latents, time_own, time_other, enc_own, enc_other, emb, matrix,
    normed, scale, hidden, kept, sent, x, time_ref, w_enc, padded, sems,
):
    core = where[1]
    enc_copies = fetch_pair(core, enc_own, enc_other, w_enc, sems.at[0])
    time_copies = fetch_pair(core, time_own, time_other, time_ref, sems.at[1])
    x_copy = pltpu.make_async_copy(latents.at[core], x, sems.at[2, 0])
    x_copy.start()
    clear_edges(padded)
    wait_all([x_copy], time_copies, enc_copies)
    setup = Setup(core, bucket, emb, time_ref, matrix)
    sent[...] = encoder_pair(setup, x[...], w_enc, padded, (normed, scale, hidden), kept)


def phase_two(
    where, bucket, x, time_own, time_other, enc_own, enc_other, dec_own, dec_other, emb, matrix,
    e_normed, e_scale, e_hidden, d_normed, d_scale, d_hidden, sent,
    kept, time_ref, w_enc, w_dec, padded, sems,
):
    core = where[1]
    time_copies = fetch_pair(core, time_own, time_other, time_ref, sems.at[1])
    enc_copies = fetch_pair(core, enc_own, enc_other, w_enc, sems.at[0])
    dec_copies = fetch_pair(core, dec_own, dec_other, w_dec, sems.at[2])
    clear_edges(padded)
    wait_all(time_copies, enc_copies)
    setup = Setup(core, bucket, emb, time_ref, matrix)
    upper = encoder_pair(setup, x[...], w_enc, padded, (e_normed, e_scale, e_hidden), kept)
    wait_all(dec_copies)
    sent[...] = decoder_pair(
        setup, upper, w_dec, padded, (d_normed, d_scale, d_hidden), kept, True
    )


def phase_three(
    scaling, where, bucket, x, cotangent, time_own, time_other, dec_own, dec_other, kept, emb,
    matrix, d_hidden, cots, skips, sent,
    d_normed, d_scale, start, time_ref, w_dec, padded, padded_cot, sems,
):
    core = where[1]
    time_copies = fetch_pair(core, time_own, time_other, time_ref, sems.at[1])
    dec_copies = fetch_pair(core, dec_own, dec_other, w_dec, sems.at[0])
    start_copy = pltpu.make_async_copy(cotangent.at[core], start, sems.at[2, 0])
    start_copy.start()
    clear_edges(padded)
    clear_edges(padded_cot)
    wait_all(time_copies, dec_copies, [start_copy])
    setup = Setup(core, bucket, emb, time_ref, matrix)
    decoder_pair(setup, x[...], w_dec, padded, (d_normed, d_scale, d_hidden), kept, False)
    cot = (start[...].astype(F32) * scaling).astype(BF16)
    sent[...] = backward_pair(
        setup, cot, 1, True, w_dec, padded_cot, (d_normed, d_scale), cots, skips, None, True
    )


def phase_four(
    where, bucket, x, time_own, time_other, enc_own, enc_other, dec_own, dec_other, emb, matrix,
    d_normed, d_scale, e_normed, e_scale, d_cots, e_cots, sent,
    skips, time_ref, w_enc, w_dec, padded_cot, sems,
):
    core = where[1]
    time_copies = fetch_pair(core, time_own, time_other, time_ref, sems.at[1])
    dec_copies = fetch_pair(core, dec_own, dec_other, w_dec, sems.at[0])
    enc_copies = fetch_pair(core, enc_own, enc_other, w_enc, sems.at[2])
    clear_edges(padded_cot)
    wait_all(time_copies, dec_copies)
    setup = Setup(core, bucket, emb, time_ref, matrix)
    cot = backward_pair(
        setup, x[...], 1, True, w_dec, padded_cot, (d_normed, d_scale), d_cots, skips, None, True
    )
    wait_all(enc_copies)
    sent[...] = backward_pair(
        setup, cot, 0, False, w_enc, padded_cot, (e_normed, e_scale), e_cots, None, skips, True
    )


def store_packed(target, slot, row, values):
    first = row * TAPS
    target[slot, first : first + TAPS, :] = values[:, 0:LANES]
    target[slot, FLAT + first : FLAT + first + TAPS, :] = values[:, LANES : 2 * LANES]
    half = FLAT // 2
    pieces = ((0, TAPS // 2), (TAPS // 2, TAPS)) if row == 1 else ((0, TAPS),)
    for begin, end in pieces:
        side = 0 if first + end <= half else 1
        at = 2 * FLAT + first + begin - side * half
        target[slot, at : at + end - begin, side * TAIL : (side + 1) * TAIL] = values[
            begin:end, 2 * LANES : C
        ]


def store_gradients(core, hidden, cots, own, other, padded_cot, turned, pair):
    column = column_index()
    pair[:, PACKED_USED:, :] = jnp.zeros((2, PACKED - PACKED_USED, LANES), F32)

    def section(k, carry):
        values = hidden[k].astype(F32)
        padded_cot[SIDE : SIDE + CELLS, :] = cots[k]
        turned[0:C, :] = shift_right(values, column).T.astype(BF16)
        turned[C : 2 * C, :] = values.T.astype(BF16)
        turned[2 * C : 3 * C, :] = shift_left(values, column).T.astype(BF16)
        for row in range(3):
            part = jnp.dot(
                turned[...],
                padded_cot[(2 - row) * SIDE : (2 - row) * SIDE + CELLS, :],
                preferred_element_type=F32,
            )
            store_packed(pair, jnp.where(core == k, 0, 1), row, part)
        return carry

    lax.fori_loop(0, 2, section, 0)

    def copy(step, carry):
        begin = pl.multiple_of(step * STRIP, STRIP)
        own[pl.ds(begin, STRIP), :] = pair[0, pl.ds(begin, STRIP), :]
        other[pl.ds(begin, STRIP), :] = pair[1, pl.ds(begin, STRIP), :].astype(BF16)
        return carry

    lax.fori_loop(0, PACKED // STRIP, copy, 0)


def weight_phase(
    where, a_hidden, a_cots, b_hidden, b_cots, own, other, padded_cot, turned, pair, hidden, cots
):
    clear_edges(padded_cot)

    @pl.when(where[0] == 0)
    def _():
        hidden[...] = a_hidden[...]
        cots[...] = a_cots[...]

    @pl.when(where[0] != 0)
    def _():
        hidden[...] = b_hidden[...]
        cots[...] = b_cots[...]

    store_gradients(where[1], hidden, cots, own, other, padded_cot, turned, pair)


def phase_five(
    where, bucket, x, time_own, time_other, enc_own, enc_other, skips, emb, matrix,
    e_normed, e_scale, a_hidden, b_hidden, b_cots,
    own, other, padded_cot, turned, pair, hidden, cots, time_ref, w_enc, sems,
):
    clear_edges(padded_cot)
    core = where[1]
    time_copies = fetch_pair(core, time_own, time_other, time_ref, sems.at[1])
    enc_copies = fetch_pair(core, enc_own, enc_other, w_enc, sems.at[0])
    wait_all(time_copies, enc_copies)

    @pl.when(where[0] == 0)
    def _():
        hidden[...] = a_hidden[...]
        setup = Setup(core, bucket, emb, time_ref, matrix)
        backward_pair(
            setup, x[...], 0, False, w_enc, padded_cot, (e_normed, e_scale), cots, None, skips,
            False,
        )

    @pl.when(where[0] != 0)
    def _():
        hidden[...] = b_hidden[...]
        cots[...] = b_cots[...]

    store_gradients(core, hidden, cots, own, other, padded_cot, turned, pair)


def core_split(where, own, other, kept, *chunks):
    count = len(chunks) + 1
    rows = own.shape[0] // count
    for ahead in range(count):
        begin = pl.multiple_of(lax.rem(where[2] + ahead, count) * rows, 16)
        part = own[pl.ds(begin, rows), :] + other[pl.ds(begin, rows), :].astype(F32)
        if ahead == 0:
            kept[...] = part
        else:
            chunks[ahead - 1][...] = part.astype(BF16)


def row_sum(kept, *rest):
    *received, out = rest
    value = kept[...]
    for part in received:
        value = value + part[...].astype(F32)
    out[...] = value.astype(BF16)


def plane_sum(parts, out):
    value = parts[0].astype(F32)
    for at in range(1, parts.shape[0]):
        value = value + parts[at].astype(F32)
    value = value.astype(BF16)
    for at in range(out.shape[0]):
        out[at] = value


def unpack(where, *rest):
    *chunks, grad, packed = rest
    count, rows, _ = packed.shape
    size = 2 * STRIP
    half = FLAT // 2
    for behind, chunk in enumerate(chunks):
        packed[lax.rem(where[2] + count - behind, count)] = chunk[...]

    def strip(step, carry):
        def source(begin):
            begin = begin + step * size
            at = pl.multiple_of(lax.rem(begin, rows), 16)
            return packed[lax.div(begin, rows), pl.ds(at, size), :].astype(F32)

        tail = source(2 * FLAT)
        for side in range(2):
            to = pl.ds(pl.multiple_of(step * size + side * half, 16), size)
            grad[to, 0:LANES] = source(side * half)
            grad[to, LANES : 2 * LANES] = source(FLAT + side * half)
            grad[to, 2 * LANES : C] = tail[:, side * TAIL : (side + 1) * TAIL]
        return carry

    lax.fori_loop(0, half // size, strip, 0)


def shape(dims, dtype):
    return jax.ShapeDtypeStruct(dims, dtype)


NORMED = ((2, CELLS, C), F32)
SCALE = ((2, 8, C), F32)
ACTS = ((2, CELLS, C), BF16)
ONE = ((CELLS, C), BF16)
PADDED = pltpu.VMEM((CELLS + 2 * SIDE, TAPS), BF16)
PADDED_COT = pltpu.VMEM((CELLS + 2 * SIDE, C), BF16)
TURNED = pltpu.VMEM((TAPS, CELLS), BF16)
OWN = ((PACKED, LANES), F32)
OTHER = ((PACKED, LANES), BF16)
WEIGHTS = pltpu.VMEM((2, 9, C, C), BF16)
TIMES = pltpu.VMEM((2, 2, C, C), BF16)
SEMS = pltpu.SemaphoreType.DMA((3, 2))


def call(body, spaces, outs, scratch, flops, name, vmem=VMEM_LIMIT):
    def run(*args):
        kinds = {"s": pltpu.SMEM, "h": pltpu.HBM, "v": pltpu.VMEM}
        moved = sum(a.size * a.dtype.itemsize for a in args) + sum(
            math.prod(d) * jnp.dtype(t).itemsize for d, t in outs
        )
        return pl.pallas_call(
            body,
            out_shape=tuple(shape(d, t) for d, t in outs),
            in_specs=[pl.BlockSpec(memory_space=kinds[space]) for space in spaces],
            out_specs=tuple(pl.BlockSpec(memory_space=pltpu.VMEM) for _ in outs),
            scratch_shapes=list(scratch),
            compiler_params=pltpu.CompilerParams(vmem_limit_bytes=vmem),
            cost_estimate=pl.CostEstimate(flops=flops, bytes_accessed=moved, transcendentals=0),
            name=name,
        )(*args)

    return run


CONV = 2 * CELLS * 9 * C * C


def time_embed(timesteps):
    half_width = C // 2
    frequencies = jnp.exp(
        -math.log(10000.0) * jnp.arange(half_width, dtype=F32) / half_width
    )
    angles = timesteps.astype(F32)[:, None] * frequencies[None, :]
    return jnp.concatenate([jnp.cos(angles), jnp.sin(angles)], axis=1).astype(BF16)


DP = ("z", "far", "y")
PLANES = ("z", "far")


def to_other_core(array):
    return lax.ppermute(array, "core", [(0, 1), (1, 0)])


def ahead(value, steps):
    count = lax.axis_size("y")
    return lax.ppermute(value, "y", [(at, (at + steps) % count) for at in range(count)])


def exchange(rows):
    parts = rows.reshape(lax.axis_size(PLANES), -1, LANES)
    return lax.all_to_all(parts, PLANES, split_axis=0, concat_axis=0, tiled=True)


def split_sum(where, own, other):
    count = lax.axis_size("y")
    chunk = (PACKED // count, LANES)
    return call(
        core_split, "svv", [(chunk, F32)] + [(chunk, BF16)] * (count - 1), [], PACKED * LANES,
        "core_split",
    )(where, own, to_other_core(other))


def sum_rows(where, own, other):
    count = lax.axis_size("y")
    kept, *chunks = split_sum(where, own, other)
    received = [ahead(part, step + 1) for step, part in enumerate(chunks)]
    (rows,) = call(
        row_sum, "v" * count, [((PACKED // count, LANES), BF16)], [], PACKED * LANES, "row_sum"
    )(kept, *received)
    return rows


def gradient(where, rows):
    count, planes = lax.axis_size("y"), lax.axis_size(PLANES)
    chunk = rows.shape
    parts = ((planes, chunk[0] // planes, LANES), BF16)
    (copies,) = call(plane_sum, "v", [parts], [], PACKED * LANES, "plane_sum")(exchange(rows))
    mine = exchange(copies).reshape(chunk)
    received = [ahead(mine, step) for step in range(1, count)]
    (grad,) = call(
        unpack, "s" + "v" * count, [((FLAT, C), F32)], [pltpu.VMEM((count, *chunk), BF16)],
        PACKED * LANES, "unpack",
    )(where, mine, *received)
    return grad.reshape(1, 3, 3, C, C)


def local(latents, cotangent, bucket, timesteps, w_enc, w_dec, w_time):
    where = jnp.stack([lax.axis_index(axis) for axis in ("near", "core", "y")])
    where = where.astype(jnp.int32)
    micro_count = latents.shape[0]
    loss_scale = float(micro_count * lax.axis_size(DP) * CELLS) ** (-0.5)

    enc = w_enc.reshape(9, C, C)
    dec = w_dec.reshape(9, C, C)
    times = w_time.reshape(2, C, C)
    times = (times, to_other_core(times))
    enc = (enc, to_other_core(enc))
    dec, enc, times = lax.optimization_barrier((dec, enc, times))
    dec = (dec, to_other_core(dec))
    latents = latents.reshape(micro_count, CELLS, C)
    cotangent = cotangent.reshape(micro_count, CELLS, C)
    emb = jnp.pad(time_embed(timesteps), ((0, 16 - micro_count), (0, 0)))
    matrix = group_matrix()

    def up(value):
        return lax.ppermute(value, "near", [(0, 1)])

    def down(value):
        return lax.ppermute(value, "near", [(1, 0)])

    one = call(
        phase_one, "ss" + "h" * 5 + "vv", [NORMED, SCALE, ACTS, ACTS, ONE],
        [pltpu.VMEM(*ONE), TIMES, WEIGHTS, PADDED, SEMS], 2 * CONV, "one", ALL_VMEM,
    )
    a_normed, a_scale, a_hidden, a_kept, sent = one(
        where, bucket, latents, *times, *enc, emb, matrix
    )
    two = call(
        phase_two, "ssv" + "h" * 6 + "vv", [NORMED, SCALE, ACTS, NORMED, SCALE, ACTS, ONE],
        [pltpu.VMEM(*ACTS), TIMES, WEIGHTS, WEIGHTS, PADDED, SEMS], 4 * CONV, "two",
    )
    be_normed, be_scale, be_hidden, bd_normed, bd_scale, bd_hidden, sent = two(
        where, bucket, up(sent), *times, *enc, *dec, emb, matrix
    )
    three = call(
        functools.partial(phase_three, loss_scale), "ssv" + "h" * 5 + "vvv",
        [ACTS, ACTS, ACTS, ONE],
        [
            pltpu.VMEM(*NORMED), pltpu.VMEM(*SCALE), pltpu.VMEM(*ONE), TIMES, WEIGHTS, PADDED,
            PADDED_COT, SEMS,
        ],
        3 * CONV, "three",
    )
    ad_hidden, ad_cots, a_skips, sent = three(
        where, bucket, down(sent), cotangent, *times, *dec, a_kept, emb, matrix
    )
    four = call(
        phase_four, "ssv" + "h" * 6 + "v" * 6, [ACTS, ACTS, ONE],
        [pltpu.VMEM(*ACTS), TIMES, WEIGHTS, WEIGHTS, PADDED_COT, SEMS], 4 * CONV, "four",
    )
    bd_cots, be_cots, sent = four(
        where, bucket, up(sent), *times, *enc, *dec, emb, matrix,
        bd_normed, bd_scale, be_normed, be_scale,
    )
    received = down(sent)
    work = [PADDED_COT, TURNED, pltpu.VMEM((2, PACKED, LANES), F32), pltpu.VMEM(*ACTS), pltpu.VMEM(*ACTS)]
    weights = call(weight_phase, "svvvv", [OWN, OTHER], work, 2 * CONV, "weights")
    dec_rows = sum_rows(where, *weights(where, ad_hidden, ad_cots, bd_hidden, bd_cots))
    received, dec_rows = lax.optimization_barrier((received, dec_rows))
    five = call(
        phase_five, "ssv" + "h" * 4 + "v" * 8, [OWN, OTHER], [*work, TIMES, WEIGHTS, SEMS],
        3 * CONV, "five",
    )
    enc_grads = five(
        where, bucket, received, *times, *enc, a_skips, emb, matrix, a_normed, a_scale, a_hidden,
        be_hidden, be_cots,
    )

    enc_rows = sum_rows(where, *enc_grads)
    return gradient(where, enc_rows), gradient(where, dec_rows)


def solution(mesh):
    segments, dp = mesh.shape["segment"], mesh.shape["dp"]
    near, far, rows = segments // 2, 2, 4
    split = Mesh(
        mesh.devices.reshape(near, 2, dp // (far * rows), far, rows),
        ("near", "core", *DP),
    )
    section, micro = ("near", "core"), DP
    placed = (
        P(micro, None, None, None),
        P(micro, None, None, None),
        P(micro, None),
        P(micro),
        P(section, None, None, None, None),
        P(section, None, None, None, None),
        P(section, None, None, None),
    )
    grads = P(section, None, None, None, None)
    return jax.shard_map(
        local, mesh=split, in_specs=placed, out_specs=(grads, grads), check_vma=False
    )
```

```python
import functools
import math

import jax
import jax.numpy as jnp
import numpy as np
from jax import lax
from jax.experimental import pallas as pl
from jax.experimental.pallas import tpu as pltpu
from jax.sharding import Mesh, PartitionSpec as P

G = 32
SIDE = 16
CELLS = SIDE * SIDE
C = 320
TAPS = 3 * C
F32 = jnp.float32
BF16 = jnp.bfloat16
VMEM_LIMIT = 30 * 1024 * 1024
ALL_VMEM = 60 * 1024 * 1024
LANES = 128
FLAT = 9 * C
TAIL = C - 2 * LANES
PACKED_USED = 2 * FLAT + FLAT // 2
PACKED = 64 * 120
STRIP = 240

NT = (((1,), (1,)), ((), ()))


def group_matrix():
    index = np.arange(C) // (C // G)
    return jnp.asarray((index[:, None] == index[None, :]).astype(np.float32), BF16)


def group_sums(columns, matrix):
    row = lax.broadcasted_iota(jnp.int32, (16, C), 0)
    stacked = jnp.zeros((16, C), F32)
    for at, column in enumerate(columns):
        high = column.astype(BF16).astype(F32)
        rest = column - high
        middle = rest.astype(BF16).astype(F32)
        low = (rest - middle).astype(BF16).astype(F32)
        for part, value in enumerate((high, middle, low)):
            stacked = jnp.where(row == 3 * at + part, value, stacked)
    sums = jnp.dot(stacked.astype(BF16), matrix, preferred_element_type=F32)
    return [
        sums[3 * at : 3 * at + 1] + sums[3 * at + 1 : 3 * at + 2] + sums[3 * at + 2 : 3 * at + 3]
        for at in range(len(columns))
    ]


def col_sum(values):
    return jnp.sum(values, axis=0, keepdims=True)


def column_index():
    return lax.broadcasted_iota(jnp.int32, (CELLS, C), 0) % SIDE


def shift_right(values, column):
    return jnp.where(column == 0, 0.0, pltpu.roll(values, 1, axis=0))


def shift_left(values, column):
    return jnp.where(column == SIDE - 1, 0.0, pltpu.roll(values, CELLS - 1, axis=0))


def clear_edges(padded):
    width = padded.shape[1]
    padded[0:SIDE, :] = jnp.zeros((SIDE, width), BF16)
    padded[SIDE + CELLS :, :] = jnp.zeros((SIDE, width), BF16)


def store_windows(padded, hidden, column):
    padded[SIDE : SIDE + CELLS, 0:C] = shift_right(hidden, column).astype(BF16)
    padded[SIDE : SIDE + CELLS, C : 2 * C] = hidden.astype(BF16)
    padded[SIDE : SIDE + CELLS, 2 * C : 3 * C] = shift_left(hidden, column).astype(BF16)


def norm_hidden(values, mask, temb, entries, matrix):
    mean = group_sums([col_sum(values * mask)], matrix)[0] / entries
    centered = values - mean
    variance = group_sums([col_sum(centered * centered * mask)], matrix)[0] / entries
    scale = lax.rsqrt(variance + 1e-05)
    normed = centered * scale
    shifted = normed + temb
    hidden = shifted / (1.0 + jnp.exp(-shifted)) * mask
    return normed, scale, hidden


def taps(kernel, row):
    return kernel[3 * row : 3 * row + 3].reshape(TAPS, C)


def conv(padded, kernel):
    total = None
    for row in range(3):
        part = jnp.dot(
            padded[row * SIDE : row * SIDE + CELLS, :], taps(kernel, row), preferred_element_type=F32
        )
        total = part if total is None else total + part
    return total


def conv_back(cot_padded, kernel, column):
    total = None
    for row in range(3):
        part = lax.dot_general(
            cot_padded[(2 - row) * SIDE : (2 - row) * SIDE + CELLS, :],
            taps(kernel, row),
            NT,
            preferred_element_type=F32,
        )
        total = part if total is None else total + part
    left, middle, right = total[:, 0:C], total[:, C : 2 * C], total[:, 2 * C : 3 * C]
    return shift_left(left, column) + middle + shift_right(right, column)


def norm_back(hidden_cot, normed, scale, temb, mask, entries, matrix):
    shifted = normed + temb
    gate = 1.0 / (1.0 + jnp.exp(-shifted))
    flow = hidden_cot * mask * (gate * (1.0 + shifted * (1.0 - gate)))
    plain, cross = group_sums([col_sum(flow), col_sum(flow * normed)], matrix)
    return scale * (flow - mask * (plain / entries + normed * (cross / entries)))


def mask_of(bucket_ref, core):
    row = lax.broadcasted_iota(jnp.int32, (CELLS, C), 0)
    inside = (row // SIDE < bucket_ref[core, 0]) & (row % SIDE < bucket_ref[core, 1])
    return inside.astype(F32)


def entries_of(bucket_ref, core):
    return (bucket_ref[core, 0] * bucket_ref[core, 1] * (C // G)).astype(F32)


class Setup:
    def __init__(self, core, bucket, embedding, time_ref, matrix):
        self.core = core
        self.column = column_index()
        self.mask = mask_of(bucket, core)
        self.entries = entries_of(bucket, core)
        self.matrix = matrix[...]
        self.embedding = embedding
        self.time_ref = time_ref

    def temb(self, k, side):
        rows = jnp.dot(self.embedding[...], self.time_ref[k, side], preferred_element_type=F32)
        at = lax.broadcasted_iota(jnp.int32, rows.shape, 0)
        return col_sum(jnp.where(at == self.core, rows, 0.0))


def fetch_pair(core, own, other, target, sems):
    copies = [
        pltpu.make_async_copy(own, target.at[core], sems.at[0]),
        pltpu.make_async_copy(other, target.at[1 - core], sems.at[1]),
    ]
    for copy in copies:
        copy.start()
    return copies


def wait_all(*groups):
    for copies in groups:
        for copy in copies:
            copy.wait()


def forward_block(setup, values, k, side, kernel, padded, out):
    normed_ref, scale_ref, hidden_ref = out
    normed, scale, hidden = norm_hidden(
        values, setup.mask, setup.temb(k, side), setup.entries, setup.matrix
    )
    normed_ref[k] = normed
    scale_ref[k] = jnp.broadcast_to(scale, (8, C))
    hidden_ref[k] = hidden.astype(BF16)
    if kernel is None:
        return None
    store_windows(padded, hidden, setup.column)
    return ((values + conv(padded, kernel)) * setup.mask).astype(BF16)


def encoder_pair(setup, value, w_enc, padded, out, inputs_ref):
    def block(k, value):
        inputs_ref[k] = value
        return forward_block(setup, value.astype(F32), k, 0, w_enc.at[k], padded, out)

    return lax.fori_loop(0, 2, block, value)


def decoder_pair(setup, value, w_dec, padded, out, inputs_ref, last):
    def block(step, value, conv_too=True):
        k = 1 - step
        summed = value.astype(F32) + inputs_ref[k].astype(F32)
        kernel = w_dec.at[k] if conv_too else None
        return forward_block(setup, summed, k, 1, kernel, padded, out)

    if last:
        return lax.fori_loop(0, 2, block, value)
    return block(1, block(0, value), conv_too=False)


def backward_pair(setup, value, side, upward, kernels, padded_cot, kept, cot_ref, skips, skip_in, last):
    normed_ref, scale_ref = kept

    def masked(k, value):
        residual = value.astype(F32) * setup.mask
        conv_cot = residual.astype(BF16)
        cot_ref[k] = conv_cot
        return residual, conv_cot

    def block(step, value):
        k = step if upward else 1 - step
        residual, conv_cot = masked(k, value)
        padded_cot[SIDE : SIDE + CELLS, :] = conv_cot
        hidden_cot = conv_back(padded_cot, kernels.at[k], setup.column)
        total = residual + norm_back(
            hidden_cot, normed_ref[k], scale_ref[k, 0:1], setup.temb(k, side), setup.mask,
            setup.entries, setup.matrix,
        )
        if skip_in is not None:
            total = total + skip_in[k].astype(F32)
        value = total.astype(BF16)
        if skips is not None:
            skips[k] = value
        return value

    if last:
        return lax.fori_loop(0, 2, block, value)
    masked(1 if upward else 0, block(0, value))
    return None


def phase_one(
    where, bucket, latents, time_own, time_other, enc_own, enc_other, emb, matrix,
    normed, scale, hidden, kept, sent, x, time_ref, w_enc, padded, sems,
):
    core = where[1]
    enc_copies = fetch_pair(core, enc_own, enc_other, w_enc, sems.at[0])
    time_copies = fetch_pair(core, time_own, time_other, time_ref, sems.at[1])
    x_copy = pltpu.make_async_copy(latents.at[core], x, sems.at[2, 0])
    x_copy.start()
    clear_edges(padded)
    wait_all([x_copy], time_copies, enc_copies)
    setup = Setup(core, bucket, emb, time_ref, matrix)
    sent[...] = encoder_pair(setup, x[...], w_enc, padded, (normed, scale, hidden), kept)


def phase_two(
    where, bucket, x, time_own, time_other, enc_own, enc_other, dec_own, dec_other, emb, matrix,
    e_normed, e_scale, e_hidden, d_normed, d_scale, d_hidden, sent,
    kept, time_ref, w_enc, w_dec, padded, sems,
):
    core = where[1]
    time_copies = fetch_pair(core, time_own, time_other, time_ref, sems.at[1])
    enc_copies = fetch_pair(core, enc_own, enc_other, w_enc, sems.at[0])
    dec_copies = fetch_pair(core, dec_own, dec_other, w_dec, sems.at[2])
    clear_edges(padded)
    wait_all(time_copies, enc_copies)
    setup = Setup(core, bucket, emb, time_ref, matrix)
    upper = encoder_pair(setup, x[...], w_enc, padded, (e_normed, e_scale, e_hidden), kept)
    wait_all(dec_copies)
    sent[...] = decoder_pair(
        setup, upper, w_dec, padded, (d_normed, d_scale, d_hidden), kept, True
    )


def phase_three(
    scaling, where, bucket, x, cotangent, time_own, time_other, dec_own, dec_other, kept, emb,
    matrix, d_hidden, cots, skips, sent,
    d_normed, d_scale, start, time_ref, w_dec, padded, padded_cot, sems,
):
    core = where[1]
    time_copies = fetch_pair(core, time_own, time_other, time_ref, sems.at[1])
    dec_copies = fetch_pair(core, dec_own, dec_other, w_dec, sems.at[0])
    start_copy = pltpu.make_async_copy(cotangent.at[core], start, sems.at[2, 0])
    start_copy.start()
    clear_edges(padded)
    clear_edges(padded_cot)
    wait_all(time_copies, dec_copies, [start_copy])
    setup = Setup(core, bucket, emb, time_ref, matrix)
    decoder_pair(setup, x[...], w_dec, padded, (d_normed, d_scale, d_hidden), kept, False)
    cot = (start[...].astype(F32) * scaling).astype(BF16)
    sent[...] = backward_pair(
        setup, cot, 1, True, w_dec, padded_cot, (d_normed, d_scale), cots, skips, None, True
    )


def phase_four(
    where, bucket, x, time_own, time_other, enc_own, enc_other, dec_own, dec_other, emb, matrix,
    d_normed, d_scale, e_normed, e_scale, d_cots, e_cots, sent,
    skips, time_ref, w_enc, w_dec, padded_cot, sems,
):
    core = where[1]
    time_copies = fetch_pair(core, time_own, time_other, time_ref, sems.at[1])
    dec_copies = fetch_pair(core, dec_own, dec_other, w_dec, sems.at[0])
    enc_copies = fetch_pair(core, enc_own, enc_other, w_enc, sems.at[2])
    clear_edges(padded_cot)
    wait_all(time_copies, dec_copies)
    setup = Setup(core, bucket, emb, time_ref, matrix)
    cot = backward_pair(
        setup, x[...], 1, True, w_dec, padded_cot, (d_normed, d_scale), d_cots, skips, None, True
    )
    wait_all(enc_copies)
    sent[...] = backward_pair(
        setup, cot, 0, False, w_enc, padded_cot, (e_normed, e_scale), e_cots, None, skips, True
    )


def store_packed(target, slot, row, values):
    first = row * TAPS
    target[slot, first : first + TAPS, :] = values[:, 0:LANES]
    target[slot, FLAT + first : FLAT + first + TAPS, :] = values[:, LANES : 2 * LANES]
    half = FLAT // 2
    pieces = ((0, TAPS // 2), (TAPS // 2, TAPS)) if row == 1 else ((0, TAPS),)
    for begin, end in pieces:
        side = 0 if first + end <= half else 1
        at = 2 * FLAT + first + begin - side * half
        target[slot, at : at + end - begin, side * TAIL : (side + 1) * TAIL] = values[
            begin:end, 2 * LANES : C
        ]


def store_gradients(core, hidden, cots, own, other, padded_cot, turned, pair):
    column = column_index()
    pair[:, PACKED_USED:, :] = jnp.zeros((2, PACKED - PACKED_USED, LANES), F32)

    def section(k, carry):
        values = hidden[k].astype(F32)
        padded_cot[SIDE : SIDE + CELLS, :] = cots[k]
        turned[0:C, :] = shift_right(values, column).T.astype(BF16)
        turned[C : 2 * C, :] = values.T.astype(BF16)
        turned[2 * C : 3 * C, :] = shift_left(values, column).T.astype(BF16)
        for row in range(3):
            part = jnp.dot(
                turned[...],
                padded_cot[(2 - row) * SIDE : (2 - row) * SIDE + CELLS, :],
                preferred_element_type=F32,
            )
            store_packed(pair, jnp.where(core == k, 0, 1), row, part)
        return carry

    lax.fori_loop(0, 2, section, 0)

    def copy(step, carry):
        begin = pl.multiple_of(step * STRIP, STRIP)
        own[pl.ds(begin, STRIP), :] = pair[0, pl.ds(begin, STRIP), :]
        other[pl.ds(begin, STRIP), :] = pair[1, pl.ds(begin, STRIP), :].astype(BF16)
        return carry

    lax.fori_loop(0, PACKED // STRIP, copy, 0)


def weight_phase(
    where, a_hidden, a_cots, b_hidden, b_cots, own, other, padded_cot, turned, pair, hidden, cots
):
    clear_edges(padded_cot)

    @pl.when(where[0] == 0)
    def _():
        hidden[...] = a_hidden[...]
        cots[...] = a_cots[...]

    @pl.when(where[0] != 0)
    def _():
        hidden[...] = b_hidden[...]
        cots[...] = b_cots[...]

    store_gradients(where[1], hidden, cots, own, other, padded_cot, turned, pair)


def phase_five(
    where, bucket, x, time_own, time_other, enc_own, enc_other, skips, emb, matrix,
    e_normed, e_scale, a_hidden, b_hidden, b_cots,
    own, other, padded_cot, turned, pair, hidden, cots, time_ref, w_enc, sems,
):
    clear_edges(padded_cot)
    core = where[1]
    time_copies = fetch_pair(core, time_own, time_other, time_ref, sems.at[1])
    enc_copies = fetch_pair(core, enc_own, enc_other, w_enc, sems.at[0])
    wait_all(time_copies, enc_copies)

    @pl.when(where[0] == 0)
    def _():
        hidden[...] = a_hidden[...]
        setup = Setup(core, bucket, emb, time_ref, matrix)
        backward_pair(
            setup, x[...], 0, False, w_enc, padded_cot, (e_normed, e_scale), cots, None, skips,
            False,
        )

    @pl.when(where[0] != 0)
    def _():
        hidden[...] = b_hidden[...]
        cots[...] = b_cots[...]

    store_gradients(core, hidden, cots, own, other, padded_cot, turned, pair)


def core_add(first, first_other, second, second_other, out):
    rows = out.shape[1] // 2

    def part(at, carry):
        source = pl.ds(pl.multiple_of(at * rows, 16), rows)
        out[at, 0:rows] = (first[source, :] + first_other[source, :].astype(F32)).astype(BF16)
        out[at, rows:] = (second[source, :] + second_other[source, :].astype(F32)).astype(BF16)
        return carry

    lax.fori_loop(0, out.shape[0], part, 0)


def added(parts):
    value = parts[0].astype(F32)
    for at in range(1, parts.shape[0]):
        value = value + parts[at].astype(F32)
    return value


def block_sums(parts, out):
    rows = out.shape[2]
    value = added(parts)
    for which in range(2):
        for layer in range(out.shape[0]):
            begin = (which * out.shape[0] + layer) * rows
            out[layer, which] = value[begin : begin + rows].astype(BF16)


def layer_sums(parts, out):
    value = added(parts).astype(BF16)
    for layer in range(out.shape[0]):
        out[layer] = value


def assemble(parts, out, total):
    layers, _, rows, _ = parts.shape
    for which in range(2):
        for layer in range(layers):
            begin = (which * layers + layer) * rows
            total[begin : begin + rows, :] = parts[layer, which].astype(F32)
    value = total[...].astype(BF16)
    for at in range(out.shape[0]):
        out[at] = value


def unpack(packed, first, second):
    rows = packed.shape[1] // 2
    size = 2 * STRIP
    half = FLAT // 2

    def strip(step, carry):
        for which, grad in enumerate((first, second)):

            def source(begin, which=which):
                begin = begin + step * size
                at = pl.multiple_of(which * rows + lax.rem(begin, rows), 16)
                return packed[lax.div(begin, rows), pl.ds(at, size), :].astype(F32)

            tail = source(2 * FLAT)
            for side in range(2):
                to = pl.ds(pl.multiple_of(step * size + side * half, 16), size)
                grad[to, 0:LANES] = source(side * half)
                grad[to, LANES : 2 * LANES] = source(FLAT + side * half)
                grad[to, 2 * LANES : C] = tail[:, side * TAIL : (side + 1) * TAIL]
        return carry

    lax.fori_loop(0, half // size, strip, 0)


def shape(dims, dtype):
    return jax.ShapeDtypeStruct(dims, dtype)


NORMED = ((2, CELLS, C), F32)
SCALE = ((2, 8, C), F32)
ACTS = ((2, CELLS, C), BF16)
ONE = ((CELLS, C), BF16)
PADDED = pltpu.VMEM((CELLS + 2 * SIDE, TAPS), BF16)
PADDED_COT = pltpu.VMEM((CELLS + 2 * SIDE, C), BF16)
TURNED = pltpu.VMEM((TAPS, CELLS), BF16)
OWN = ((PACKED, LANES), F32)
OTHER = ((PACKED, LANES), BF16)
WEIGHTS = pltpu.VMEM((2, 9, C, C), BF16)
TIMES = pltpu.VMEM((2, 2, C, C), BF16)
SEMS = pltpu.SemaphoreType.DMA((3, 2))


def call(body, spaces, outs, scratch, flops, name, vmem=VMEM_LIMIT):
    def run(*args):
        kinds = {"s": pltpu.SMEM, "h": pltpu.HBM, "v": pltpu.VMEM}
        moved = sum(a.size * a.dtype.itemsize for a in args) + sum(
            math.prod(d) * jnp.dtype(t).itemsize for d, t in outs
        )
        return pl.pallas_call(
            body,
            out_shape=tuple(shape(d, t) for d, t in outs),
            in_specs=[pl.BlockSpec(memory_space=kinds[space]) for space in spaces],
            out_specs=tuple(pl.BlockSpec(memory_space=pltpu.VMEM) for _ in outs),
            scratch_shapes=list(scratch),
            compiler_params=pltpu.CompilerParams(vmem_limit_bytes=vmem),
            cost_estimate=pl.CostEstimate(flops=flops, bytes_accessed=moved, transcendentals=0),
            name=name,
        )(*args)

    return run


CONV = 2 * CELLS * 9 * C * C


def time_embed(timesteps):
    half_width = C // 2
    frequencies = jnp.exp(
        -math.log(10000.0) * jnp.arange(half_width, dtype=F32) / half_width
    )
    angles = timesteps.astype(F32)[:, None] * frequencies[None, :]
    return jnp.concatenate([jnp.cos(angles), jnp.sin(angles)], axis=1).astype(BF16)


def to_other_core(array):
    return lax.ppermute(array, "core", [(0, 1), (1, 0)])


BLOCK = ("z_low", "far", "y")
LAYERS = "z_high"
DP = (LAYERS, *BLOCK)


def exchange(parts, axes):
    return lax.all_to_all(parts, axes, split_axis=0, concat_axis=0, tiled=True)


def gradients(first, second):
    count, layers = lax.axis_size(BLOCK), lax.axis_size(LAYERS)
    rows = PACKED // count
    (pair,) = call(
        core_add, "vvvv", [((count, 2 * rows, LANES), BF16)], [], 2 * PACKED * LANES, "core_add"
    )(*first, *second)
    cut = ((layers, 2, rows // layers, LANES), BF16)
    (sums,) = call(block_sums, "v", [cut], [], 2 * PACKED * LANES, "block_sums")(
        exchange(pair, BLOCK)
    )
    (sums,) = call(layer_sums, "v", [cut], [], 2 * rows * LANES, "layer_sums")(
        exchange(sums, LAYERS)
    )
    (copies,) = call(
        assemble, "v", [((count, 2 * rows, LANES), BF16)], [pltpu.VMEM((2 * rows, LANES), F32)],
        2 * PACKED * LANES, "assemble",
    )(exchange(sums, LAYERS))
    grads = call(unpack, "v", [((FLAT, C), F32)] * 2, [], 2 * PACKED * LANES, "unpack")(
        exchange(copies, BLOCK)
    )
    return tuple(grad.reshape(1, 3, 3, C, C) for grad in grads)


def local(latents, cotangent, bucket, timesteps, w_enc, w_dec, w_time):
    where = jnp.stack([lax.axis_index(axis) for axis in ("near", "core")])
    where = where.astype(jnp.int32)
    micro_count = latents.shape[0]
    loss_scale = float(micro_count * lax.axis_size(DP) * CELLS) ** (-0.5)

    enc = w_enc.reshape(9, C, C)
    dec = w_dec.reshape(9, C, C)
    times = w_time.reshape(2, C, C)
    times = (times, to_other_core(times))
    enc = (enc, to_other_core(enc))
    emb = jnp.pad(time_embed(timesteps), ((0, 16 - micro_count), (0, 0)))
    dec, enc, times, emb, where = lax.optimization_barrier((dec, enc, times, emb, where))
    dec = (dec, to_other_core(dec))
    latents = latents.reshape(micro_count, CELLS, C)
    cotangent = cotangent.reshape(micro_count, CELLS, C)
    matrix = group_matrix()

    def up(value):
        return lax.ppermute(value, "near", [(0, 1)])

    def down(value):
        return lax.ppermute(value, "near", [(1, 0)])

    one = call(
        phase_one, "ss" + "h" * 5 + "vv", [NORMED, SCALE, ACTS, ACTS, ONE],
        [pltpu.VMEM(*ONE), TIMES, WEIGHTS, PADDED, SEMS], 2 * CONV, "one",
    )
    a_normed, a_scale, a_hidden, a_kept, sent = one(
        where, bucket, latents, *times, *enc, emb, matrix
    )
    two = call(
        phase_two, "ssv" + "h" * 6 + "vv", [NORMED, SCALE, ACTS, NORMED, SCALE, ACTS, ONE],
        [pltpu.VMEM(*ACTS), TIMES, WEIGHTS, WEIGHTS, PADDED, SEMS], 4 * CONV, "two",
    )
    be_normed, be_scale, be_hidden, bd_normed, bd_scale, bd_hidden, sent = two(
        where, bucket, up(sent), *times, *enc, *dec, emb, matrix
    )
    three = call(
        functools.partial(phase_three, loss_scale), "ssv" + "h" * 5 + "vvv",
        [ACTS, ACTS, ACTS, ONE],
        [
            pltpu.VMEM(*NORMED), pltpu.VMEM(*SCALE), pltpu.VMEM(*ONE), TIMES, WEIGHTS, PADDED,
            PADDED_COT, SEMS,
        ],
        3 * CONV, "three",
    )
    ad_hidden, ad_cots, a_skips, sent = three(
        where, bucket, down(sent), cotangent, *times, *dec, a_kept, emb, matrix
    )
    four = call(
        phase_four, "ssv" + "h" * 6 + "v" * 6, [ACTS, ACTS, ONE],
        [pltpu.VMEM(*ACTS), TIMES, WEIGHTS, WEIGHTS, PADDED_COT, SEMS], 4 * CONV, "four",
    )
    bd_cots, be_cots, sent = four(
        where, bucket, up(sent), *times, *enc, *dec, emb, matrix,
        bd_normed, bd_scale, be_normed, be_scale,
    )
    received = down(sent)
    work = [PADDED_COT, TURNED, pltpu.VMEM((2, PACKED, LANES), F32), pltpu.VMEM(*ACTS), pltpu.VMEM(*ACTS)]
    weights = call(weight_phase, "svvvv", [OWN, OTHER], work, 2 * CONV, "weights")
    own_dec, other_dec = weights(where, ad_hidden, ad_cots, bd_hidden, bd_cots)
    dec_pair = (own_dec, to_other_core(other_dec))
    five = call(
        phase_five, "ssv" + "h" * 4 + "v" * 8, [OWN, OTHER], [*work, TIMES, WEIGHTS, SEMS],
        3 * CONV, "five",
    )
    own_enc, other_enc = five(
        where, bucket, received, *times, *enc, a_skips, emb, matrix, a_normed, a_scale, a_hidden,
        be_hidden, be_cots,
    )

    return gradients((own_enc, to_other_core(other_enc)), dec_pair)


def solution(mesh):
    segments, dp = mesh.shape["segment"], mesh.shape["dp"]
    near, far, rows = segments // 2, 2, 4
    split = Mesh(
        mesh.devices.reshape(near, 2, dp // (2 * far * rows), 2, far, rows),
        ("near", "core", *DP),
    )
    section, micro = ("near", "core"), DP
    placed = (
        P(micro, None, None, None),
        P(micro, None, None, None),
        P(micro, None),
        P(micro),
        P(section, None, None, None, None),
        P(section, None, None, None, None),
        P(section, None, None, None),
    )
    grads = P(section, None, None, None, None)
    return jax.shard_map(
        local, mesh=split, in_specs=placed, out_specs=(grads, grads), check_vma=False
    )
```

```python
import functools
import math

import jax
import jax.numpy as jnp
import numpy as np
from jax import lax
from jax.experimental import pallas as pl
from jax.experimental.pallas import tpu as pltpu
from jax.sharding import Mesh, PartitionSpec as P

G = 32
SIDE = 16
CELLS = SIDE * SIDE
C = 320
TAPS = 3 * C
F32 = jnp.float32
BF16 = jnp.bfloat16
VMEM_LIMIT = 30 * 1024 * 1024
ALL_VMEM = 60 * 1024 * 1024
LANES = 128
FLAT = 9 * C
TAIL = C - 2 * LANES
PACKED_USED = 2 * FLAT + FLAT // 2
PACKED = 64 * 120
STRIP = 240

NT = (((1,), (1,)), ((), ()))


def group_matrix():
    index = np.arange(C) // (C // G)
    return jnp.asarray((index[:, None] == index[None, :]).astype(np.float32), BF16)


def group_sums(columns, matrix):
    row = lax.broadcasted_iota(jnp.int32, (16, C), 0)
    stacked = jnp.zeros((16, C), F32)
    for at, column in enumerate(columns):
        high = column.astype(BF16).astype(F32)
        rest = column - high
        middle = rest.astype(BF16).astype(F32)
        low = (rest - middle).astype(BF16).astype(F32)
        for part, value in enumerate((high, middle, low)):
            stacked = jnp.where(row == 3 * at + part, value, stacked)
    sums = jnp.dot(stacked.astype(BF16), matrix, preferred_element_type=F32)
    return [
        sums[3 * at : 3 * at + 1] + sums[3 * at + 1 : 3 * at + 2] + sums[3 * at + 2 : 3 * at + 3]
        for at in range(len(columns))
    ]


def col_sum(values):
    return jnp.sum(values, axis=0, keepdims=True)


def column_index():
    return lax.broadcasted_iota(jnp.int32, (CELLS, C), 0) % SIDE


def shift_right(values, column):
    return jnp.where(column == 0, 0.0, pltpu.roll(values, 1, axis=0))


def shift_left(values, column):
    return jnp.where(column == SIDE - 1, 0.0, pltpu.roll(values, CELLS - 1, axis=0))


def clear_edges(padded):
    width = padded.shape[1]
    padded[0:SIDE, :] = jnp.zeros((SIDE, width), BF16)
    padded[SIDE + CELLS :, :] = jnp.zeros((SIDE, width), BF16)


def store_windows(padded, hidden, column):
    padded[SIDE : SIDE + CELLS, 0:C] = shift_right(hidden, column).astype(BF16)
    padded[SIDE : SIDE + CELLS, C : 2 * C] = hidden.astype(BF16)
    padded[SIDE : SIDE + CELLS, 2 * C : 3 * C] = shift_left(hidden, column).astype(BF16)


def norm_hidden(values, mask, temb, entries, matrix):
    mean = group_sums([col_sum(values * mask)], matrix)[0] / entries
    centered = values - mean
    variance = group_sums([col_sum(centered * centered * mask)], matrix)[0] / entries
    scale = lax.rsqrt(variance + 1e-05)
    normed = centered * scale
    shifted = normed + temb
    hidden = shifted / (1.0 + jnp.exp(-shifted)) * mask
    return normed, scale, hidden


def taps(kernel, row):
    return kernel[3 * row : 3 * row + 3].reshape(TAPS, C)


def conv(padded, kernel):
    total = None
    for row in range(3):
        part = jnp.dot(
            padded[row * SIDE : row * SIDE + CELLS, :], taps(kernel, row), preferred_element_type=F32
        )
        total = part if total is None else total + part
    return total


def conv_back(cot_padded, kernel, column):
    total = None
    for row in range(3):
        part = lax.dot_general(
            cot_padded[(2 - row) * SIDE : (2 - row) * SIDE + CELLS, :],
            taps(kernel, row),
            NT,
            preferred_element_type=F32,
        )
        total = part if total is None else total + part
    left, middle, right = total[:, 0:C], total[:, C : 2 * C], total[:, 2 * C : 3 * C]
    return shift_left(left, column) + middle + shift_right(right, column)


def norm_back(hidden_cot, normed, scale, temb, mask, entries, matrix):
    shifted = normed + temb
    gate = 1.0 / (1.0 + jnp.exp(-shifted))
    flow = hidden_cot * mask * (gate * (1.0 + shifted * (1.0 - gate)))
    plain, cross = group_sums([col_sum(flow), col_sum(flow * normed)], matrix)
    return scale * (flow - mask * (plain / entries + normed * (cross / entries)))


def mask_of(bucket_ref, core):
    row = lax.broadcasted_iota(jnp.int32, (CELLS, C), 0)
    inside = (row // SIDE < bucket_ref[core, 0]) & (row % SIDE < bucket_ref[core, 1])
    return inside.astype(F32)


def entries_of(bucket_ref, core):
    return (bucket_ref[core, 0] * bucket_ref[core, 1] * (C // G)).astype(F32)


class Setup:
    def __init__(self, core, bucket, embedding, time_ref, matrix):
        self.core = core
        self.column = column_index()
        self.mask = mask_of(bucket, core)
        self.entries = entries_of(bucket, core)
        self.matrix = matrix[...]
        self.embedding = embedding
        self.time_ref = time_ref

    def temb(self, k, side):
        rows = jnp.dot(self.embedding[...], self.time_ref[k, side], preferred_element_type=F32)
        at = lax.broadcasted_iota(jnp.int32, rows.shape, 0)
        return col_sum(jnp.where(at == self.core, rows, 0.0))


def fetch_pair(core, own, other, target, sems):
    copies = [
        pltpu.make_async_copy(own, target.at[core], sems.at[0]),
        pltpu.make_async_copy(other, target.at[1 - core], sems.at[1]),
    ]
    for copy in copies:
        copy.start()
    return copies


def wait_all(*groups):
    for copies in groups:
        for copy in copies:
            copy.wait()


def forward_block(setup, values, k, side, kernel, padded, out):
    normed_ref, scale_ref, hidden_ref = out
    normed, scale, hidden = norm_hidden(
        values, setup.mask, setup.temb(k, side), setup.entries, setup.matrix
    )
    normed_ref[k] = normed
    scale_ref[k] = jnp.broadcast_to(scale, (8, C))
    hidden_ref[k] = hidden.astype(BF16)
    if kernel is None:
        return None
    store_windows(padded, hidden, setup.column)
    return ((values + conv(padded, kernel)) * setup.mask).astype(BF16)


def encoder_pair(setup, value, w_enc, padded, out, inputs_ref):
    def block(k, value):
        inputs_ref[k] = value
        return forward_block(setup, value.astype(F32), k, 0, w_enc.at[k], padded, out)

    return lax.fori_loop(0, 2, block, value)


def decoder_pair(setup, value, w_dec, padded, out, inputs_ref, last):
    def block(step, value, conv_too=True):
        k = 1 - step
        summed = value.astype(F32) + inputs_ref[k].astype(F32)
        kernel = w_dec.at[k] if conv_too else None
        return forward_block(setup, summed, k, 1, kernel, padded, out)

    if last:
        return lax.fori_loop(0, 2, block, value)
    return block(1, block(0, value), conv_too=False)


def backward_pair(setup, value, side, upward, kernels, padded_cot, kept, cot_ref, skips, skip_in, last):
    normed_ref, scale_ref = kept

    def masked(k, value):
        residual = value.astype(F32) * setup.mask
        conv_cot = residual.astype(BF16)
        cot_ref[k] = conv_cot
        return residual, conv_cot

    def block(step, value):
        k = step if upward else 1 - step
        residual, conv_cot = masked(k, value)
        padded_cot[SIDE : SIDE + CELLS, :] = conv_cot
        hidden_cot = conv_back(padded_cot, kernels.at[k], setup.column)
        total = residual + norm_back(
            hidden_cot, normed_ref[k], scale_ref[k, 0:1], setup.temb(k, side), setup.mask,
            setup.entries, setup.matrix,
        )
        if skip_in is not None:
            total = total + skip_in[k].astype(F32)
        value = total.astype(BF16)
        if skips is not None:
            skips[k] = value
        return value

    if last:
        return lax.fori_loop(0, 2, block, value)
    masked(1 if upward else 0, block(0, value))
    return None


def phase_one(
    where, bucket, latents, time_own, time_other, enc_own, enc_other, emb, matrix,
    normed, scale, hidden, kept, sent, x, time_ref, w_enc, padded, sems,
):
    core = where[1]
    enc_copies = fetch_pair(core, enc_own, enc_other, w_enc, sems.at[0])
    time_copies = fetch_pair(core, time_own, time_other, time_ref, sems.at[1])
    x_copy = pltpu.make_async_copy(latents.at[core], x, sems.at[2, 0])
    x_copy.start()
    clear_edges(padded)
    wait_all([x_copy], time_copies, enc_copies)
    setup = Setup(core, bucket, emb, time_ref, matrix)
    sent[...] = encoder_pair(setup, x[...], w_enc, padded, (normed, scale, hidden), kept)


def phase_two(
    where, bucket, x, time_own, time_other, enc_own, enc_other, dec_own, dec_other, emb, matrix,
    e_normed, e_scale, e_hidden, d_normed, d_scale, d_hidden, sent,
    kept, time_ref, w_enc, w_dec, padded, sems,
):
    core = where[1]
    time_copies = fetch_pair(core, time_own, time_other, time_ref, sems.at[1])
    enc_copies = fetch_pair(core, enc_own, enc_other, w_enc, sems.at[0])
    dec_copies = fetch_pair(core, dec_own, dec_other, w_dec, sems.at[2])
    clear_edges(padded)
    wait_all(time_copies, enc_copies)
    setup = Setup(core, bucket, emb, time_ref, matrix)
    upper = encoder_pair(setup, x[...], w_enc, padded, (e_normed, e_scale, e_hidden), kept)
    wait_all(dec_copies)
    sent[...] = decoder_pair(
        setup, upper, w_dec, padded, (d_normed, d_scale, d_hidden), kept, True
    )


def phase_three(
    scaling, where, bucket, x, cotangent, time_own, time_other, dec_own, dec_other, kept, emb,
    matrix, d_hidden, cots, skips, sent,
    d_normed, d_scale, start, time_ref, w_dec, padded, padded_cot, sems,
):
    core = where[1]
    time_copies = fetch_pair(core, time_own, time_other, time_ref, sems.at[1])
    dec_copies = fetch_pair(core, dec_own, dec_other, w_dec, sems.at[0])
    start_copy = pltpu.make_async_copy(cotangent.at[core], start, sems.at[2, 0])
    start_copy.start()
    clear_edges(padded)
    clear_edges(padded_cot)
    wait_all(time_copies, dec_copies, [start_copy])
    setup = Setup(core, bucket, emb, time_ref, matrix)
    decoder_pair(setup, x[...], w_dec, padded, (d_normed, d_scale, d_hidden), kept, False)
    cot = (start[...].astype(F32) * scaling).astype(BF16)
    sent[...] = backward_pair(
        setup, cot, 1, True, w_dec, padded_cot, (d_normed, d_scale), cots, skips, None, True
    )


def phase_four(
    where, bucket, x, time_own, time_other, enc_own, enc_other, dec_own, dec_other, emb, matrix,
    d_normed, d_scale, e_normed, e_scale, d_cots, e_cots, sent,
    skips, time_ref, w_enc, w_dec, padded_cot, sems,
):
    core = where[1]
    time_copies = fetch_pair(core, time_own, time_other, time_ref, sems.at[1])
    dec_copies = fetch_pair(core, dec_own, dec_other, w_dec, sems.at[0])
    enc_copies = fetch_pair(core, enc_own, enc_other, w_enc, sems.at[2])
    clear_edges(padded_cot)
    wait_all(time_copies, dec_copies)
    setup = Setup(core, bucket, emb, time_ref, matrix)
    cot = backward_pair(
        setup, x[...], 1, True, w_dec, padded_cot, (d_normed, d_scale), d_cots, skips, None, True
    )
    wait_all(enc_copies)
    sent[...] = backward_pair(
        setup, cot, 0, False, w_enc, padded_cot, (e_normed, e_scale), e_cots, None, skips, True
    )


def store_packed(target, slot, row, values):
    first = row * TAPS
    target[slot, first : first + TAPS, :] = values[:, 0:LANES]
    target[slot, FLAT + first : FLAT + first + TAPS, :] = values[:, LANES : 2 * LANES]
    half = FLAT // 2
    pieces = ((0, TAPS // 2), (TAPS // 2, TAPS)) if row == 1 else ((0, TAPS),)
    for begin, end in pieces:
        side = 0 if first + end <= half else 1
        at = 2 * FLAT + first + begin - side * half
        target[slot, at : at + end - begin, side * TAIL : (side + 1) * TAIL] = values[
            begin:end, 2 * LANES : C
        ]


def store_gradients(core, hidden, cots, own, other, padded_cot, turned, pair):
    column = column_index()
    pair[:, PACKED_USED:, :] = jnp.zeros((2, PACKED - PACKED_USED, LANES), F32)

    def section(k, carry):
        values = hidden[k].astype(F32)
        padded_cot[SIDE : SIDE + CELLS, :] = cots[k]
        turned[0:C, :] = shift_right(values, column).T.astype(BF16)
        turned[C : 2 * C, :] = values.T.astype(BF16)
        turned[2 * C : 3 * C, :] = shift_left(values, column).T.astype(BF16)
        for row in range(3):
            part = jnp.dot(
                turned[...],
                padded_cot[(2 - row) * SIDE : (2 - row) * SIDE + CELLS, :],
                preferred_element_type=F32,
            )
            store_packed(pair, jnp.where(core == k, 0, 1), row, part)
        return carry

    lax.fori_loop(0, 2, section, 0)

    def copy(step, carry):
        begin = pl.multiple_of(step * STRIP, STRIP)
        own[pl.ds(begin, STRIP), :] = pair[0, pl.ds(begin, STRIP), :]
        other[pl.ds(begin, STRIP), :] = pair[1, pl.ds(begin, STRIP), :].astype(BF16)
        return carry

    lax.fori_loop(0, PACKED // STRIP, copy, 0)


def weight_phase(
    where, a_hidden, a_cots, b_hidden, b_cots, own, other, padded_cot, turned, pair, hidden, cots
):
    clear_edges(padded_cot)

    @pl.when(where[0] == 0)
    def _():
        hidden[...] = a_hidden[...]
        cots[...] = a_cots[...]

    @pl.when(where[0] != 0)
    def _():
        hidden[...] = b_hidden[...]
        cots[...] = b_cots[...]

    store_gradients(where[1], hidden, cots, own, other, padded_cot, turned, pair)


def phase_five(
    where, bucket, x, time_own, time_other, enc_own, enc_other, skips, emb, matrix,
    e_normed, e_scale, a_hidden, b_hidden, b_cots,
    own, other, padded_cot, turned, pair, hidden, cots, time_ref, w_enc, sems,
):
    clear_edges(padded_cot)
    core = where[1]
    time_copies = fetch_pair(core, time_own, time_other, time_ref, sems.at[1])
    enc_copies = fetch_pair(core, enc_own, enc_other, w_enc, sems.at[0])
    wait_all(time_copies, enc_copies)

    @pl.when(where[0] == 0)
    def _():
        hidden[...] = a_hidden[...]
        setup = Setup(core, bucket, emb, time_ref, matrix)
        backward_pair(
            setup, x[...], 0, False, w_enc, padded_cot, (e_normed, e_scale), cots, None, skips,
            False,
        )

    @pl.when(where[0] != 0)
    def _():
        hidden[...] = b_hidden[...]
        cots[...] = b_cots[...]

    store_gradients(core, hidden, cots, own, other, padded_cot, turned, pair)


def core_add(first, first_other, second, second_other, out):
    rows = out.shape[1] // 2

    def part(at, carry):
        source = pl.ds(pl.multiple_of(at * rows, 16), rows)
        out[at, 0:rows] = (first[source, :] + first_other[source, :].astype(F32)).astype(BF16)
        out[at, rows:] = (second[source, :] + second_other[source, :].astype(F32)).astype(BF16)
        return carry

    lax.fori_loop(0, out.shape[0], part, 0)


def added(parts):
    value = parts[0].astype(F32)
    for at in range(1, parts.shape[0]):
        value = value + parts[at].astype(F32)
    return value


def block_sums(where, parts, kept, *rest):
    *chunks, total = rest
    layers = len(chunks) + 1
    rows = kept.shape[1]
    total[...] = added(parts)
    for which in range(2):
        for ahead in range(layers):
            at = which * layers + lax.rem(where[2] + ahead, layers)
            value = total[pl.ds(pl.multiple_of(at * rows, 8), rows), :]
            if ahead == 0:
                kept[which] = value
            else:
                chunks[ahead - 1][which] = value.astype(BF16)


def layer_sums(kept, *rest):
    *received, out = rest
    value = kept[...]
    for part in received:
        value = value + part[...].astype(F32)
    out[...] = value.astype(BF16)


def assemble(where, *rest):
    *chunks, out, total = rest
    layers = len(chunks)
    rows = chunks[0].shape[1]
    for which in range(2):
        for behind, chunk in enumerate(chunks):
            at = which * layers + lax.rem(where[2] + layers - behind, layers)
            total[pl.ds(pl.multiple_of(at * rows, 8), rows), :] = chunk[which].astype(F32)
    value = total[...].astype(BF16)
    for at in range(out.shape[0]):
        out[at] = value


def unpack(packed, first, second):
    rows = packed.shape[1] // 2
    size = 2 * STRIP
    half = FLAT // 2

    def strip(step, carry):
        for which, grad in enumerate((first, second)):

            def source(begin, which=which):
                begin = begin + step * size
                at = pl.multiple_of(which * rows + lax.rem(begin, rows), 16)
                return packed[lax.div(begin, rows), pl.ds(at, size), :].astype(F32)

            tail = source(2 * FLAT)
            for side in range(2):
                to = pl.ds(pl.multiple_of(step * size + side * half, 16), size)
                grad[to, 0:LANES] = source(side * half)
                grad[to, LANES : 2 * LANES] = source(FLAT + side * half)
                grad[to, 2 * LANES : C] = tail[:, side * TAIL : (side + 1) * TAIL]
        return carry

    lax.fori_loop(0, half // size, strip, 0)


def shape(dims, dtype):
    return jax.ShapeDtypeStruct(dims, dtype)


NORMED = ((2, CELLS, C), F32)
SCALE = ((2, 8, C), F32)
ACTS = ((2, CELLS, C), BF16)
ONE = ((CELLS, C), BF16)
PADDED = pltpu.VMEM((CELLS + 2 * SIDE, TAPS), BF16)
PADDED_COT = pltpu.VMEM((CELLS + 2 * SIDE, C), BF16)
TURNED = pltpu.VMEM((TAPS, CELLS), BF16)
OWN = ((PACKED, LANES), F32)
OTHER = ((PACKED, LANES), BF16)
WEIGHTS = pltpu.VMEM((2, 9, C, C), BF16)
TIMES = pltpu.VMEM((2, 2, C, C), BF16)
SEMS = pltpu.SemaphoreType.DMA((3, 2))


def call(body, spaces, outs, scratch, flops, name, vmem=VMEM_LIMIT):
    def run(*args):
        kinds = {"s": pltpu.SMEM, "h": pltpu.HBM, "v": pltpu.VMEM}
        moved = sum(a.size * a.dtype.itemsize for a in args) + sum(
            math.prod(d) * jnp.dtype(t).itemsize for d, t in outs
        )
        return pl.pallas_call(
            body,
            out_shape=tuple(shape(d, t) for d, t in outs),
            in_specs=[pl.BlockSpec(memory_space=kinds[space]) for space in spaces],
            out_specs=tuple(pl.BlockSpec(memory_space=pltpu.VMEM) for _ in outs),
            scratch_shapes=list(scratch),
            compiler_params=pltpu.CompilerParams(vmem_limit_bytes=vmem),
            cost_estimate=pl.CostEstimate(flops=flops, bytes_accessed=moved, transcendentals=0),
            name=name,
        )(*args)

    return run


CONV = 2 * CELLS * 9 * C * C


def time_embed(timesteps):
    half_width = C // 2
    frequencies = jnp.exp(
        -math.log(10000.0) * jnp.arange(half_width, dtype=F32) / half_width
    )
    angles = timesteps.astype(F32)[:, None] * frequencies[None, :]
    return jnp.concatenate([jnp.cos(angles), jnp.sin(angles)], axis=1).astype(BF16)


def to_other_core(array):
    return lax.ppermute(array, "core", [(0, 1), (1, 0)])


BLOCK = ("z_low", "far", "y")
LAYERS = "z_high"
DP = (LAYERS, *BLOCK)


def exchange(parts, axes):
    return lax.all_to_all(parts, axes, split_axis=0, concat_axis=0, tiled=True)


def ahead(value, steps):
    count = lax.axis_size(LAYERS)
    return lax.ppermute(value, LAYERS, [(at, (at + steps) % count) for at in range(count)])


def gradients(where, first, second):
    count, layers = lax.axis_size(BLOCK), lax.axis_size(LAYERS)
    rows = PACKED // count
    (pair,) = call(
        core_add, "vvvv", [((count, 2 * rows, LANES), BF16)], [], 2 * PACKED * LANES, "core_add"
    )(*first, *second)
    cut = (2, rows // layers, LANES)
    total = [pltpu.VMEM((2 * rows, LANES), F32)]
    kept, *chunks = call(
        block_sums, "sv", [(cut, F32)] + [(cut, BF16)] * (layers - 1), total, 2 * PACKED * LANES,
        "block_sums",
    )(where, exchange(pair, BLOCK))
    received = [ahead(chunk, step + 1) for step, chunk in enumerate(chunks)]
    (mine,) = call(
        layer_sums, "v" * layers, [(cut, BF16)], [], 2 * rows * LANES, "layer_sums"
    )(kept, *received)
    received = [ahead(mine, step) for step in range(1, layers)]
    (copies,) = call(
        assemble, "s" + "v" * layers, [((count, 2 * rows, LANES), BF16)], total,
        2 * PACKED * LANES, "assemble",
    )(where, mine, *received)
    grads = call(unpack, "v", [((FLAT, C), F32)] * 2, [], 2 * PACKED * LANES, "unpack")(
        exchange(copies, BLOCK)
    )
    return tuple(grad.reshape(1, 3, 3, C, C) for grad in grads)


def local(latents, cotangent, bucket, timesteps, w_enc, w_dec, w_time):
    where = jnp.stack([lax.axis_index(axis) for axis in ("near", "core", LAYERS)])
    where = where.astype(jnp.int32)
    micro_count = latents.shape[0]
    loss_scale = float(micro_count * lax.axis_size(DP) * CELLS) ** (-0.5)

    enc = w_enc.reshape(9, C, C)
    dec = w_dec.reshape(9, C, C)
    times = w_time.reshape(2, C, C)
    times = (times, to_other_core(times))
    enc = (enc, to_other_core(enc))
    emb = jnp.pad(time_embed(timesteps), ((0, 16 - micro_count), (0, 0)))
    dec, enc, times, emb, where = lax.optimization_barrier((dec, enc, times, emb, where))
    dec = (dec, to_other_core(dec))
    latents = latents.reshape(micro_count, CELLS, C)
    cotangent = cotangent.reshape(micro_count, CELLS, C)
    matrix = group_matrix()

    def up(value):
        return lax.ppermute(value, "near", [(0, 1)])

    def down(value):
        return lax.ppermute(value, "near", [(1, 0)])

    one = call(
        phase_one, "ss" + "h" * 5 + "vv", [NORMED, SCALE, ACTS, ACTS, ONE],
        [pltpu.VMEM(*ONE), TIMES, WEIGHTS, PADDED, SEMS], 2 * CONV, "one",
    )
    a_normed, a_scale, a_hidden, a_kept, sent = one(
        where, bucket, latents, *times, *enc, emb, matrix
    )
    two = call(
        phase_two, "ssv" + "h" * 6 + "vv", [NORMED, SCALE, ACTS, NORMED, SCALE, ACTS, ONE],
        [pltpu.VMEM(*ACTS), TIMES, WEIGHTS, WEIGHTS, PADDED, SEMS], 4 * CONV, "two",
    )
    be_normed, be_scale, be_hidden, bd_normed, bd_scale, bd_hidden, sent = two(
        where, bucket, up(sent), *times, *enc, *dec, emb, matrix
    )
    three = call(
        functools.partial(phase_three, loss_scale), "ssv" + "h" * 5 + "vvv",
        [ACTS, ACTS, ACTS, ONE],
        [
            pltpu.VMEM(*NORMED), pltpu.VMEM(*SCALE), pltpu.VMEM(*ONE), TIMES, WEIGHTS, PADDED,
            PADDED_COT, SEMS,
        ],
        3 * CONV, "three",
    )
    ad_hidden, ad_cots, a_skips, sent = three(
        where, bucket, down(sent), cotangent, *times, *dec, a_kept, emb, matrix
    )
    four = call(
        phase_four, "ssv" + "h" * 6 + "v" * 6, [ACTS, ACTS, ONE],
        [pltpu.VMEM(*ACTS), TIMES, WEIGHTS, WEIGHTS, PADDED_COT, SEMS], 4 * CONV, "four",
    )
    bd_cots, be_cots, sent = four(
        where, bucket, up(sent), *times, *enc, *dec, emb, matrix,
        bd_normed, bd_scale, be_normed, be_scale,
    )
    received = down(sent)
    work = [PADDED_COT, TURNED, pltpu.VMEM((2, PACKED, LANES), F32), pltpu.VMEM(*ACTS), pltpu.VMEM(*ACTS)]
    weights = call(weight_phase, "svvvv", [OWN, OTHER], work, 2 * CONV, "weights")
    own_dec, other_dec = weights(where, ad_hidden, ad_cots, bd_hidden, bd_cots)
    dec_pair = (own_dec, to_other_core(other_dec))
    five = call(
        phase_five, "ssv" + "h" * 4 + "v" * 8, [OWN, OTHER], [*work, TIMES, WEIGHTS, SEMS],
        3 * CONV, "five",
    )
    own_enc, other_enc = five(
        where, bucket, received, *times, *enc, a_skips, emb, matrix, a_normed, a_scale, a_hidden,
        be_hidden, be_cots,
    )

    return gradients(where, (own_enc, to_other_core(other_enc)), dec_pair)


def solution(mesh):
    segments, dp = mesh.shape["segment"], mesh.shape["dp"]
    near, far, rows = segments // 2, 2, 4
    split = Mesh(
        mesh.devices.reshape(near, 2, dp // (2 * far * rows), 2, far, rows),
        ("near", "core", *DP),
    )
    section, micro = ("near", "core"), DP
    placed = (
        P(micro, None, None, None),
        P(micro, None, None, None),
        P(micro, None),
        P(micro),
        P(section, None, None, None, None),
        P(section, None, None, None, None),
        P(section, None, None, None),
    )
    grads = P(section, None, None, None, None)
    return jax.shard_map(
        local, mesh=split, in_specs=placed, out_specs=(grads, grads), check_vma=False
    )
```

```python
import functools
import math

import jax
import jax.numpy as jnp
import numpy as np
from jax import lax
from jax.experimental import pallas as pl
from jax.experimental.pallas import tpu as pltpu
from jax.sharding import Mesh, PartitionSpec as P

G = 32
SIDE = 16
CELLS = SIDE * SIDE
C = 320
TAPS = 3 * C
F32 = jnp.float32
BF16 = jnp.bfloat16
VMEM_LIMIT = 30 * 1024 * 1024
ALL_VMEM = 60 * 1024 * 1024
LANES = 128
FLAT = 9 * C
TAIL = C - 2 * LANES
PACKED_USED = 2 * FLAT + FLAT // 2
PACKED = 64 * 120
STRIP = 240

NT = (((1,), (1,)), ((), ()))


def group_matrix():
    index = np.arange(C) // (C // G)
    return jnp.asarray((index[:, None] == index[None, :]).astype(np.float32), BF16)


def group_sums(columns, matrix):
    row = lax.broadcasted_iota(jnp.int32, (16, C), 0)
    stacked = jnp.zeros((16, C), F32)
    for at, column in enumerate(columns):
        high = column.astype(BF16).astype(F32)
        rest = column - high
        middle = rest.astype(BF16).astype(F32)
        low = (rest - middle).astype(BF16).astype(F32)
        for part, value in enumerate((high, middle, low)):
            stacked = jnp.where(row == 3 * at + part, value, stacked)
    sums = jnp.dot(stacked.astype(BF16), matrix, preferred_element_type=F32)
    return [
        sums[3 * at : 3 * at + 1] + sums[3 * at + 1 : 3 * at + 2] + sums[3 * at + 2 : 3 * at + 3]
        for at in range(len(columns))
    ]


def col_sum(values):
    return jnp.sum(values, axis=0, keepdims=True)


def column_index():
    return lax.broadcasted_iota(jnp.int32, (CELLS, C), 0) % SIDE


def shift_right(values, column):
    return jnp.where(column == 0, 0.0, pltpu.roll(values, 1, axis=0))


def shift_left(values, column):
    return jnp.where(column == SIDE - 1, 0.0, pltpu.roll(values, CELLS - 1, axis=0))


def clear_edges(padded):
    width = padded.shape[1]
    padded[0:SIDE, :] = jnp.zeros((SIDE, width), BF16)
    padded[SIDE + CELLS :, :] = jnp.zeros((SIDE, width), BF16)


def store_windows(padded, hidden, column):
    padded[SIDE : SIDE + CELLS, 0:C] = shift_right(hidden, column).astype(BF16)
    padded[SIDE : SIDE + CELLS, C : 2 * C] = hidden.astype(BF16)
    padded[SIDE : SIDE + CELLS, 2 * C : 3 * C] = shift_left(hidden, column).astype(BF16)


def norm_hidden(values, mask, temb, entries, matrix):
    mean = group_sums([col_sum(values * mask)], matrix)[0] / entries
    centered = values - mean
    variance = group_sums([col_sum(centered * centered * mask)], matrix)[0] / entries
    scale = lax.rsqrt(variance + 1e-05)
    normed = centered * scale
    shifted = normed + temb
    hidden = shifted / (1.0 + jnp.exp(-shifted)) * mask
    return normed, scale, hidden


def taps(kernel, row):
    return kernel[3 * row : 3 * row + 3].reshape(TAPS, C)


def conv(padded, kernel):
    total = None
    for row in range(3):
        part = jnp.dot(
            padded[row * SIDE : row * SIDE + CELLS, :], taps(kernel, row), preferred_element_type=F32
        )
        total = part if total is None else total + part
    return total


def conv_back(cot_padded, kernel, column):
    total = None
    for row in range(3):
        part = lax.dot_general(
            cot_padded[(2 - row) * SIDE : (2 - row) * SIDE + CELLS, :],
            taps(kernel, row),
            NT,
            preferred_element_type=F32,
        )
        total = part if total is None else total + part
    left, middle, right = total[:, 0:C], total[:, C : 2 * C], total[:, 2 * C : 3 * C]
    return shift_left(left, column) + middle + shift_right(right, column)


def norm_back(hidden_cot, normed, scale, temb, mask, entries, matrix):
    shifted = normed + temb
    gate = 1.0 / (1.0 + jnp.exp(-shifted))
    flow = hidden_cot * mask * (gate * (1.0 + shifted * (1.0 - gate)))
    plain, cross = group_sums([col_sum(flow), col_sum(flow * normed)], matrix)
    return scale * (flow - mask * (plain / entries + normed * (cross / entries)))


def mask_of(bucket_ref, core):
    row = lax.broadcasted_iota(jnp.int32, (CELLS, C), 0)
    inside = (row // SIDE < bucket_ref[core, 0]) & (row % SIDE < bucket_ref[core, 1])
    return inside.astype(F32)


def entries_of(bucket_ref, core):
    return (bucket_ref[core, 0] * bucket_ref[core, 1] * (C // G)).astype(F32)


class Setup:
    def __init__(self, core, bucket, embedding, time_ref, matrix):
        self.core = core
        self.column = column_index()
        self.mask = mask_of(bucket, core)
        self.entries = entries_of(bucket, core)
        self.matrix = matrix[...]
        self.embedding = embedding
        self.time_ref = time_ref

    def temb(self, k, side):
        rows = jnp.dot(self.embedding[...], self.time_ref[k, side], preferred_element_type=F32)
        at = lax.broadcasted_iota(jnp.int32, rows.shape, 0)
        return col_sum(jnp.where(at == self.core, rows, 0.0))


def fetch_pair(core, own, other, target, sems):
    copies = [
        pltpu.make_async_copy(own, target.at[core], sems.at[0]),
        pltpu.make_async_copy(other, target.at[1 - core], sems.at[1]),
    ]
    for copy in copies:
        copy.start()
    return copies


def wait_all(*groups):
    for copies in groups:
        for copy in copies:
            copy.wait()


def forward_block(setup, values, k, side, kernel, padded, out):
    normed_ref, scale_ref, hidden_ref = out
    normed, scale, hidden = norm_hidden(
        values, setup.mask, setup.temb(k, side), setup.entries, setup.matrix
    )
    normed_ref[k] = normed
    scale_ref[k] = jnp.broadcast_to(scale, (8, C))
    hidden_ref[k] = hidden.astype(BF16)
    if kernel is None:
        return None
    store_windows(padded, hidden, setup.column)
    return ((values + conv(padded, kernel)) * setup.mask).astype(BF16)


def encoder_pair(setup, value, w_enc, padded, out, inputs_ref):
    def block(k, value):
        inputs_ref[k] = value
        return forward_block(setup, value.astype(F32), k, 0, w_enc.at[k], padded, out)

    return lax.fori_loop(0, 2, block, value)


def decoder_pair(setup, value, w_dec, padded, out, inputs_ref, last):
    def block(step, value, conv_too=True):
        k = 1 - step
        summed = value.astype(F32) + inputs_ref[k].astype(F32)
        kernel = w_dec.at[k] if conv_too else None
        return forward_block(setup, summed, k, 1, kernel, padded, out)

    if last:
        return lax.fori_loop(0, 2, block, value)
    return block(1, block(0, value), conv_too=False)


def backward_pair(setup, value, side, upward, kernels, padded_cot, kept, cot_ref, skips, skip_in, last):
    normed_ref, scale_ref = kept

    def masked(k, value):
        residual = value.astype(F32) * setup.mask
        conv_cot = residual.astype(BF16)
        cot_ref[k] = conv_cot
        return residual, conv_cot

    def block(step, value):
        k = step if upward else 1 - step
        residual, conv_cot = masked(k, value)
        padded_cot[SIDE : SIDE + CELLS, :] = conv_cot
        hidden_cot = conv_back(padded_cot, kernels.at[k], setup.column)
        total = residual + norm_back(
            hidden_cot, normed_ref[k], scale_ref[k, 0:1], setup.temb(k, side), setup.mask,
            setup.entries, setup.matrix,
        )
        if skip_in is not None:
            total = total + skip_in[k].astype(F32)
        value = total.astype(BF16)
        if skips is not None:
            skips[k] = value
        return value

    if last:
        return lax.fori_loop(0, 2, block, value)
    masked(1 if upward else 0, block(0, value))
    return None


def phase_one(
    where, bucket, latents, time_own, time_other, enc_own, enc_other, emb, matrix,
    normed, scale, hidden, kept, sent, x, time_ref, w_enc, padded, sems,
):
    core = where[1]
    enc_copies = fetch_pair(core, enc_own, enc_other, w_enc, sems.at[0])
    time_copies = fetch_pair(core, time_own, time_other, time_ref, sems.at[1])
    x_copy = pltpu.make_async_copy(latents.at[core], x, sems.at[2, 0])
    x_copy.start()
    clear_edges(padded)
    wait_all([x_copy], time_copies, enc_copies)
    setup = Setup(core, bucket, emb, time_ref, matrix)
    sent[...] = encoder_pair(setup, x[...], w_enc, padded, (normed, scale, hidden), kept)


def phase_two(
    where, bucket, x, time_own, time_other, enc_own, enc_other, dec_own, dec_other, emb, matrix,
    e_normed, e_scale, e_hidden, d_normed, d_scale, d_hidden, sent,
    kept, time_ref, w_enc, w_dec, padded, sems,
):
    core = where[1]
    time_copies = fetch_pair(core, time_own, time_other, time_ref, sems.at[1])
    enc_copies = fetch_pair(core, enc_own, enc_other, w_enc, sems.at[0])
    dec_copies = fetch_pair(core, dec_own, dec_other, w_dec, sems.at[2])
    clear_edges(padded)
    wait_all(time_copies, enc_copies)
    setup = Setup(core, bucket, emb, time_ref, matrix)
    upper = encoder_pair(setup, x[...], w_enc, padded, (e_normed, e_scale, e_hidden), kept)
    wait_all(dec_copies)
    sent[...] = decoder_pair(
        setup, upper, w_dec, padded, (d_normed, d_scale, d_hidden), kept, True
    )


def phase_three(
    scaling, where, bucket, x, cotangent, time_own, time_other, dec_own, dec_other, kept, emb,
    matrix, d_hidden, cots, skips, sent,
    d_normed, d_scale, start, time_ref, w_dec, padded, padded_cot, sems,
):
    core = where[1]
    time_copies = fetch_pair(core, time_own, time_other, time_ref, sems.at[1])
    dec_copies = fetch_pair(core, dec_own, dec_other, w_dec, sems.at[0])
    start_copy = pltpu.make_async_copy(cotangent.at[core], start, sems.at[2, 0])
    start_copy.start()
    clear_edges(padded)
    clear_edges(padded_cot)
    wait_all(time_copies, dec_copies, [start_copy])
    setup = Setup(core, bucket, emb, time_ref, matrix)
    decoder_pair(setup, x[...], w_dec, padded, (d_normed, d_scale, d_hidden), kept, False)
    cot = (start[...].astype(F32) * scaling).astype(BF16)
    sent[...] = backward_pair(
        setup, cot, 1, True, w_dec, padded_cot, (d_normed, d_scale), cots, skips, None, True
    )


def phase_four(
    where, bucket, x, time_own, time_other, enc_own, enc_other, dec_own, dec_other, emb, matrix,
    d_normed, d_scale, e_normed, e_scale, d_cots, e_cots, sent,
    skips, time_ref, w_enc, w_dec, padded_cot, sems,
):
    core = where[1]
    time_copies = fetch_pair(core, time_own, time_other, time_ref, sems.at[1])
    dec_copies = fetch_pair(core, dec_own, dec_other, w_dec, sems.at[0])
    enc_copies = fetch_pair(core, enc_own, enc_other, w_enc, sems.at[2])
    clear_edges(padded_cot)
    wait_all(time_copies, dec_copies)
    setup = Setup(core, bucket, emb, time_ref, matrix)
    cot = backward_pair(
        setup, x[...], 1, True, w_dec, padded_cot, (d_normed, d_scale), d_cots, skips, None, True
    )
    wait_all(enc_copies)
    sent[...] = backward_pair(
        setup, cot, 0, False, w_enc, padded_cot, (e_normed, e_scale), e_cots, None, skips, True
    )


def store_packed(target, slot, row, values):
    first = row * TAPS
    target[slot, first : first + TAPS, :] = values[:, 0:LANES]
    target[slot, FLAT + first : FLAT + first + TAPS, :] = values[:, LANES : 2 * LANES]
    half = FLAT // 2
    pieces = ((0, TAPS // 2), (TAPS // 2, TAPS)) if row == 1 else ((0, TAPS),)
    for begin, end in pieces:
        side = 0 if first + end <= half else 1
        at = 2 * FLAT + first + begin - side * half
        target[slot, at : at + end - begin, side * TAIL : (side + 1) * TAIL] = values[
            begin:end, 2 * LANES : C
        ]


def store_gradients(core, hidden, cots, own, other, padded_cot, turned, pair):
    column = column_index()
    pair[:, PACKED_USED:, :] = jnp.zeros((2, PACKED - PACKED_USED, LANES), F32)

    def section(k, carry):
        values = hidden[k].astype(F32)
        padded_cot[SIDE : SIDE + CELLS, :] = cots[k]
        turned[0:C, :] = shift_right(values, column).T.astype(BF16)
        turned[C : 2 * C, :] = values.T.astype(BF16)
        turned[2 * C : 3 * C, :] = shift_left(values, column).T.astype(BF16)
        for row in range(3):
            part = jnp.dot(
                turned[...],
                padded_cot[(2 - row) * SIDE : (2 - row) * SIDE + CELLS, :],
                preferred_element_type=F32,
            )
            store_packed(pair, jnp.where(core == k, 0, 1), row, part)
        return carry

    lax.fori_loop(0, 2, section, 0)

    def copy(step, carry):
        begin = pl.multiple_of(step * STRIP, STRIP)
        own[pl.ds(begin, STRIP), :] = pair[0, pl.ds(begin, STRIP), :]
        other[pl.ds(begin, STRIP), :] = pair[1, pl.ds(begin, STRIP), :].astype(BF16)
        return carry

    lax.fori_loop(0, PACKED // STRIP, copy, 0)


def weight_phase(
    where, a_hidden, a_cots, b_hidden, b_cots, own, other, padded_cot, turned, pair, hidden, cots
):
    clear_edges(padded_cot)

    @pl.when(where[0] == 0)
    def _():
        hidden[...] = a_hidden[...]
        cots[...] = a_cots[...]

    @pl.when(where[0] != 0)
    def _():
        hidden[...] = b_hidden[...]
        cots[...] = b_cots[...]

    store_gradients(where[1], hidden, cots, own, other, padded_cot, turned, pair)


def phase_five(
    where, bucket, x, time_own, time_other, enc_own, enc_other, skips, emb, matrix,
    e_normed, e_scale, a_hidden, b_hidden, b_cots,
    own, other, padded_cot, turned, pair, hidden, cots, time_ref, w_enc, sems,
):
    clear_edges(padded_cot)
    core = where[1]
    time_copies = fetch_pair(core, time_own, time_other, time_ref, sems.at[1])
    enc_copies = fetch_pair(core, enc_own, enc_other, w_enc, sems.at[0])
    wait_all(time_copies, enc_copies)

    @pl.when(where[0] == 0)
    def _():
        hidden[...] = a_hidden[...]
        setup = Setup(core, bucket, emb, time_ref, matrix)
        backward_pair(
            setup, x[...], 0, False, w_enc, padded_cot, (e_normed, e_scale), cots, None, skips,
            False,
        )

    @pl.when(where[0] != 0)
    def _():
        hidden[...] = b_hidden[...]
        cots[...] = b_cots[...]

    store_gradients(core, hidden, cots, own, other, padded_cot, turned, pair)


def core_add(first, first_other, second, second_other, out):
    rows = out.shape[1] // 2

    def part(at, carry):
        source = pl.ds(pl.multiple_of(at * rows, 16), rows)
        out[at, 0:rows] = (first[source, :] + first_other[source, :].astype(F32)).astype(BF16)
        out[at, rows:] = (second[source, :] + second_other[source, :].astype(F32)).astype(BF16)
        return carry

    lax.fori_loop(0, out.shape[0], part, 0)


def added(parts):
    value = parts[0].astype(F32)
    for at in range(1, parts.shape[0]):
        value = value + parts[at].astype(F32)
    return value


def block_sums(parts, out):
    rows = out.shape[2]
    value = added(parts)
    for which in range(2):
        for layer in range(out.shape[0]):
            begin = (which * out.shape[0] + layer) * rows
            out[layer, which] = value[begin : begin + rows].astype(BF16)


def layer_sums(parts, out):
    value = added(parts).astype(BF16)
    for layer in range(out.shape[0]):
        out[layer] = value


def assemble(parts, out, total):
    layers, _, rows, _ = parts.shape
    for which in range(2):
        for layer in range(layers):
            begin = (which * layers + layer) * rows
            total[begin : begin + rows, :] = parts[layer, which].astype(F32)
    value = total[...].astype(BF16)
    for at in range(out.shape[0]):
        out[at] = value


def unpack(packed, first, second):
    rows = packed.shape[1] // 2
    size = 2 * STRIP
    half = FLAT // 2

    def strip(step, carry):
        for which, grad in enumerate((first, second)):

            def source(begin, which=which):
                begin = begin + step * size
                at = pl.multiple_of(which * rows + lax.rem(begin, rows), 16)
                return packed[lax.div(begin, rows), pl.ds(at, size), :].astype(F32)

            tail = source(2 * FLAT)
            for side in range(2):
                to = pl.ds(pl.multiple_of(step * size + side * half, 16), size)
                grad[to, 0:LANES] = source(side * half)
                grad[to, LANES : 2 * LANES] = source(FLAT + side * half)
                grad[to, 2 * LANES : C] = tail[:, side * TAIL : (side + 1) * TAIL]
        return carry

    lax.fori_loop(0, half // size, strip, 0)


def shape(dims, dtype):
    return jax.ShapeDtypeStruct(dims, dtype)


NORMED = ((2, CELLS, C), F32)
SCALE = ((2, 8, C), F32)
ACTS = ((2, CELLS, C), BF16)
ONE = ((CELLS, C), BF16)
PADDED = pltpu.VMEM((CELLS + 2 * SIDE, TAPS), BF16)
PADDED_COT = pltpu.VMEM((CELLS + 2 * SIDE, C), BF16)
TURNED = pltpu.VMEM((TAPS, CELLS), BF16)
OWN = ((PACKED, LANES), F32)
OTHER = ((PACKED, LANES), BF16)
WEIGHTS = pltpu.VMEM((2, 9, C, C), BF16)
TIMES = pltpu.VMEM((2, 2, C, C), BF16)
SEMS = pltpu.SemaphoreType.DMA((3, 2))


def call(body, spaces, outs, scratch, flops, name, vmem=VMEM_LIMIT):
    def run(*args):
        kinds = {"s": pltpu.SMEM, "h": pltpu.HBM, "v": pltpu.VMEM}
        moved = sum(a.size * a.dtype.itemsize for a in args) + sum(
            math.prod(d) * jnp.dtype(t).itemsize for d, t in outs
        )
        return pl.pallas_call(
            body,
            out_shape=tuple(shape(d, t) for d, t in outs),
            in_specs=[pl.BlockSpec(memory_space=kinds[space]) for space in spaces],
            out_specs=tuple(pl.BlockSpec(memory_space=pltpu.VMEM) for _ in outs),
            scratch_shapes=list(scratch),
            compiler_params=pltpu.CompilerParams(vmem_limit_bytes=vmem),
            cost_estimate=pl.CostEstimate(flops=flops, bytes_accessed=moved, transcendentals=0),
            name=name,
        )(*args)

    return run


CONV = 2 * CELLS * 9 * C * C


def time_embed(timesteps):
    half_width = C // 2
    frequencies = jnp.exp(
        -math.log(10000.0) * jnp.arange(half_width, dtype=F32) / half_width
    )
    angles = timesteps.astype(F32)[:, None] * frequencies[None, :]
    return jnp.concatenate([jnp.cos(angles), jnp.sin(angles)], axis=1).astype(BF16)


def to_other_core(array):
    return lax.ppermute(array, "core", [(0, 1), (1, 0)])


BLOCK = ("z_low", "y")
LAYERS = ("z_high", "far")
DP = ("z_high", "z_low", "far", "y")


def exchange(parts, axes):
    return lax.all_to_all(parts, axes, split_axis=0, concat_axis=0, tiled=True)


def gradients(first, second):
    count, layers = lax.axis_size(BLOCK), lax.axis_size(LAYERS)
    rows = PACKED // count
    (pair,) = call(
        core_add, "vvvv", [((count, 2 * rows, LANES), BF16)], [], 2 * PACKED * LANES, "core_add"
    )(*first, *second)
    cut = ((layers, 2, rows // layers, LANES), BF16)
    (sums,) = call(block_sums, "v", [cut], [], 2 * PACKED * LANES, "block_sums")(
        exchange(pair, BLOCK)
    )
    (sums,) = call(layer_sums, "v", [cut], [], 2 * rows * LANES, "layer_sums")(
        exchange(sums, LAYERS)
    )
    (copies,) = call(
        assemble, "v", [((count, 2 * rows, LANES), BF16)], [pltpu.VMEM((2 * rows, LANES), F32)],
        2 * PACKED * LANES, "assemble",
    )(exchange(sums, LAYERS))
    grads = call(unpack, "v", [((FLAT, C), F32)] * 2, [], 2 * PACKED * LANES, "unpack")(
        exchange(copies, BLOCK)
    )
    return tuple(grad.reshape(1, 3, 3, C, C) for grad in grads)


def local(latents, cotangent, bucket, timesteps, w_enc, w_dec, w_time):
    where = jnp.stack([lax.axis_index(axis) for axis in ("near", "core")])
    where = where.astype(jnp.int32)
    micro_count = latents.shape[0]
    loss_scale = float(micro_count * lax.axis_size(DP) * CELLS) ** (-0.5)

    enc = w_enc.reshape(9, C, C)
    dec = w_dec.reshape(9, C, C)
    times = w_time.reshape(2, C, C)
    times = (times, to_other_core(times))
    enc = (enc, to_other_core(enc))
    emb = jnp.pad(time_embed(timesteps), ((0, 16 - micro_count), (0, 0)))
    dec, enc, times, emb, where = lax.optimization_barrier((dec, enc, times, emb, where))
    dec = (dec, to_other_core(dec))
    latents = latents.reshape(micro_count, CELLS, C)
    cotangent = cotangent.reshape(micro_count, CELLS, C)
    matrix = group_matrix()

    def up(value):
        return lax.ppermute(value, "near", [(0, 1)])

    def down(value):
        return lax.ppermute(value, "near", [(1, 0)])

    one = call(
        phase_one, "ss" + "h" * 5 + "vv", [NORMED, SCALE, ACTS, ACTS, ONE],
        [pltpu.VMEM(*ONE), TIMES, WEIGHTS, PADDED, SEMS], 2 * CONV, "one",
    )
    a_normed, a_scale, a_hidden, a_kept, sent = one(
        where, bucket, latents, *times, *enc, emb, matrix
    )
    two = call(
        phase_two, "ssv" + "h" * 6 + "vv", [NORMED, SCALE, ACTS, NORMED, SCALE, ACTS, ONE],
        [pltpu.VMEM(*ACTS), TIMES, WEIGHTS, WEIGHTS, PADDED, SEMS], 4 * CONV, "two",
    )
    be_normed, be_scale, be_hidden, bd_normed, bd_scale, bd_hidden, sent = two(
        where, bucket, up(sent), *times, *enc, *dec, emb, matrix
    )
    three = call(
        functools.partial(phase_three, loss_scale), "ssv" + "h" * 5 + "vvv",
        [ACTS, ACTS, ACTS, ONE],
        [
            pltpu.VMEM(*NORMED), pltpu.VMEM(*SCALE), pltpu.VMEM(*ONE), TIMES, WEIGHTS, PADDED,
            PADDED_COT, SEMS,
        ],
        3 * CONV, "three",
    )
    ad_hidden, ad_cots, a_skips, sent = three(
        where, bucket, down(sent), cotangent, *times, *dec, a_kept, emb, matrix
    )
    four = call(
        phase_four, "ssv" + "h" * 6 + "v" * 6, [ACTS, ACTS, ONE],
        [pltpu.VMEM(*ACTS), TIMES, WEIGHTS, WEIGHTS, PADDED_COT, SEMS], 4 * CONV, "four",
    )
    bd_cots, be_cots, sent = four(
        where, bucket, up(sent), *times, *enc, *dec, emb, matrix,
        bd_normed, bd_scale, be_normed, be_scale,
    )
    received = down(sent)
    work = [PADDED_COT, TURNED, pltpu.VMEM((2, PACKED, LANES), F32), pltpu.VMEM(*ACTS), pltpu.VMEM(*ACTS)]
    weights = call(weight_phase, "svvvv", [OWN, OTHER], work, 2 * CONV, "weights")
    own_dec, other_dec = weights(where, ad_hidden, ad_cots, bd_hidden, bd_cots)
    dec_pair = (own_dec, to_other_core(other_dec))
    five = call(
        phase_five, "ssv" + "h" * 4 + "v" * 8, [OWN, OTHER], [*work, TIMES, WEIGHTS, SEMS],
        3 * CONV, "five",
    )
    own_enc, other_enc = five(
        where, bucket, received, *times, *enc, a_skips, emb, matrix, a_normed, a_scale, a_hidden,
        be_hidden, be_cots,
    )

    return gradients((own_enc, to_other_core(other_enc)), dec_pair)


def solution(mesh):
    segments, dp = mesh.shape["segment"], mesh.shape["dp"]
    near, far, rows = segments // 2, 2, 4
    split = Mesh(
        mesh.devices.reshape(near, 2, dp // (2 * far * rows), 2, far, rows),
        ("near", "core", *DP),
    )
    section, micro = ("near", "core"), DP
    placed = (
        P(micro, None, None, None),
        P(micro, None, None, None),
        P(micro, None),
        P(micro),
        P(section, None, None, None, None),
        P(section, None, None, None, None),
        P(section, None, None, None),
    )
    grads = P(section, None, None, None, None)
    return jax.shard_map(
        local, mesh=split, in_specs=placed, out_specs=(grads, grads), check_vma=False
    )
```

```python
import functools
import math

import jax
import jax.numpy as jnp
import numpy as np
from jax import lax
from jax.experimental import pallas as pl
from jax.experimental.pallas import tpu as pltpu
from jax.sharding import Mesh, PartitionSpec as P

G = 32
SIDE = 16
CELLS = SIDE * SIDE
C = 320
TAPS = 3 * C
F32 = jnp.float32
BF16 = jnp.bfloat16
VMEM_LIMIT = 30 * 1024 * 1024
ALL_VMEM = 60 * 1024 * 1024
LANES = 128
FLAT = 9 * C
TAIL = C - 2 * LANES
PACKED_USED = 2 * FLAT + FLAT // 2
PACKED = 64 * 120
STRIP = 240

NT = (((1,), (1,)), ((), ()))


def group_matrix():
    index = np.arange(C) // (C // G)
    return jnp.asarray((index[:, None] == index[None, :]).astype(np.float32), BF16)


def group_sums(columns, matrix):
    row = lax.broadcasted_iota(jnp.int32, (16, C), 0)
    stacked = jnp.zeros((16, C), F32)
    for at, column in enumerate(columns):
        high = column.astype(BF16).astype(F32)
        rest = column - high
        middle = rest.astype(BF16).astype(F32)
        low = (rest - middle).astype(BF16).astype(F32)
        for part, value in enumerate((high, middle, low)):
            stacked = jnp.where(row == 3 * at + part, value, stacked)
    sums = jnp.dot(stacked.astype(BF16), matrix, preferred_element_type=F32)
    return [
        sums[3 * at : 3 * at + 1] + sums[3 * at + 1 : 3 * at + 2] + sums[3 * at + 2 : 3 * at + 3]
        for at in range(len(columns))
    ]


def col_sum(values):
    return jnp.sum(values, axis=0, keepdims=True)


def column_index():
    return lax.broadcasted_iota(jnp.int32, (CELLS, C), 0) % SIDE


def shift_right(values, column):
    return jnp.where(column == 0, 0.0, pltpu.roll(values, 1, axis=0))


def shift_left(values, column):
    return jnp.where(column == SIDE - 1, 0.0, pltpu.roll(values, CELLS - 1, axis=0))


def clear_edges(padded):
    width = padded.shape[1]
    padded[0:SIDE, :] = jnp.zeros((SIDE, width), BF16)
    padded[SIDE + CELLS :, :] = jnp.zeros((SIDE, width), BF16)


def store_windows(padded, hidden, column):
    padded[SIDE : SIDE + CELLS, 0:C] = shift_right(hidden, column).astype(BF16)
    padded[SIDE : SIDE + CELLS, C : 2 * C] = hidden.astype(BF16)
    padded[SIDE : SIDE + CELLS, 2 * C : 3 * C] = shift_left(hidden, column).astype(BF16)


def norm_hidden(values, mask, temb, entries, matrix):
    mean = group_sums([col_sum(values * mask)], matrix)[0] / entries
    centered = values - mean
    variance = group_sums([col_sum(centered * centered * mask)], matrix)[0] / entries
    scale = lax.rsqrt(variance + 1e-05)
    normed = centered * scale
    shifted = normed + temb
    hidden = shifted / (1.0 + jnp.exp(-shifted)) * mask
    return normed, scale, hidden


def taps(kernel, row):
    return kernel[3 * row : 3 * row + 3].reshape(TAPS, C)


def conv(padded, kernel):
    total = None
    for row in range(3):
        part = jnp.dot(
            padded[row * SIDE : row * SIDE + CELLS, :], taps(kernel, row), preferred_element_type=F32
        )
        total = part if total is None else total + part
    return total


def conv_back(cot_padded, kernel, column):
    total = None
    for row in range(3):
        part = lax.dot_general(
            cot_padded[(2 - row) * SIDE : (2 - row) * SIDE + CELLS, :],
            taps(kernel, row),
            NT,
            preferred_element_type=F32,
        )
        total = part if total is None else total + part
    left, middle, right = total[:, 0:C], total[:, C : 2 * C], total[:, 2 * C : 3 * C]
    return shift_left(left, column) + middle + shift_right(right, column)


def norm_back(hidden_cot, normed, scale, temb, mask, entries, matrix):
    shifted = normed + temb
    gate = 1.0 / (1.0 + jnp.exp(-shifted))
    flow = hidden_cot * mask * (gate * (1.0 + shifted * (1.0 - gate)))
    plain, cross = group_sums([col_sum(flow), col_sum(flow * normed)], matrix)
    return scale * (flow - mask * (plain / entries + normed * (cross / entries)))


def mask_of(bucket_ref, core):
    row = lax.broadcasted_iota(jnp.int32, (CELLS, C), 0)
    inside = (row // SIDE < bucket_ref[core, 0]) & (row % SIDE < bucket_ref[core, 1])
    return inside.astype(F32)


def entries_of(bucket_ref, core):
    return (bucket_ref[core, 0] * bucket_ref[core, 1] * (C // G)).astype(F32)


class Setup:
    def __init__(self, core, bucket, embedding, time_ref, matrix):
        self.core = core
        self.column = column_index()
        self.mask = mask_of(bucket, core)
        self.entries = entries_of(bucket, core)
        self.matrix = matrix[...]
        self.embedding = embedding
        self.time_ref = time_ref

    def temb(self, k, side):
        rows = jnp.dot(self.embedding[...], self.time_ref[k, side], preferred_element_type=F32)
        at = lax.broadcasted_iota(jnp.int32, rows.shape, 0)
        return col_sum(jnp.where(at == self.core, rows, 0.0))


def fetch_pair(core, own, other, target, sems):
    copies = [
        pltpu.make_async_copy(own, target.at[core], sems.at[0]),
        pltpu.make_async_copy(other, target.at[1 - core], sems.at[1]),
    ]
    for copy in copies:
        copy.start()
    return copies


def wait_all(*groups):
    for copies in groups:
        for copy in copies:
            copy.wait()


def forward_block(setup, values, k, side, kernel, padded, out):
    normed_ref, scale_ref, hidden_ref = out
    normed, scale, hidden = norm_hidden(
        values, setup.mask, setup.temb(k, side), setup.entries, setup.matrix
    )
    normed_ref[k] = normed
    scale_ref[k] = jnp.broadcast_to(scale, (8, C))
    hidden_ref[k] = hidden.astype(BF16)
    if kernel is None:
        return None
    store_windows(padded, hidden, setup.column)
    return ((values + conv(padded, kernel)) * setup.mask).astype(BF16)


def encoder_pair(setup, value, w_enc, padded, out, inputs_ref):
    def block(k, value):
        inputs_ref[k] = value
        return forward_block(setup, value.astype(F32), k, 0, w_enc.at[k], padded, out)

    return lax.fori_loop(0, 2, block, value)


def decoder_pair(setup, value, w_dec, padded, out, inputs_ref, last):
    def block(step, value, conv_too=True):
        k = 1 - step
        summed = value.astype(F32) + inputs_ref[k].astype(F32)
        kernel = w_dec.at[k] if conv_too else None
        return forward_block(setup, summed, k, 1, kernel, padded, out)

    if last:
        return lax.fori_loop(0, 2, block, value)
    return block(1, block(0, value), conv_too=False)


def backward_pair(setup, value, side, upward, kernels, padded_cot, kept, cot_ref, skips, skip_in, last):
    normed_ref, scale_ref = kept

    def masked(k, value):
        residual = value.astype(F32) * setup.mask
        conv_cot = residual.astype(BF16)
        cot_ref[k] = conv_cot
        return residual, conv_cot

    def block(step, value):
        k = step if upward else 1 - step
        residual, conv_cot = masked(k, value)
        padded_cot[SIDE : SIDE + CELLS, :] = conv_cot
        hidden_cot = conv_back(padded_cot, kernels.at[k], setup.column)
        total = residual + norm_back(
            hidden_cot, normed_ref[k], scale_ref[k, 0:1], setup.temb(k, side), setup.mask,
            setup.entries, setup.matrix,
        )
        if skip_in is not None:
            total = total + skip_in[k].astype(F32)
        value = total.astype(BF16)
        if skips is not None:
            skips[k] = value
        return value

    if last:
        return lax.fori_loop(0, 2, block, value)
    masked(1 if upward else 0, block(0, value))
    return None


def phase_one(
    where, bucket, latents, time_own, time_other, enc_own, enc_other, emb, matrix,
    normed, scale, hidden, kept, sent, x, time_ref, w_enc, padded, sems,
):
    core = where[1]
    enc_copies = fetch_pair(core, enc_own, enc_other, w_enc, sems.at[0])
    time_copies = fetch_pair(core, time_own, time_other, time_ref, sems.at[1])
    x_copy = pltpu.make_async_copy(latents.at[core], x, sems.at[2, 0])
    x_copy.start()
    clear_edges(padded)
    wait_all([x_copy], time_copies, enc_copies)
    setup = Setup(core, bucket, emb, time_ref, matrix)
    sent[...] = encoder_pair(setup, x[...], w_enc, padded, (normed, scale, hidden), kept)


def phase_two(
    where, bucket, x, time_own, time_other, enc_own, enc_other, dec_own, dec_other, emb, matrix,
    e_normed, e_scale, e_hidden, d_normed, d_scale, d_hidden, sent,
    kept, time_ref, w_enc, w_dec, padded, sems,
):
    core = where[1]
    time_copies = fetch_pair(core, time_own, time_other, time_ref, sems.at[1])
    enc_copies = fetch_pair(core, enc_own, enc_other, w_enc, sems.at[0])
    dec_copies = fetch_pair(core, dec_own, dec_other, w_dec, sems.at[2])
    clear_edges(padded)
    wait_all(time_copies, enc_copies)
    setup = Setup(core, bucket, emb, time_ref, matrix)
    upper = encoder_pair(setup, x[...], w_enc, padded, (e_normed, e_scale, e_hidden), kept)
    wait_all(dec_copies)
    sent[...] = decoder_pair(
        setup, upper, w_dec, padded, (d_normed, d_scale, d_hidden), kept, True
    )


def phase_three(
    scaling, where, bucket, x, cotangent, time_own, time_other, dec_own, dec_other, kept, emb,
    matrix, d_hidden, cots, skips, sent,
    d_normed, d_scale, start, time_ref, w_dec, padded, padded_cot, sems,
):
    core = where[1]
    time_copies = fetch_pair(core, time_own, time_other, time_ref, sems.at[1])
    dec_copies = fetch_pair(core, dec_own, dec_other, w_dec, sems.at[0])
    start_copy = pltpu.make_async_copy(cotangent.at[core], start, sems.at[2, 0])
    start_copy.start()
    clear_edges(padded)
    clear_edges(padded_cot)
    wait_all(time_copies, dec_copies, [start_copy])
    setup = Setup(core, bucket, emb, time_ref, matrix)
    decoder_pair(setup, x[...], w_dec, padded, (d_normed, d_scale, d_hidden), kept, False)
    cot = (start[...].astype(F32) * scaling).astype(BF16)
    sent[...] = backward_pair(
        setup, cot, 1, True, w_dec, padded_cot, (d_normed, d_scale), cots, skips, None, True
    )


def phase_four(
    where, bucket, x, time_own, time_other, enc_own, enc_other, dec_own, dec_other, emb, matrix,
    d_normed, d_scale, e_normed, e_scale, d_cots, e_cots, sent,
    skips, time_ref, w_enc, w_dec, padded_cot, sems,
):
    core = where[1]
    time_copies = fetch_pair(core, time_own, time_other, time_ref, sems.at[1])
    dec_copies = fetch_pair(core, dec_own, dec_other, w_dec, sems.at[0])
    enc_copies = fetch_pair(core, enc_own, enc_other, w_enc, sems.at[2])
    clear_edges(padded_cot)
    wait_all(time_copies, dec_copies)
    setup = Setup(core, bucket, emb, time_ref, matrix)
    cot = backward_pair(
        setup, x[...], 1, True, w_dec, padded_cot, (d_normed, d_scale), d_cots, skips, None, True
    )
    wait_all(enc_copies)
    sent[...] = backward_pair(
        setup, cot, 0, False, w_enc, padded_cot, (e_normed, e_scale), e_cots, None, skips, True
    )


def store_packed(target, slot, row, values):
    first = row * TAPS
    target[slot, first : first + TAPS, :] = values[:, 0:LANES]
    target[slot, FLAT + first : FLAT + first + TAPS, :] = values[:, LANES : 2 * LANES]
    half = FLAT // 2
    pieces = ((0, TAPS // 2), (TAPS // 2, TAPS)) if row == 1 else ((0, TAPS),)
    for begin, end in pieces:
        side = 0 if first + end <= half else 1
        at = 2 * FLAT + first + begin - side * half
        target[slot, at : at + end - begin, side * TAIL : (side + 1) * TAIL] = values[
            begin:end, 2 * LANES : C
        ]


def store_gradients(core, hidden, cots, own, other, padded_cot, turned, pair):
    column = column_index()
    pair[:, PACKED_USED:, :] = jnp.zeros((2, PACKED - PACKED_USED, LANES), F32)

    def section(k, carry):
        values = hidden[k].astype(F32)
        padded_cot[SIDE : SIDE + CELLS, :] = cots[k]
        turned[0:C, :] = shift_right(values, column).T.astype(BF16)
        turned[C : 2 * C, :] = values.T.astype(BF16)
        turned[2 * C : 3 * C, :] = shift_left(values, column).T.astype(BF16)
        for row in range(3):
            part = jnp.dot(
                turned[...],
                padded_cot[(2 - row) * SIDE : (2 - row) * SIDE + CELLS, :],
                preferred_element_type=F32,
            )
            store_packed(pair, jnp.where(core == k, 0, 1), row, part)
        return carry

    lax.fori_loop(0, 2, section, 0)

    def copy(step, carry):
        begin = pl.multiple_of(step * STRIP, STRIP)
        own[pl.ds(begin, STRIP), :] = pair[0, pl.ds(begin, STRIP), :]
        other[pl.ds(begin, STRIP), :] = pair[1, pl.ds(begin, STRIP), :].astype(BF16)
        return carry

    lax.fori_loop(0, PACKED // STRIP, copy, 0)


def weight_phase(
    where, a_hidden, a_cots, b_hidden, b_cots, own, other, padded_cot, turned, pair, hidden, cots
):
    clear_edges(padded_cot)

    @pl.when(where[0] == 0)
    def _():
        hidden[...] = a_hidden[...]
        cots[...] = a_cots[...]

    @pl.when(where[0] != 0)
    def _():
        hidden[...] = b_hidden[...]
        cots[...] = b_cots[...]

    store_gradients(where[1], hidden, cots, own, other, padded_cot, turned, pair)


def phase_five(
    where, bucket, x, time_own, time_other, enc_own, enc_other, skips, emb, matrix,
    e_normed, e_scale, a_hidden, b_hidden, b_cots,
    own, other, padded_cot, turned, pair, hidden, cots, time_ref, w_enc, sems,
):
    clear_edges(padded_cot)
    core = where[1]
    time_copies = fetch_pair(core, time_own, time_other, time_ref, sems.at[1])
    enc_copies = fetch_pair(core, enc_own, enc_other, w_enc, sems.at[0])
    wait_all(time_copies, enc_copies)

    @pl.when(where[0] == 0)
    def _():
        hidden[...] = a_hidden[...]
        setup = Setup(core, bucket, emb, time_ref, matrix)
        backward_pair(
            setup, x[...], 0, False, w_enc, padded_cot, (e_normed, e_scale), cots, None, skips,
            False,
        )

    @pl.when(where[0] != 0)
    def _():
        hidden[...] = b_hidden[...]
        cots[...] = b_cots[...]

    store_gradients(core, hidden, cots, own, other, padded_cot, turned, pair)


def core_add(first, first_other, second, second_other, out):
    rows = out.shape[1] // 2

    def part(at, carry):
        source = pl.ds(pl.multiple_of(at * rows, 16), rows)
        out[at, 0:rows] = (first[source, :] + first_other[source, :].astype(F32)).astype(BF16)
        out[at, rows:] = (second[source, :] + second_other[source, :].astype(F32)).astype(BF16)
        return carry

    lax.fori_loop(0, out.shape[0], part, 0)


def added(parts):
    value = parts[0].astype(F32)
    for at in range(1, parts.shape[0]):
        value = value + parts[at].astype(F32)
    return value


def block_sums(where, parts, kept, *rest):
    *chunks, total = rest
    layers = len(chunks) + 1
    rows = kept.shape[1]
    total[...] = added(parts)
    for which in range(2):
        for ahead in range(layers):
            at = which * layers + lax.rem(where[2] + ahead, layers)
            value = total[pl.ds(pl.multiple_of(at * rows, 8), rows), :]
            if ahead == 0:
                kept[which] = value
            else:
                chunks[ahead - 1][which] = value.astype(BF16)


def layer_sums(kept, *rest):
    *received, out = rest
    value = kept[...]
    for part in received:
        value = value + part[...].astype(F32)
    out[...] = value.astype(BF16)


def assemble(where, *rest):
    *chunks, out, total = rest
    layers = len(chunks)
    rows = chunks[0].shape[1]
    for which in range(2):
        for behind, chunk in enumerate(chunks):
            at = which * layers + lax.rem(where[2] + layers - behind, layers)
            total[pl.ds(pl.multiple_of(at * rows, 8), rows), :] = chunk[which].astype(F32)
    value = total[...].astype(BF16)
    for at in range(out.shape[0]):
        out[at] = value


def unpack(packed, first, second):
    rows = packed.shape[1] // 2
    size = 2 * STRIP
    half = FLAT // 2

    step = pl.program_id(0)
    for which, grad in enumerate((first, second)):

        def source(begin, which=which):
            begin = begin + step * size
            at = pl.multiple_of(which * rows + lax.rem(begin, rows), 16)
            return packed[lax.div(begin, rows), pl.ds(at, size), :].astype(F32)

        tail = source(2 * FLAT)
        for side in range(2):
            grad[side, :, 0:LANES] = source(side * half)
            grad[side, :, LANES : 2 * LANES] = source(FLAT + side * half)
            grad[side, :, 2 * LANES : C] = tail[:, side * TAIL : (side + 1) * TAIL]


def shape(dims, dtype):
    return jax.ShapeDtypeStruct(dims, dtype)


NORMED = ((2, CELLS, C), F32)
SCALE = ((2, 8, C), F32)
ACTS = ((2, CELLS, C), BF16)
ONE = ((CELLS, C), BF16)
PADDED = pltpu.VMEM((CELLS + 2 * SIDE, TAPS), BF16)
PADDED_COT = pltpu.VMEM((CELLS + 2 * SIDE, C), BF16)
TURNED = pltpu.VMEM((TAPS, CELLS), BF16)
OWN = ((PACKED, LANES), F32)
OTHER = ((PACKED, LANES), BF16)
WEIGHTS = pltpu.VMEM((2, 9, C, C), BF16)
TIMES = pltpu.VMEM((2, 2, C, C), BF16)
SEMS = pltpu.SemaphoreType.DMA((3, 2))


def call(body, spaces, outs, scratch, flops, name, vmem=VMEM_LIMIT):
    def run(*args):
        kinds = {"s": pltpu.SMEM, "h": pltpu.HBM, "v": pltpu.VMEM}
        moved = sum(a.size * a.dtype.itemsize for a in args) + sum(
            math.prod(d) * jnp.dtype(t).itemsize for d, t in outs
        )
        return pl.pallas_call(
            body,
            out_shape=tuple(shape(d, t) for d, t in outs),
            in_specs=[pl.BlockSpec(memory_space=kinds[space]) for space in spaces],
            out_specs=tuple(pl.BlockSpec(memory_space=pltpu.VMEM) for _ in outs),
            scratch_shapes=list(scratch),
            compiler_params=pltpu.CompilerParams(vmem_limit_bytes=vmem),
            cost_estimate=pl.CostEstimate(flops=flops, bytes_accessed=moved, transcendentals=0),
            name=name,
        )(*args)

    return run


CONV = 2 * CELLS * 9 * C * C


def time_embed(timesteps):
    half_width = C // 2
    frequencies = jnp.exp(
        -math.log(10000.0) * jnp.arange(half_width, dtype=F32) / half_width
    )
    angles = timesteps.astype(F32)[:, None] * frequencies[None, :]
    return jnp.concatenate([jnp.cos(angles), jnp.sin(angles)], axis=1).astype(BF16)


def to_other_core(array):
    return lax.ppermute(array, "core", [(0, 1), (1, 0)])


BLOCK = ("z_low", "far", "y")
LAYERS = "z_high"
DP = (LAYERS, *BLOCK)


def exchange(parts, axes):
    return lax.all_to_all(parts, axes, split_axis=0, concat_axis=0, tiled=True)


def ahead(value, steps):
    count = lax.axis_size(LAYERS)
    return lax.ppermute(value, LAYERS, [(at, (at + steps) % count) for at in range(count)])


def gradients(where, first, second):
    count, layers = lax.axis_size(BLOCK), lax.axis_size(LAYERS)
    rows = PACKED // count
    (pair,) = call(
        core_add, "vvvv", [((count, 2 * rows, LANES), BF16)], [], 2 * PACKED * LANES, "core_add"
    )(*first, *second)
    cut = (2, rows // layers, LANES)
    total = [pltpu.VMEM((2 * rows, LANES), F32)]
    kept, *chunks = call(
        block_sums, "sv", [(cut, F32)] + [(cut, BF16)] * (layers - 1), total, 2 * PACKED * LANES,
        "block_sums",
    )(where, exchange(pair, BLOCK))
    received = [ahead(chunk, step + 1) for step, chunk in enumerate(chunks)]
    (mine,) = call(
        layer_sums, "v" * layers, [(cut, BF16)], [], 2 * rows * LANES, "layer_sums"
    )(kept, *received)
    received = [ahead(mine, step) for step in range(1, layers)]
    (copies,) = call(
        assemble, "s" + "v" * layers, [((count, 2 * rows, LANES), BF16)], total,
        2 * PACKED * LANES, "assemble",
    )(where, mine, *received)
    packed = exchange(copies, BLOCK)
    half = FLAT // 2
    strip = pl.BlockSpec((2, 2 * STRIP, C), lambda step: (0, step, 0))
    grads = pl.pallas_call(
        unpack,
        out_shape=(shape((2, half, C), F32),) * 2,
        grid=(half // (2 * STRIP),),
        in_specs=[pl.BlockSpec(packed.shape, lambda step: (0, 0, 0))],
        out_specs=(strip, strip),
        compiler_params=pltpu.CompilerParams(vmem_limit_bytes=VMEM_LIMIT),
        name="unpack",
    )(packed)
    return tuple(grad.reshape(1, 3, 3, C, C) for grad in grads)


def local(latents, cotangent, bucket, timesteps, w_enc, w_dec, w_time):
    where = jnp.stack([lax.axis_index(axis) for axis in ("near", "core", LAYERS)])
    where = where.astype(jnp.int32)
    micro_count = latents.shape[0]
    loss_scale = float(micro_count * lax.axis_size(DP) * CELLS) ** (-0.5)

    enc = w_enc.reshape(9, C, C)
    dec = w_dec.reshape(9, C, C)
    times = w_time.reshape(2, C, C)
    times = (times, to_other_core(times))
    enc = (enc, to_other_core(enc))
    emb = jnp.pad(time_embed(timesteps), ((0, 16 - micro_count), (0, 0)))
    dec, enc, times, emb, where = lax.optimization_barrier((dec, enc, times, emb, where))
    dec = (dec, to_other_core(dec))
    latents = latents.reshape(micro_count, CELLS, C)
    cotangent = cotangent.reshape(micro_count, CELLS, C)
    matrix = group_matrix()

    def up(value):
        return lax.ppermute(value, "near", [(0, 1)])

    def down(value):
        return lax.ppermute(value, "near", [(1, 0)])

    one = call(
        phase_one, "ss" + "h" * 5 + "vv", [NORMED, SCALE, ACTS, ACTS, ONE],
        [pltpu.VMEM(*ONE), TIMES, WEIGHTS, PADDED, SEMS], 2 * CONV, "one",
    )
    a_normed, a_scale, a_hidden, a_kept, sent = one(
        where, bucket, latents, *times, *enc, emb, matrix
    )
    two = call(
        phase_two, "ssv" + "h" * 6 + "vv", [NORMED, SCALE, ACTS, NORMED, SCALE, ACTS, ONE],
        [pltpu.VMEM(*ACTS), TIMES, WEIGHTS, WEIGHTS, PADDED, SEMS], 4 * CONV, "two",
    )
    be_normed, be_scale, be_hidden, bd_normed, bd_scale, bd_hidden, sent = two(
        where, bucket, up(sent), *times, *enc, *dec, emb, matrix
    )
    three = call(
        functools.partial(phase_three, loss_scale), "ssv" + "h" * 5 + "vvv",
        [ACTS, ACTS, ACTS, ONE],
        [
            pltpu.VMEM(*NORMED), pltpu.VMEM(*SCALE), pltpu.VMEM(*ONE), TIMES, WEIGHTS, PADDED,
            PADDED_COT, SEMS,
        ],
        3 * CONV, "three",
    )
    ad_hidden, ad_cots, a_skips, sent = three(
        where, bucket, down(sent), cotangent, *times, *dec, a_kept, emb, matrix
    )
    four = call(
        phase_four, "ssv" + "h" * 6 + "v" * 6, [ACTS, ACTS, ONE],
        [pltpu.VMEM(*ACTS), TIMES, WEIGHTS, WEIGHTS, PADDED_COT, SEMS], 4 * CONV, "four",
    )
    bd_cots, be_cots, sent = four(
        where, bucket, up(sent), *times, *enc, *dec, emb, matrix,
        bd_normed, bd_scale, be_normed, be_scale,
    )
    received = down(sent)
    work = [PADDED_COT, TURNED, pltpu.VMEM((2, PACKED, LANES), F32), pltpu.VMEM(*ACTS), pltpu.VMEM(*ACTS)]
    weights = call(weight_phase, "svvvv", [OWN, OTHER], work, 2 * CONV, "weights")
    own_dec, other_dec = weights(where, ad_hidden, ad_cots, bd_hidden, bd_cots)
    dec_pair = (own_dec, to_other_core(other_dec))
    five = call(
        phase_five, "ssv" + "h" * 4 + "v" * 8, [OWN, OTHER], [*work, TIMES, WEIGHTS, SEMS],
        3 * CONV, "five",
    )
    own_enc, other_enc = five(
        where, bucket, received, *times, *enc, a_skips, emb, matrix, a_normed, a_scale, a_hidden,
        be_hidden, be_cots,
    )

    return gradients(where, (own_enc, to_other_core(other_enc)), dec_pair)


def solution(mesh):
    segments, dp = mesh.shape["segment"], mesh.shape["dp"]
    near, far, rows = segments // 2, 2, 4
    split = Mesh(
        mesh.devices.reshape(near, 2, dp // (2 * far * rows), 2, far, rows),
        ("near", "core", *DP),
    )
    section, micro = ("near", "core"), DP
    placed = (
        P(micro, None, None, None),
        P(micro, None, None, None),
        P(micro, None),
        P(micro),
        P(section, None, None, None, None),
        P(section, None, None, None, None),
        P(section, None, None, None),
    )
    grads = P(section, None, None, None, None)
    return jax.shard_map(
        local, mesh=split, in_specs=placed, out_specs=(grads, grads), check_vma=False
    )
```
